32 devices in a mesh: dp: 2 (over x), ts: 16 (over z, y, core).
Axes of the slice: x: 2, y: 2, z: 4, core: 2. Of those that a mesh axis runs over, the one named last changes fastest.
Arguments:
- clip_video: bfloat16 [64, 4, 40, 128], P(('dp', 'ts')), may hold values from -6 to 6
- conv_weight: bfloat16 [3, 3, 3, 128, 128], replicated, may hold values from -0.109375 to 0.109375
- embed_weight: bfloat16 [128, 5120], replicated, may hold values from -0.5 to 0.5
- gain_spatial: float32 [5120], replicated, may hold values from 0.5 to 1.5
- gain_temporal: float32 [5120], replicated, may hold values from 0.5 to 1.5
- input_spatial: bfloat16 [5120, 384], P(('dp', 'ts')), may hold values from -0.078125 to 0.078125
- input_temporal: bfloat16 [5120, 384], P(('dp', 'ts')), may hold values from -0.078125 to 0.078125
- output_spatial: bfloat16 [128, 5120], replicated, may hold values from -2 to 2
- output_temporal: bfloat16 [128, 5120], replicated, may hold values from -2 to 2
- cotangent: bfloat16 [64, 4, 40, 5120], P(('dp', 'ts')), may hold values from -6 to 6
Outputs:
- layer_output: bfloat16 [64, 4, 40, 5120], P(('dp', 'ts'))
- grad_spatial: float32 [5120, 384], P(('dp', 'ts'))
The draws below stay inside these ranges and needn't reach their ends.
All inputs are finite; a program needn't handle non-finite values.
Results may differ from the reference program's by a relative error of at most 0.015.
Values may be sent and summed in bfloat16 or wider, within the bound.
A program may use at most 128 MiB of HBM per device.

```python
import jax
import jax.numpy as jnp
from jax import lax

D = 5120
HEAD = 128
CH = 128
FR = 16
H = 4
WC = 40
FRAMES = 64
N_DP = 2


def level_of(stream_key, extent, shards, least, largest):
    def one(position, blocks):
        heights = jax.random.uniform(jax.random.fold_in(jax.random.fold_in(stream_key, 6), position), (blocks,), jnp.float32, least / len(shards), largest / len(shards))
        return jnp.repeat(jnp.exp(heights), extent[position] // blocks).reshape((-1,) + (1,) * (len(extent) - position - 1))

    level = one(*shards[0])
    for cut in shards[1:]:
        level = level * one(*cut)
    return level


def bell_draw(stream_key, extent, scale, limit, split=(), dtype=jnp.bfloat16):
    factor_of = level_of(stream_key, extent, split, -0.22, 0.18) if split else 1.0
    drawn = jax.random.normal(stream_key, extent, jnp.float32) * scale * factor_of
    return jnp.minimum(jnp.maximum(drawn, -limit), limit).astype(dtype)


def setup_inputs(seed: int = 0) -> dict:
    keys = jax.random.split(jax.random.key(seed), 11)
    clip_video = bell_draw(keys[0], (FRAMES, H, WC, CH), 1.0, 6.0, ((0, 32),))
    conv_weight = bell_draw(keys[1], (3, 3, 3, CH, CH), (27 * CH) ** -0.5, 0.109375)
    embed_weight = bell_draw(keys[2], (CH, D), CH ** -0.5, 0.5)
    gain_spatial = jnp.clip(1.0 + 0.1 * jax.random.normal(keys[3], (D,), jnp.float32), 0.5, 1.5)
    gain_temporal = jnp.clip(1.0 + 0.1 * jax.random.normal(keys[4], (D,), jnp.float32), 0.5, 1.5)
    input_spatial = bell_draw(keys[5], (D, 3 * HEAD), D ** -0.5, 0.078125, ((0, 32),))
    input_temporal = bell_draw(keys[6], (D, 3 * HEAD), D ** -0.5, 0.078125, ((0, 32),))
    output_spatial = bell_draw(keys[7], (HEAD, D), (HEAD // 16) ** -0.5, 2.0)
    output_temporal = bell_draw(keys[8], (HEAD, D), (HEAD // 16) ** -0.5, 2.0)
    cotangent = bell_draw(keys[9], (FRAMES, H, WC, D), 1.0, 6.0, ((0, 32),))
    return {"clip_video": clip_video, "conv_weight": conv_weight, "embed_weight": embed_weight, "gain_spatial": gain_spatial, "gain_temporal": gain_temporal, "input_spatial": input_spatial, "input_temporal": input_temporal, "output_spatial": output_spatial, "output_temporal": output_temporal, "cotangent": cotangent}


epsilon = 1e-06
masked = -1e+30

def widen(array):
    return lax.optimization_barrier(array).astype(jnp.float32)

def conv_clips(video, weight):
    frames, height, columns, channels = video.shape
    out_channels = weight.shape[-1]
    volume = jnp.pad(video, ((2, 0), (1, 1), (1, 1), (0, 0)))
    summed = jnp.zeros((frames * height * columns, out_channels), jnp.float32)
    for time_tap in range(3):
        for row_tap in range(3):
            for col_tap in range(3):
                window = volume[2 - time_tap:2 - time_tap + frames, row_tap:row_tap + height, col_tap:col_tap + columns, :]
                summed = summed + jnp.dot(window.reshape(-1, channels), weight[time_tap, row_tap, col_tap], preferred_element_type=jnp.float32)
    return summed.reshape(frames, height, columns, out_channels)

def rms_norm(hidden, norm_gain):
    widened = hidden.astype(jnp.float32)
    factor = lax.rsqrt(lax.optimization_barrier(jnp.mean(widened * widened, axis=-1, keepdims=True)) + epsilon)
    return ((widened * factor * norm_gain).astype(jnp.bfloat16), factor)

def rms_norm_grad(hidden, norm_gain, factor, upstream):
    widened = hidden.astype(jnp.float32)
    scaled = upstream * norm_gain
    inner_mean = lax.optimization_barrier(jnp.mean(widened * scaled, axis=-1, keepdims=True))
    return factor * scaled - widened * factor ** 3 * inner_mean

def frame_forward(packed):
    frames, places, triple = packed.shape
    head_size = triple // 3
    flattened = widen(packed)
    queries = flattened[..., :head_size]
    key_rows = flattened[..., head_size:2 * head_size]
    values = flattened[..., 2 * head_size:]
    scores = jnp.einsum('fqd,fkd->fqk', queries, key_rows) * head_size ** (-0.5)
    attend = jax.nn.softmax(scores, axis=-1)
    rounded = widen(attend.astype(jnp.bfloat16))
    mixture = jnp.einsum('fqk,fkd->fqd', rounded, values)
    return (mixture.astype(jnp.bfloat16), attend)

def frame_backward(packed, attend, upstream):
    frames, places, triple = packed.shape
    head_size = triple // 3
    scale_factor = head_size ** (-0.5)
    flattened = widen(packed)
    queries = flattened[..., :head_size]
    key_rows = flattened[..., head_size:2 * head_size]
    values = flattened[..., 2 * head_size:]
    grad_out = widen(upstream)
    rounded = widen(attend.astype(jnp.bfloat16))
    grad_attend = jnp.einsum('fqd,fkd->fqk', grad_out, values)
    grad_values = jnp.einsum('fqk,fqd->fkd', rounded, grad_out)
    grad_scores = attend * (grad_attend - lax.optimization_barrier(jnp.sum(grad_attend * attend, axis=-1, keepdims=True)))
    grad_rounded = widen(grad_scores.astype(jnp.bfloat16))
    grad_queries = jnp.einsum('fqk,fkd->fqd', grad_rounded, key_rows) * scale_factor
    grad_keys = jnp.einsum('fqk,fqd->fkd', grad_rounded, queries) * scale_factor
    joined = jnp.concatenate([grad_queries, grad_keys, grad_values], axis=-1)
    return joined.astype(jnp.bfloat16)

def clip_forward(packed):
    frames, places, triple = packed.shape
    head_size = triple // 3
    volume = widen(packed.reshape(frames // FR, FR, places, triple))
    queries = volume[..., :head_size]
    key_rows = volume[..., head_size:2 * head_size]
    values = volume[..., 2 * head_size:]
    scores = jnp.einsum('cqpd,ckpd->cpqk', queries, key_rows) * head_size ** (-0.5)
    allowed = jnp.arange(FR)[:, None] >= jnp.arange(FR)[None, :]
    scores = jnp.where(allowed, scores, masked)
    attend = jax.nn.softmax(scores, axis=-1)
    rounded = widen(attend.astype(jnp.bfloat16))
    mixture = jnp.einsum('cpqk,ckpd->cqpd', rounded, values)
    return (mixture.astype(jnp.bfloat16).reshape(frames, places, head_size), attend)

def clip_backward(packed, attend, upstream):
    frames, places, triple = packed.shape
    head_size = triple // 3
    scale_factor = head_size ** (-0.5)
    volume = widen(packed.reshape(frames // FR, FR, places, triple))
    queries = volume[..., :head_size]
    key_rows = volume[..., head_size:2 * head_size]
    values = volume[..., 2 * head_size:]
    grad_out = widen(upstream.reshape(frames // FR, FR, places, head_size))
    rounded = widen(attend.astype(jnp.bfloat16))
    grad_attend = jnp.einsum('cqpd,ckpd->cpqk', grad_out, values)
    grad_values = jnp.einsum('cpqk,cqpd->ckpd', rounded, grad_out)
    grad_scores = attend * (grad_attend - lax.optimization_barrier(jnp.sum(grad_attend * attend, axis=-1, keepdims=True)))
    grad_rounded = widen(grad_scores.astype(jnp.bfloat16))
    grad_queries = jnp.einsum('cpqk,ckpd->cqpd', grad_rounded, key_rows) * scale_factor
    grad_keys = jnp.einsum('cpqk,cqpd->ckpd', grad_rounded, queries) * scale_factor
    joined = jnp.concatenate([grad_queries, grad_keys, grad_values], axis=-1)
    return joined.astype(jnp.bfloat16).reshape(frames, places, triple)

def reference(clip_video, conv_weight, embed_weight, gain_spatial, gain_temporal, input_spatial, input_temporal, output_spatial, output_temporal, cotangent):

    def group_pass(grad_first, inputs):
        group_video, group_cotangent = inputs
        features = jax.nn.gelu(conv_clips(group_video, conv_weight), approximate=True).astype(jnp.bfloat16)
        frames, height, columns, channels = features.shape
        places = height * columns
        tokens = frames * places
        embedded = jnp.dot(features.reshape(tokens, channels), embed_weight, preferred_element_type=jnp.float32).astype(jnp.bfloat16)
        normed_one, factor_one = rms_norm(embedded, gain_spatial)
        packed_one = jnp.dot(normed_one, input_spatial, preferred_element_type=jnp.float32).astype(jnp.bfloat16)
        packed_one = packed_one.reshape(frames, places, -1)
        mixture_one, attend_one = frame_forward(packed_one)
        after_space = (embedded.astype(jnp.float32) + jnp.dot(mixture_one.reshape(tokens, -1), output_spatial, preferred_element_type=jnp.float32)).astype(jnp.bfloat16)
        normed_two, factor_two = rms_norm(after_space, gain_temporal)
        packed_two = jnp.dot(normed_two, input_temporal, preferred_element_type=jnp.float32).astype(jnp.bfloat16)
        packed_two = packed_two.reshape(frames, places, -1)
        mixture_two, attend_two = clip_forward(packed_two)
        after_time = (after_space.astype(jnp.float32) + jnp.dot(mixture_two.reshape(tokens, -1), output_temporal, preferred_element_type=jnp.float32)).astype(jnp.bfloat16)
        cotangent_rows = group_cotangent.reshape(tokens, -1)
        grad_mix_two = jnp.dot(cotangent_rows, output_temporal.T, preferred_element_type=jnp.float32).astype(jnp.bfloat16)
        grad_packed_two = clip_backward(packed_two, attend_two, grad_mix_two.reshape(frames, places, -1)).reshape(tokens, -1)
        grad_normed_two = jnp.dot(grad_packed_two, input_temporal.T, preferred_element_type=jnp.float32)
        grad_after = (cotangent_rows.astype(jnp.float32) + rms_norm_grad(after_space, gain_temporal, factor_two, grad_normed_two)).astype(jnp.bfloat16)
        grad_mix_one = jnp.dot(grad_after, output_spatial.T, preferred_element_type=jnp.float32).astype(jnp.bfloat16)
        grad_packed_one = frame_backward(packed_one, attend_one, grad_mix_one.reshape(frames, places, -1)).reshape(tokens, -1)
        grad_first = grad_first + lax.dot_general(normed_one, grad_packed_one, (((0,), (0,)), ((), ())), preferred_element_type=jnp.float32)
        return (grad_first, after_time.reshape(frames, height, columns, -1))
    group_frames = clip_video.shape[0] // N_DP
    stacked_video = clip_video.reshape((N_DP, group_frames) + clip_video.shape[1:])
    stacked_cotangent = cotangent.reshape((N_DP, group_frames) + cotangent.shape[1:])
    zeros_grad = jnp.zeros(input_spatial.shape, jnp.float32)
    total, outputs = lax.scan(group_pass, zeros_grad, (stacked_video, stacked_cotangent))
    return (outputs.reshape(cotangent.shape), total)
```

```python
import functools

import jax
import jax.numpy as jnp
import numpy as np
from jax import lax
from jax.experimental import pallas as pl
from jax.experimental.pallas import tpu as pltpu
from jax.sharding import PartitionSpec as P

FR = 16
REDUCERS = 16
epsilon = 1e-06
masked = -1e30
F32 = jnp.float32
BF16 = jnp.bfloat16
MESH = pl.DeviceIdType.MESH


def mm(a, b, dims=((1,), (0,))):
    return lax.dot_general(a, b, (dims, ((), ())), preferred_element_type=F32)


def mm_t(a, b):
    return mm(a, b, ((1,), (1,)))


def t_mm(a, b):
    return mm(a, b, ((0,), (0,)))


def wide_mm(a, b):
    high = b.astype(BF16)
    low = (b - high.astype(F32)).astype(BF16)
    return mm(a, high) + mm(a, low)


def softmax(scores):
    raised = jnp.exp(scores - jnp.max(scores, axis=-1, keepdims=True))
    return raised / jnp.sum(raised, axis=-1, keepdims=True)


def softmax_grad(attend, grad_attend):
    inner = jnp.sum(grad_attend * attend, axis=-1, keepdims=True)
    return attend * (grad_attend - inner)


def stacked(block):
    third = block.shape[1] // 3
    return jnp.concatenate([block[:, i * third : (i + 1) * third] for i in range(3)], axis=0)


def unstacked(block):
    third = block.shape[0] // 3
    return jnp.concatenate([block[i * third : (i + 1) * third] for i in range(3)], axis=1)


def moved(block, distance):
    if distance == 0:
        return block
    return pltpu.roll(block, distance % block.shape[0], 0)


def whole_kernel(
    dims,
    video_hbm, conv_hbm, embed_hbm, gain_s_hbm, gain_t_hbm, in_s_hbm, in_t_hbm, out_s_hbm,
    out_t_hbm, cot_hbm, perm_hbm, clip_bias_hbm, edge_hbm,
    result, grad_result,
    video, prior, taps, basis, gain_s, gain_t, in_s, in_t, cot, perm, clip_bias, edge,
    twin_a, twin_b, pre_a, pre_b, part_a, part_b, part_c, land_a, land_b, land_c, full_a, full_b, full_c,
    clip, sent, got, back, home, gram, direct,
    local_sem, send_sem, recv_sem,
):
    n_dp, n_ts, frames, places, columns, team, pad, rows, window = dims
    n = n_dp * n_ts
    head = 128
    width = basis.shape[1]
    tokens = frames * places
    dp, ts = lax.axis_index("dp"), lax.axis_index("ts")
    me = dp * n_ts + ts

    loads = [
        (in_s_hbm, in_s), (in_t_hbm, in_t), (gain_s_hbm, gain_s), (gain_t_hbm, gain_t),
        (embed_hbm, basis.at[0:head]), (out_s_hbm, basis.at[head : 2 * head]),
        (video_hbm, video), (edge_hbm, edge), (conv_hbm, taps), (perm_hbm, perm),
        (out_t_hbm, basis.at[2 * head : 3 * head]), (cot_hbm, cot),
        (clip_bias_hbm, clip_bias),
    ]
    copies = [pltpu.make_async_copy(s, d, local_sem.at[i]) for i, (s, d) in enumerate(loads)]
    for copy in copies:
        copy.start()

    barrier = pltpu.get_barrier_semaphore()

    def greet(i, carry):
        dev = lax.rem(me + i, n)
        pl.semaphore_signal(
            barrier, inc=1, device_id=(dev // n_ts, lax.rem(dev, n_ts)), device_id_type=MESH
        )
        return carry

    lax.fori_loop(1, n, greet, 0)

    def remote(src, dst, index, dev):
        return pltpu.make_async_remote_copy(
            src_ref=src, dst_ref=dst, send_sem=send_sem.at[index], recv_sem=recv_sem.at[index],
            device_id=(dev // n_ts, lax.rem(dev, n_ts)), device_id_type=MESH,
        )

    def settle(ref, count, sem):
        piece = ref.at[pl.ds(0, count)]
        pltpu.make_async_copy(piece, piece, sem).wait()

    half, quarter = n_ts // 2, n_ts // 4
    core = lax.rem(ts, 2)
    partner = me + 1 - 2 * core
    pairs = REDUCERS // 2
    seated = dp * (half // 2) + (ts - quarter) // 2
    mine = core * pairs + seated

    def leader(side, i):
        return i // (half // 2) * n_ts + quarter + 2 * lax.rem(i, half // 2) + side

    leads = jnp.logical_and(
        jnp.logical_and(ts >= quarter, ts < quarter + half), seated < pairs
    )

    def scatter(part, land, index):
        def step(i, carry):
            r = lax.rem(me + i, REDUCERS)
            dev = leader(r // pairs, lax.rem(r, pairs))

            @pl.when(dev != me)
            def _():
                remote(part.at[r], land.at[me], index, dev).start()

            return carry

        lax.fori_loop(0, REDUCERS, step, 0)

    def gather(part, land, full, index):
        @pl.when(leads)
        def _():
            land[pl.ds(me, 1)] = part[pl.ds(mine, 1)]
            settle(land, n - 1, recv_sem.at[index])
            total = jnp.sum(land[...].astype(F32), axis=0, keepdims=True)
            full[pl.ds(mine, 1)] = total.astype(BF16)

            def step(i, carry):
                dev = lax.rem(me + i, n)
                remote(full.at[mine], full.at[mine], index + 1, dev).start()
                return carry

            lax.fori_loop(1, n, step, 0)

    def collect(part, land, full, index):
        @pl.when(leads)
        def _():
            settle(full, REDUCERS - 1, recv_sem.at[index + 1])
            settle(part, REDUCERS - 1, send_sem.at[index])
            settle(land, n - 1, send_sem.at[index + 1])

        @pl.when(jnp.logical_not(leads))
        def _():
            settle(full, REDUCERS, recv_sem.at[index + 1])
            settle(part, REDUCERS, send_sem.at[index])

        return unstacked(full[...].astype(F32).reshape(-1, head)).astype(BF16)

    def pair_start(part, twin, index):
        other = pl.ds((1 - core) * pairs, pairs)
        remote(part.at[other], twin, index, partner).start()

    def pair_scatter(part, twin, pre, land, index, pair_index):
        settle(twin, pairs, recv_sem.at[pair_index])
        own = part[pl.ds(core * pairs, pairs)].astype(F32)
        pre[...] = (own + twin[...].astype(F32)).astype(BF16)

        def step(i, carry):
            r = lax.rem(me // 2 + i, pairs)
            dev = leader(core, r)

            @pl.when(dev != me)
            def _():
                remote(pre.at[r], land.at[me // 2], index, dev).start()

            return carry

        lax.fori_loop(0, pairs, step, 0)

    def pair_gather(pre, land, full, index):
        @pl.when(leads)
        def _():
            land[pl.ds(me // 2, 1)] = pre[pl.ds(seated, 1)]
            settle(land, n // 2 - 1, recv_sem.at[index])
            total = jnp.sum(land[...].astype(F32), axis=0, keepdims=True)
            full[pl.ds(mine, 1)] = total.astype(BF16)

            def step(i, carry):
                dev = 2 * lax.rem(me // 2 + i, n // 2) + core
                remote(full.at[mine], full.at[mine], index + 1, dev).start()
                return carry

            lax.fori_loop(1, n // 2, step, 0)

    def pair_forward(pre, land, full, index, pair_index):
        @pl.when(leads)
        def _():
            settle(full, pairs - 1, recv_sem.at[index + 1])
            settle(pre, pairs - 1, send_sem.at[index])
            settle(land, n // 2 - 1, send_sem.at[index + 1])

        @pl.when(jnp.logical_not(leads))
        def _():
            settle(full, pairs, recv_sem.at[index + 1])
            settle(pre, pairs, send_sem.at[index])

        own = pl.ds(core * pairs, pairs)
        remote(full.at[own], full.at[own], pair_index + 2, partner).start()

    def pair_collect(twin, full, pair_index):
        settle(full, pairs, recv_sem.at[pair_index + 2])
        settle(twin, pairs, send_sem.at[pair_index])
        settle(full, pairs, send_sem.at[pair_index + 2])
        return unstacked(full[...].astype(F32).reshape(-1, head)).astype(BF16)

    for copy in copies[:6]:
        copy.wait()
    first = me * rows
    start = pl.multiple_of(first // 128 * 128, 128)
    if (n * rows - rows) // 128 * 128 + window > width:
        limit = width - window
        start = pl.multiple_of(jnp.where(start > limit, limit, start), 128)
    shift = first - start
    place = lax.broadcasted_iota(jnp.int32, (window, rows), 0)
    source = lax.broadcasted_iota(jnp.int32, (window, rows), 1)
    chosen = jnp.where(place == source + shift, 1.0, 0.0).astype(BF16)
    spread_s = mm(chosen, in_s[...]).astype(BF16)
    spread_t = mm(chosen, in_t[...]).astype(BF16)
    span = basis[0 : 2 * head, pl.ds(start, window)].astype(F32)
    span_s = (span[:head] * gain_s[:, pl.ds(start, window)]).astype(BF16)
    span_t = (span * gain_t[:, pl.ds(start, window)]).astype(BF16)
    part_a[...] = stacked(mm(span_s, spread_s)).reshape(part_a.shape).astype(BF16)
    part_b[...] = stacked(mm(span_t, spread_t)).reshape(part_b.shape).astype(BF16)
    copies[6].wait()

    pl.semaphore_wait(barrier, n - 1)
    halo = remote(video.at[pl.ds(frames - 2, 2)], prior, 0, me + 1)
    halo_in = remote(video.at[pl.ds(frames - 2, 2)], prior, 0, me)

    @pl.when(ts < n_ts - 1)
    def _():
        halo.start()

    pair_start(part_a, twin_a, 11)
    pair_start(part_b, twin_b, 12)
    chunk = width // 5
    gram[...] = jnp.zeros_like(gram)
    direct[...] = jnp.zeros_like(direct)

    def gram_slab(i, carry):
        pair = basis[0 : 2 * head, pl.ds(pl.multiple_of(i * chunk, 128), chunk)]
        gram[...] += mm_t(pair, pair)
        return carry

    lax.fori_loop(0, 3, gram_slab, 0)
    pair_scatter(part_a, twin_a, pre_a, land_a, 1, 11)
    pair_scatter(part_b, twin_b, pre_b, land_b, 3, 12)
    lax.fori_loop(3, 5, gram_slab, 0)
    embed_rows = mm(span_s, chosen).astype(BF16)

    @pl.when(ts == 0)
    def _():
        prior[...] = jnp.zeros_like(prior)

    @pl.when(ts > 0)
    def _():
        halo_in.wait_recv()

    for copy in copies[7:10]:
        copy.wait()
    volume = jnp.concatenate([prior[...], video[...]], axis=0)
    deep = jnp.concatenate(
        [volume[2 - a : 2 - a + frames].reshape(tokens, head) for a in range(3)], axis=1
    )
    edges = edge[...].astype(F32)
    by_col = [None, None, None]
    for b in range(3):
        weight = jnp.concatenate(
            [jnp.concatenate([taps[a, b, e] for a in range(3)], axis=0) for e in range(3)], axis=1
        )
        product = mm(deep, weight)
        product = moved(product, -(b - 1) * columns)
        if b == 0:
            product = product * edges[:, 0:1]
        if b == 2:
            product = product * edges[:, 1:2]
        for e in range(3):
            piece = product[:, e * head : (e + 1) * head]
            by_col[e] = piece if by_col[e] is None else by_col[e] + piece
    summed = (
        by_col[1] + moved(by_col[0], 1) * edges[:, 2:3] + moved(by_col[2], -1) * edges[:, 3:4]
    )
    features = jax.nn.gelu(summed, approximate=True).astype(BF16)

    grams = gram[...]

    def factor_of(tokens_in):
        squares = jnp.sum(
            wide_mm(tokens_in, grams[:head, :head]) * tokens_in.astype(F32),
            axis=-1, keepdims=True,
        )
        return lax.rsqrt(jnp.maximum(squares, 0.0) / width + epsilon)

    seat = lax.rem(ts, team)
    base = me - seat

    def swap(source_of, target, index):
        def step(i, carry):
            other = lax.rem(seat + i, team)
            remote(source_of(other), target.at[seat], index, base + other).start()
            return carry

        lax.fori_loop(1, team, step, 0)

    scaled = (features.astype(F32) * factor_of(features)).astype(BF16)
    clip[pl.ds(seat, 1)] = scaled.astype(F32).reshape(1, tokens, head).astype(BF16)
    swap(lambda other: clip.at[seat], clip, 5)

    pair_gather(pre_a, land_a, full_a, 1)

    for copy in copies[10:]:
        copy.wait()

    def direct_slab(i, carry):
        cols = pl.ds(pl.multiple_of(i * chunk, 128), chunk)
        direct[...] += mm_t(cot[:, cols], basis[head : 3 * head, cols])
        return carry

    lax.fori_loop(0, 5, direct_slab, 0)
    dealt = mm(perm[...], jnp.concatenate([features, direct[...].astype(BF16)], axis=1))
    sent[...] = dealt.reshape(sent.shape).astype(BF16)
    swap(lambda other: sent.at[other], got, 6)
    got[pl.ds(seat, 1)] = sent[pl.ds(seat, 1)]

    pair_gather(pre_b, land_b, full_b, 3)

    settle(clip, team - 1, recv_sem.at[5])
    settle(got, team - 1, recv_sem.at[6])
    arrived = got[...].astype(F32).reshape(team * frames * pad, 3 * head)
    own = arrived[:, :head].astype(BF16)
    direct_s, g_time = arrived[:, head : 2 * head], arrived[:, 2 * head :].astype(BF16)
    factor_one = factor_of(own)
    own_scaled = (own.astype(F32) * factor_one).astype(BF16)
    volumes = clip[...].astype(F32).reshape(team * frames, places, head).astype(BF16)
    scale = head ** -0.5

    def frame_rows(values, f):
        return values[f * pad : (f + 1) * pad].astype(BF16)

    def by_frame(values, transposed):
        form = mm_t if transposed else mm
        return jnp.concatenate(
            [form(frame_rows(values, f), volumes[f]) for f in range(team * frames)], axis=0
        )

    pair_forward(pre_a, land_a, full_a, 1, 11)
    map_space = pair_collect(twin_a, full_a, 11)
    map_q, map_k, map_v = (map_space[:, i * head : (i + 1) * head] for i in range(3))
    q = mm(own_scaled, map_q).astype(BF16)
    attend_one = softmax(by_frame(mm_t(q, map_k) * scale, True))
    looked = by_frame(attend_one, False).astype(BF16)
    mixture_one = mm(looked, map_v).astype(BF16)
    joint = jnp.concatenate([own, mixture_one], axis=-1)
    spread = wide_mm(joint, grams)
    squares = jnp.sum(spread * joint.astype(F32), axis=-1, keepdims=True)
    factor_two = lax.rsqrt(jnp.maximum(squares, 0.0) / width + epsilon)

    pair_forward(pre_b, land_b, full_b, 3, 12)
    map_time = pair_collect(twin_b, full_b, 12)
    packed_two = (mm(joint, map_time) * factor_two).astype(BF16)
    tq, tk, tv = (packed_two[:, i * head : (i + 1) * head] for i in range(3))
    attend_two = softmax(mm_t(tq, tk) * scale + clip_bias[...].astype(F32))
    attend_bf = attend_two.astype(BF16)
    mixture_two = mm(attend_bf, tv).astype(BF16)
    back[...] = (
        jnp.concatenate([mixture_one, mixture_two], axis=-1)
        .astype(F32).reshape(back.shape).astype(BF16)
    )
    swap(lambda other: back.at[other], home, 9)
    home[pl.ds(seat, 1)] = back[pl.ds(seat, 1)]

    grad_scores = softmax_grad(attend_two, mm_t(g_time, tv)).astype(BF16)
    grad_two = jnp.concatenate(
        [mm(grad_scores, tk) * scale, t_mm(grad_scores, tq) * scale, t_mm(attend_bf, g_time)],
        axis=-1,
    ).astype(BF16)
    inner = jnp.sum(grad_two.astype(F32) * packed_two.astype(F32), axis=-1, keepdims=True)
    g_space = (
        direct_s
        + factor_two * mm_t(grad_two, map_time[head:])
        - (factor_two * factor_two * inner / width) * spread[:, head:]
    ).astype(BF16)
    grad_attend = by_frame(mm_t(g_space, map_v), True)
    looked_back = by_frame(softmax_grad(attend_one, grad_attend), False).astype(BF16)
    cross = (t_mm(own_scaled, looked_back) * scale).astype(BF16)
    part = jnp.concatenate([mm(cross, map_k), t_mm(cross, map_q), t_mm(looked, g_space)], axis=1)
    part_c[...] = stacked(part).reshape(part_c.shape).astype(BF16)
    scatter(part_c, land_c, 7)

    settle(home, team - 1, recv_sem.at[9])
    returned = home[...].astype(F32).reshape(team * frames * pad, 2 * head).astype(BF16)
    triple = jnp.concatenate([features, t_mm(perm[...], returned).astype(BF16)], axis=-1)

    def write(i, carry):
        cols = pl.ds(pl.multiple_of(i * chunk, 128), chunk)
        result[:, cols] = mm(triple, basis[:, cols]).astype(BF16)
        return carry

    lax.fori_loop(0, 2, write, 0)
    gather(part_c, land_c, full_c, 7)
    lax.fori_loop(2, 5, write, 0)
    total = collect(part_c, land_c, full_c, 7)
    grad_result[...] = t_mm(embed_rows, total)

    @pl.when(ts < n_ts - 1)
    def _():
        halo.wait_send()

    settle(clip, team - 1, send_sem.at[5])
    settle(sent, team - 1, send_sem.at[6])
    settle(back, team - 1, send_sem.at[9])


def shards(
    clip_video, conv_weight, embed_weight, gain_spatial, gain_temporal, input_spatial,
    input_temporal, output_spatial, output_temporal, cotangent,
):
    frames, height, columns, channels = clip_video.shape
    rows, triple = input_spatial.shape
    head = triple // 3
    width = embed_weight.shape[-1]
    places = height * columns
    tokens = frames * places
    n_dp, n_ts = lax.axis_size("dp"), lax.axis_size("ts")
    n = n_dp * n_ts
    team = FR // frames
    share = places // team
    pad = -(-share // 8) * 8
    reach = max(i * rows % 128 + rows for i in range(n))
    window = -(-reach // 128) * 128

    token = np.arange(tokens)
    frame, spot = token // places, token % places
    slot = (spot // share * frames + frame) * pad + spot % share
    held = team * frames * pad
    perm = np.zeros((held, tokens), np.float32)
    perm[slot, token] = 1.0
    seat = np.arange(held)
    when, local = seat // pad, seat % pad
    allowed = (
        (local[:, None] == local[None, :])
        & (when[:, None] >= when[None, :])
        & (local[:, None] < share)
        & (local[None, :] < share)
    )
    clip_bias = np.where(allowed, 0.0, masked)
    edge = np.zeros((tokens, 128), np.float32)
    edge[:, 0] = spot // columns >= 1
    edge[:, 1] = spot // columns < height - 1
    edge[:, 2] = spot % columns >= 1
    edge[:, 3] = spot % columns < columns - 1

    dims = (n_dp, n_ts, frames, places, columns, team, pad, rows, window)
    any_space = pl.BlockSpec(memory_space=pltpu.HBM)
    vmem = pl.BlockSpec(memory_space=pltpu.VMEM)
    buffer = lambda *shape: pltpu.VMEM(shape, BF16)
    wide = lambda *shape: pltpu.VMEM(shape, F32)
    output, grad = pl.pallas_call(
        functools.partial(whole_kernel, dims),
        out_shape=(
            jax.ShapeDtypeStruct((tokens, width), BF16),
            jax.ShapeDtypeStruct((rows, triple), F32),
        ),
        in_specs=[any_space] * 13,
        out_specs=(vmem, vmem),
        scratch_shapes=[
            buffer(frames, places, channels), buffer(2, places, channels),
            buffer(*conv_weight.shape), buffer(3 * head, width), wide(1, width), wide(1, width),
            buffer(rows, triple), buffer(rows, triple), buffer(tokens, width),
            buffer(held, tokens), buffer(held, held),
            buffer(tokens, 128),
            buffer(REDUCERS // 2, 24, 128), buffer(REDUCERS // 2, 48, 128),
            buffer(REDUCERS // 2, 24, 128), buffer(REDUCERS // 2, 48, 128),
            buffer(REDUCERS, 24, 128), buffer(REDUCERS, 48, 128), buffer(REDUCERS, 24, 128),
            buffer(n // 2, 24, 128), buffer(n // 2, 48, 128), buffer(n, 24, 128),
            buffer(REDUCERS, 24, 128), buffer(REDUCERS, 48, 128), buffer(REDUCERS, 24, 128),
            buffer(team, tokens, head),
            buffer(team, frames * pad, triple), buffer(team, frames * pad, triple),
            buffer(team, frames * pad, 2 * head), buffer(team, frames * pad, 2 * head),
            wide(2 * head, 2 * head), wide(tokens, 2 * head),
            pltpu.SemaphoreType.DMA((13,)), pltpu.SemaphoreType.DMA((15,)),
            pltpu.SemaphoreType.DMA((15,)),
        ],
        compiler_params=pltpu.CompilerParams(
            collective_id=0, has_side_effects=True, vmem_limit_bytes=36 * 1024 * 1024
        ),
    )(*(pltpu.with_memory_space_constraint(x, pltpu.HBM) for x in (
        clip_video.reshape(frames, places, channels),
        conv_weight,
        embed_weight,
        gain_spatial.reshape(1, width),
        gain_temporal.reshape(1, width),
        input_spatial,
        input_temporal,
        output_spatial,
        output_temporal,
        cotangent.reshape(tokens, width),
        jnp.asarray(perm, BF16),
        jnp.asarray(clip_bias, BF16),
        jnp.asarray(edge, BF16),
    )))
    return output.reshape(frames, height, columns, width), grad


def solution(mesh):
    placed = (
        P(("dp", "ts"), None, None, None), P(), P(), P(), P(), P(("dp", "ts"), None),
        P(("dp", "ts"), None), P(), P(), P(("dp", "ts"), None, None, None),
    )
    return jax.shard_map(
        shards,
        mesh=mesh,
        in_specs=placed,
        out_specs=(P(("dp", "ts"), None, None, None), P(("dp", "ts"), None)),
        check_vma=False,
    )
```

```python
import functools

import jax
import jax.numpy as jnp
import numpy as np
from jax import lax
from jax.experimental import pallas as pl
from jax.experimental.pallas import tpu as pltpu
from jax.sharding import PartitionSpec as P

FR = 16
REDUCERS = 16
epsilon = 1e-06
masked = -1e30
F32 = jnp.float32
BF16 = jnp.bfloat16
MESH = pl.DeviceIdType.MESH


def mm(a, b, dims=((1,), (0,))):
    return lax.dot_general(a, b, (dims, ((), ())), preferred_element_type=F32)


def mm_t(a, b):
    return mm(a, b, ((1,), (1,)))


def t_mm(a, b):
    return mm(a, b, ((0,), (0,)))


def wide_mm(a, b):
    high = b.astype(BF16)
    low = (b - high.astype(F32)).astype(BF16)
    return mm(a, high) + mm(a, low)


def softmax(scores):
    raised = jnp.exp(scores - jnp.max(scores, axis=-1, keepdims=True))
    return raised / jnp.sum(raised, axis=-1, keepdims=True)


def softmax_grad(attend, grad_attend):
    inner = jnp.sum(grad_attend * attend, axis=-1, keepdims=True)
    return attend * (grad_attend - inner)


def stacked(block):
    third = block.shape[1] // 3
    return jnp.concatenate([block[:, i * third : (i + 1) * third] for i in range(3)], axis=0)


def unstacked(block):
    third = block.shape[0] // 3
    return jnp.concatenate([block[i * third : (i + 1) * third] for i in range(3)], axis=1)


def moved(block, distance):
    if distance == 0:
        return block
    return pltpu.roll(block, distance % block.shape[0], 0)


def whole_kernel(
    dims,
    video_hbm, conv_hbm, embed_hbm, gain_s_hbm, gain_t_hbm, in_s_hbm, in_t_hbm, out_s_hbm,
    out_t_hbm, cot_hbm, perm_hbm, clip_bias_hbm, edge_hbm,
    result, grad_result,
    video, prior, taps, basis, gain_s, gain_t, in_s, in_t, cot, perm, clip_bias, edge,
    twin_a, twin_b, pre_a, pre_b, part_a, part_b, part_c, land_a, land_b, land_c, full_a, full_b, full_c,
    clip, sent, got, sent_f, got_f, back, home, gram, direct,
    local_sem, send_sem, recv_sem,
):
    n_dp, n_ts, frames, places, columns, team, pad, rows, window = dims
    n = n_dp * n_ts
    head = 128
    width = basis.shape[1]
    tokens = frames * places
    dp, ts = lax.axis_index("dp"), lax.axis_index("ts")
    me = dp * n_ts + ts

    loads = [
        (in_s_hbm, in_s), (in_t_hbm, in_t), (gain_s_hbm, gain_s), (gain_t_hbm, gain_t),
        (embed_hbm, basis.at[0:head]), (out_s_hbm, basis.at[head : 2 * head]),
        (video_hbm, video), (edge_hbm, edge), (conv_hbm, taps), (perm_hbm, perm),
        (out_t_hbm, basis.at[2 * head : 3 * head]), (cot_hbm, cot),
        (clip_bias_hbm, clip_bias),
    ]
    copies = [pltpu.make_async_copy(s, d, local_sem.at[i]) for i, (s, d) in enumerate(loads)]
    for copy in copies:
        copy.start()

    half, quarter = n_ts // 2, n_ts // 4
    barrier = pltpu.get_barrier_semaphore()

    def leading(dev):
        group, spot = dev // n_ts, lax.rem(dev, n_ts)
        place = group * (half // 2) + (spot - quarter) // 2
        inside = jnp.logical_and(spot >= quarter, spot < quarter + half)
        return jnp.logical_and(inside, place < REDUCERS // 2)

    leads = leading(me)

    def greet(i, count):
        dev = lax.rem(me + i, n)
        beside = jnp.logical_or(dev - me == 1, me - dev == 1)
        related = jnp.logical_or(
            jnp.logical_or(leads, leading(dev)),
            jnp.logical_or(dev // team == me // team, beside),
        )

        @pl.when(related)
        def _():
            pl.semaphore_signal(
                barrier, inc=1, device_id=(dev // n_ts, lax.rem(dev, n_ts)), device_id_type=MESH
            )

        return count + jnp.where(related, 1, 0)

    greeted = lax.fori_loop(1, n, greet, 0)

    def remote(src, dst, index, dev):
        return pltpu.make_async_remote_copy(
            src_ref=src, dst_ref=dst, send_sem=send_sem.at[index], recv_sem=recv_sem.at[index],
            device_id=(dev // n_ts, lax.rem(dev, n_ts)), device_id_type=MESH,
        )

    def settle(ref, count, sem):
        piece = ref.at[pl.ds(0, count)]
        pltpu.make_async_copy(piece, piece, sem).wait()

    core = lax.rem(ts, 2)
    partner = me + 1 - 2 * core
    pairs = REDUCERS // 2
    seated = dp * (half // 2) + (ts - quarter) // 2
    mine = core * pairs + seated

    def leader(side, i):
        return i // (half // 2) * n_ts + quarter + 2 * lax.rem(i, half // 2) + side

    def scatter(part, land, index):
        def step(i, carry):
            r = lax.rem(me + i, REDUCERS)
            dev = leader(r // pairs, lax.rem(r, pairs))

            @pl.when(dev != me)
            def _():
                remote(part.at[r], land.at[me], index, dev).start()

            return carry

        lax.fori_loop(0, REDUCERS, step, 0)

    def gather(part, land, full, index):
        @pl.when(leads)
        def _():
            land[pl.ds(me, 1)] = part[pl.ds(mine, 1)]
            settle(land, n - 1, recv_sem.at[index])
            total = jnp.sum(land[...].astype(F32), axis=0, keepdims=True)
            full[pl.ds(mine, 1)] = total.astype(BF16)

            def step(i, carry):
                dev = lax.rem(me + i, n)
                remote(full.at[mine], full.at[mine], index + 1, dev).start()
                return carry

            lax.fori_loop(1, n, step, 0)

    def collect(part, land, full, index):
        @pl.when(leads)
        def _():
            settle(full, REDUCERS - 1, recv_sem.at[index + 1])
            settle(part, REDUCERS - 1, send_sem.at[index])
            settle(land, n - 1, send_sem.at[index + 1])

        @pl.when(jnp.logical_not(leads))
        def _():
            settle(full, REDUCERS, recv_sem.at[index + 1])
            settle(part, REDUCERS, send_sem.at[index])

        return unstacked(full[...].astype(F32).reshape(-1, head)).astype(BF16)

    def pair_start(part, twin, index):
        other = pl.ds((1 - core) * pairs, pairs)
        remote(part.at[other], twin, index, partner).start()

    def pair_scatter(part, twin, pre, land, index, pair_index):
        settle(twin, pairs, recv_sem.at[pair_index])
        own = part[pl.ds(core * pairs, pairs)].astype(F32)
        pre[...] = (own + twin[...].astype(F32)).astype(BF16)

        def step(i, carry):
            r = lax.rem(me // 2 + i, pairs)
            dev = leader(core, r)

            @pl.when(dev != me)
            def _():
                remote(pre.at[r], land.at[me // 2], index, dev).start()

            return carry

        lax.fori_loop(0, pairs, step, 0)

    def pair_gather(pre, land, full, index):
        @pl.when(leads)
        def _():
            land[pl.ds(me // 2, 1)] = pre[pl.ds(seated, 1)]
            settle(land, n // 2 - 1, recv_sem.at[index])
            total = jnp.sum(land[...].astype(F32), axis=0, keepdims=True)
            full[pl.ds(mine, 1)] = total.astype(BF16)

            def step(i, carry):
                dev = 2 * lax.rem(me // 2 + i, n // 2) + core
                remote(full.at[mine], full.at[mine], index + 1, dev).start()
                return carry

            lax.fori_loop(1, n // 2, step, 0)

    def pair_forward(pre, land, full, index, pair_index):
        @pl.when(leads)
        def _():
            settle(full, pairs - 1, recv_sem.at[index + 1])
            settle(pre, pairs - 1, send_sem.at[index])
            settle(land, n // 2 - 1, send_sem.at[index + 1])

        @pl.when(jnp.logical_not(leads))
        def _():
            settle(full, pairs, recv_sem.at[index + 1])
            settle(pre, pairs, send_sem.at[index])

        own = pl.ds(core * pairs, pairs)
        remote(full.at[own], full.at[own], pair_index + 2, partner).start()

    def pair_collect(twin, full, pair_index):
        settle(full, pairs, recv_sem.at[pair_index + 2])
        settle(twin, pairs, send_sem.at[pair_index])
        settle(full, pairs, send_sem.at[pair_index + 2])
        return unstacked(full[...].astype(F32).reshape(-1, head)).astype(BF16)

    for copy in copies[:6]:
        copy.wait()
    first = me * rows
    start = pl.multiple_of(first // 128 * 128, 128)
    if (n * rows - rows) // 128 * 128 + window > width:
        limit = width - window
        start = pl.multiple_of(jnp.where(start > limit, limit, start), 128)
    shift = first - start
    place = lax.broadcasted_iota(jnp.int32, (window, rows), 0)
    source = lax.broadcasted_iota(jnp.int32, (window, rows), 1)
    chosen = jnp.where(place == source + shift, 1.0, 0.0).astype(BF16)
    spread_s = mm(chosen, in_s[...]).astype(BF16)
    spread_t = mm(chosen, in_t[...]).astype(BF16)
    span = basis[0 : 2 * head, pl.ds(start, window)].astype(F32)
    span_s = (span[:head] * gain_s[:, pl.ds(start, window)]).astype(BF16)
    span_t = (span * gain_t[:, pl.ds(start, window)]).astype(BF16)
    part_a[...] = stacked(mm(span_s, spread_s)).reshape(part_a.shape).astype(BF16)
    part_b[...] = stacked(mm(span_t, spread_t)).reshape(part_b.shape).astype(BF16)
    copies[6].wait()

    pl.semaphore_wait(barrier, greeted)
    halo = remote(video.at[pl.ds(frames - 2, 2)], prior, 0, me + 1)
    halo_in = remote(video.at[pl.ds(frames - 2, 2)], prior, 0, me)

    @pl.when(ts < n_ts - 1)
    def _():
        halo.start()

    pair_start(part_a, twin_a, 11)
    pair_start(part_b, twin_b, 12)
    chunk = width // 5
    gram[...] = jnp.zeros_like(gram)
    direct[...] = jnp.zeros_like(direct)

    def gram_slab(i, carry):
        pair = basis[0 : 2 * head, pl.ds(pl.multiple_of(i * chunk, 128), chunk)]
        gram[...] += mm_t(pair, pair)
        return carry

    lax.fori_loop(0, 3, gram_slab, 0)
    pair_scatter(part_a, twin_a, pre_a, land_a, 1, 11)
    pair_scatter(part_b, twin_b, pre_b, land_b, 3, 12)
    lax.fori_loop(3, 5, gram_slab, 0)
    embed_rows = mm(span_s, chosen).astype(BF16)

    @pl.when(ts == 0)
    def _():
        prior[...] = jnp.zeros_like(prior)

    @pl.when(ts > 0)
    def _():
        halo_in.wait_recv()

    for copy in copies[7:10]:
        copy.wait()
    volume = jnp.concatenate([prior[...], video[...]], axis=0)
    deep = jnp.concatenate(
        [volume[2 - a : 2 - a + frames].reshape(tokens, head) for a in range(3)], axis=1
    )
    edges = edge[...].astype(F32)
    by_col = [None, None, None]
    for b in range(3):
        weight = jnp.concatenate(
            [jnp.concatenate([taps[a, b, e] for a in range(3)], axis=0) for e in range(3)], axis=1
        )
        product = mm(deep, weight)
        product = moved(product, -(b - 1) * columns)
        if b == 0:
            product = product * edges[:, 0:1]
        if b == 2:
            product = product * edges[:, 1:2]
        for e in range(3):
            piece = product[:, e * head : (e + 1) * head]
            by_col[e] = piece if by_col[e] is None else by_col[e] + piece
    summed = (
        by_col[1] + moved(by_col[0], 1) * edges[:, 2:3] + moved(by_col[2], -1) * edges[:, 3:4]
    )
    features = jax.nn.gelu(summed, approximate=True).astype(BF16)

    grams = gram[...]

    def factor_of(tokens_in):
        squares = jnp.sum(
            wide_mm(tokens_in, grams[:head, :head]) * tokens_in.astype(F32),
            axis=-1, keepdims=True,
        )
        return lax.rsqrt(jnp.maximum(squares, 0.0) / width + epsilon)

    seat = lax.rem(ts, team)
    base = me - seat

    def swap(source_of, target, index):
        def step(i, carry):
            other = lax.rem(seat + i, team)
            remote(source_of(other), target.at[seat], index, base + other).start()
            return carry

        lax.fori_loop(1, team, step, 0)

    scaled = (features.astype(F32) * factor_of(features)).astype(BF16)
    clip[pl.ds(seat, 1)] = scaled.astype(F32).reshape(1, tokens, head).astype(BF16)
    mates = team // 2 - 1

    def mate(i):
        return lax.rem(seat + 2 * i, team)

    def clip_send(i, carry):
        remote(clip.at[seat], clip.at[seat], 5, base + mate(i)).start()
        return carry

    lax.fori_loop(1, mates + 1, clip_send, 0)
    remote(clip.at[seat], clip.at[seat], 15, partner).start()
    sent_f[...] = mm(perm[...], features).reshape(sent_f.shape).astype(BF16)
    swap(lambda other: sent_f.at[other], got_f, 10)
    got_f[pl.ds(seat, 1)] = sent_f[pl.ds(seat, 1)]

    pair_gather(pre_a, land_a, full_a, 1)

    for copy in copies[10:]:
        copy.wait()

    def direct_slab(i, carry):
        cols = pl.ds(pl.multiple_of(i * chunk, 128), chunk)
        direct[...] += mm_t(cot[:, cols], basis[head : 3 * head, cols])
        return carry

    lax.fori_loop(0, 5, direct_slab, 0)
    dealt = mm(perm[...], direct[...].astype(BF16))
    sent[...] = dealt.reshape(sent.shape).astype(BF16)
    swap(lambda other: sent.at[other], got, 6)
    got[pl.ds(seat, 1)] = sent[pl.ds(seat, 1)]

    pair_gather(pre_b, land_b, full_b, 3)

    def own_rows(ref):
        return ref[...].astype(F32).reshape(team * frames * pad, -1)

    settle(got_f, team - 1, recv_sem.at[10])
    own = own_rows(got_f).astype(BF16)
    factor_one = factor_of(own)
    own_scaled = (own.astype(F32) * factor_one).astype(BF16)
    settle(clip, mates, recv_sem.at[5])

    def clip_forward(i, carry):
        remote(clip.at[mate(i)], clip.at[mate(i)], 16, partner).start()
        return carry

    lax.fori_loop(1, mates + 1, clip_forward, 0)
    pair_forward(pre_a, land_a, full_a, 1, 11)
    settle(clip, 1, recv_sem.at[15])
    settle(clip, mates, recv_sem.at[16])
    volumes = clip[...].astype(F32).reshape(team * frames, places, head).astype(BF16)
    scale = head ** -0.5

    def frame_rows(values, f):
        return values[f * pad : (f + 1) * pad].astype(BF16)

    def by_frame(values, transposed):
        form = mm_t if transposed else mm
        return jnp.concatenate(
            [form(frame_rows(values, f), volumes[f]) for f in range(team * frames)], axis=0
        )

    map_space = pair_collect(twin_a, full_a, 11)
    map_q, map_k, map_v = (map_space[:, i * head : (i + 1) * head] for i in range(3))
    q = mm(own_scaled, map_q).astype(BF16)
    attend_one = softmax(by_frame(mm_t(q, map_k) * scale, True))
    pair_forward(pre_b, land_b, full_b, 3, 12)
    looked = by_frame(attend_one, False).astype(BF16)
    mixture_one = mm(looked, map_v).astype(BF16)
    joint = jnp.concatenate([own, mixture_one], axis=-1)
    spread = wide_mm(joint, grams)
    squares = jnp.sum(spread * joint.astype(F32), axis=-1, keepdims=True)
    factor_two = lax.rsqrt(jnp.maximum(squares, 0.0) / width + epsilon)
    settle(got, team - 1, recv_sem.at[6])
    arrived = own_rows(got)
    direct_s, g_time = arrived[:, :head], arrived[:, head:].astype(BF16)
    map_time = pair_collect(twin_b, full_b, 12)
    packed_two = (mm(joint, map_time) * factor_two).astype(BF16)
    tq, tk, tv = (packed_two[:, i * head : (i + 1) * head] for i in range(3))
    attend_two = softmax(mm_t(tq, tk) * scale + clip_bias[...].astype(F32))
    attend_bf = attend_two.astype(BF16)
    mixture_two = mm(attend_bf, tv).astype(BF16)
    back[...] = (
        jnp.concatenate([mixture_one, mixture_two], axis=-1)
        .astype(F32).reshape(back.shape).astype(BF16)
    )
    home[pl.ds(seat, 1)] = back[pl.ds(seat, 1)]

    grad_scores = softmax_grad(attend_two, mm_t(g_time, tv)).astype(BF16)
    grad_two = jnp.concatenate(
        [mm(grad_scores, tk) * scale, t_mm(grad_scores, tq) * scale, t_mm(attend_bf, g_time)],
        axis=-1,
    ).astype(BF16)
    inner = jnp.sum(grad_two.astype(F32) * packed_two.astype(F32), axis=-1, keepdims=True)
    g_space = (
        direct_s
        + factor_two * mm_t(grad_two, map_time[head:])
        - (factor_two * factor_two * inner / width) * spread[:, head:]
    ).astype(BF16)
    grad_attend = by_frame(mm_t(g_space, map_v), True)
    looked_back = by_frame(softmax_grad(attend_one, grad_attend), False).astype(BF16)
    cross = (t_mm(own_scaled, looked_back) * scale).astype(BF16)
    part = jnp.concatenate([mm(cross, map_k), t_mm(cross, map_q), t_mm(looked, g_space)], axis=1)
    part_c[...] = stacked(part).reshape(part_c.shape).astype(BF16)
    scatter(part_c, land_c, 7)
    swap(lambda other: back.at[other], home, 9)
    gather(part_c, land_c, full_c, 7)

    settle(home, team - 1, recv_sem.at[9])
    returned = home[...].astype(F32).reshape(team * frames * pad, 2 * head).astype(BF16)
    triple = jnp.concatenate([features, t_mm(perm[...], returned).astype(BF16)], axis=-1)

    def write(i, carry):
        cols = pl.ds(pl.multiple_of(i * chunk, 128), chunk)
        result[:, cols] = mm(triple, basis[:, cols]).astype(BF16)
        return carry

    lax.fori_loop(0, 5, write, 0)
    total = collect(part_c, land_c, full_c, 7)
    grad_result[...] = t_mm(embed_rows, total)

    @pl.when(ts < n_ts - 1)
    def _():
        halo.wait_send()

    settle(clip, mates, send_sem.at[5])
    settle(sent, team - 1, send_sem.at[6])
    settle(sent_f, team - 1, send_sem.at[10])
    settle(clip, 1, send_sem.at[15])
    settle(clip, mates, send_sem.at[16])
    settle(back, team - 1, send_sem.at[9])


def shards(
    clip_video, conv_weight, embed_weight, gain_spatial, gain_temporal, input_spatial,
    input_temporal, output_spatial, output_temporal, cotangent,
):
    frames, height, columns, channels = clip_video.shape
    rows, triple = input_spatial.shape
    head = triple // 3
    width = embed_weight.shape[-1]
    places = height * columns
    tokens = frames * places
    n_dp, n_ts = lax.axis_size("dp"), lax.axis_size("ts")
    n = n_dp * n_ts
    team = FR // frames
    share = places // team
    pad = -(-share // 8) * 8
    reach = max(i * rows % 128 + rows for i in range(n))
    window = -(-reach // 128) * 128

    token = np.arange(tokens)
    frame, spot = token // places, token % places
    slot = (spot // share * frames + frame) * pad + spot % share
    held = team * frames * pad
    perm = np.zeros((held, tokens), np.float32)
    perm[slot, token] = 1.0
    seat = np.arange(held)
    when, local = seat // pad, seat % pad
    allowed = (
        (local[:, None] == local[None, :])
        & (when[:, None] >= when[None, :])
        & (local[:, None] < share)
        & (local[None, :] < share)
    )
    clip_bias = np.where(allowed, 0.0, masked)
    edge = np.zeros((tokens, 128), np.float32)
    edge[:, 0] = spot // columns >= 1
    edge[:, 1] = spot // columns < height - 1
    edge[:, 2] = spot % columns >= 1
    edge[:, 3] = spot % columns < columns - 1

    dims = (n_dp, n_ts, frames, places, columns, team, pad, rows, window)
    any_space = pl.BlockSpec(memory_space=pltpu.HBM)
    vmem = pl.BlockSpec(memory_space=pltpu.VMEM)
    buffer = lambda *shape: pltpu.VMEM(shape, BF16)
    wide = lambda *shape: pltpu.VMEM(shape, F32)
    output, grad = pl.pallas_call(
        functools.partial(whole_kernel, dims),
        out_shape=(
            jax.ShapeDtypeStruct((tokens, width), BF16),
            jax.ShapeDtypeStruct((rows, triple), F32),
        ),
        in_specs=[any_space] * 13,
        out_specs=(vmem, vmem),
        scratch_shapes=[
            buffer(frames, places, channels), buffer(2, places, channels),
            buffer(*conv_weight.shape), buffer(3 * head, width), wide(1, width), wide(1, width),
            buffer(rows, triple), buffer(rows, triple), buffer(tokens, width),
            buffer(held, tokens), buffer(held, held),
            buffer(tokens, 128),
            buffer(REDUCERS // 2, 24, 128), buffer(REDUCERS // 2, 48, 128),
            buffer(REDUCERS // 2, 24, 128), buffer(REDUCERS // 2, 48, 128),
            buffer(REDUCERS, 24, 128), buffer(REDUCERS, 48, 128), buffer(REDUCERS, 24, 128),
            buffer(n // 2, 24, 128), buffer(n // 2, 48, 128), buffer(n, 24, 128),
            buffer(REDUCERS, 24, 128), buffer(REDUCERS, 48, 128), buffer(REDUCERS, 24, 128),
            buffer(team, tokens, head),
            buffer(team, frames * pad, 2 * head), buffer(team, frames * pad, 2 * head),
            buffer(team, frames * pad, head), buffer(team, frames * pad, head),
            buffer(team, frames * pad, 2 * head), buffer(team, frames * pad, 2 * head),
            wide(2 * head, 2 * head), wide(tokens, 2 * head),
            pltpu.SemaphoreType.DMA((13,)), pltpu.SemaphoreType.DMA((17,)),
            pltpu.SemaphoreType.DMA((17,)),
        ],
        compiler_params=pltpu.CompilerParams(
            collective_id=0, has_side_effects=True, vmem_limit_bytes=36 * 1024 * 1024
        ),
    )(*(pltpu.with_memory_space_constraint(x, pltpu.HBM) for x in (
        clip_video.reshape(frames, places, channels),
        conv_weight,
        embed_weight,
        gain_spatial.reshape(1, width),
        gain_temporal.reshape(1, width),
        input_spatial,
        input_temporal,
        output_spatial,
        output_temporal,
        cotangent.reshape(tokens, width),
        jnp.asarray(perm, BF16),
        jnp.asarray(clip_bias, BF16),
        jnp.asarray(edge, BF16),
    )))
    return output.reshape(frames, height, columns, width), grad


def solution(mesh):
    placed = (
        P(("dp", "ts"), None, None, None), P(), P(), P(), P(), P(("dp", "ts"), None),
        P(("dp", "ts"), None), P(), P(), P(("dp", "ts"), None, None, None),
    )
    return jax.shard_map(
        shards,
        mesh=mesh,
        in_specs=placed,
        out_specs=(P(("dp", "ts"), None, None, None), P(("dp", "ts"), None)),
        check_vma=False,
    )
```

```python
import functools

import jax
import jax.numpy as jnp
import numpy as np
from jax import lax
from jax.experimental import pallas as pl
from jax.experimental.pallas import tpu as pltpu
from jax.sharding import PartitionSpec as P

FR = 16
REDUCERS = 16
epsilon = 1e-06
masked = -1e30
F32 = jnp.float32
BF16 = jnp.bfloat16
MESH = pl.DeviceIdType.MESH


def mm(a, b, dims=((1,), (0,))):
    return lax.dot_general(a, b, (dims, ((), ())), preferred_element_type=F32)


def mm_t(a, b):
    return mm(a, b, ((1,), (1,)))


def t_mm(a, b):
    return mm(a, b, ((0,), (0,)))


def wide_mm(a, b):
    high = b.astype(BF16)
    low = (b - high.astype(F32)).astype(BF16)
    return mm(a, high) + mm(a, low)


def softmax(scores):
    raised = jnp.exp(scores - jnp.max(scores, axis=-1, keepdims=True))
    return raised / jnp.sum(raised, axis=-1, keepdims=True)


def softmax_grad(attend, grad_attend):
    inner = jnp.sum(grad_attend * attend, axis=-1, keepdims=True)
    return attend * (grad_attend - inner)


def stacked(block):
    third = block.shape[1] // 3
    return jnp.concatenate([block[:, i * third : (i + 1) * third] for i in range(3)], axis=0)


def unstacked(block):
    third = block.shape[0] // 3
    return jnp.concatenate([block[i * third : (i + 1) * third] for i in range(3)], axis=1)


def moved(block, distance):
    if distance == 0:
        return block
    return pltpu.roll(block, distance % block.shape[0], 0)


def whole_kernel(
    dims,
    video_hbm, conv_hbm, embed_hbm, gain_s_hbm, gain_t_hbm, in_s_hbm, in_t_hbm, out_s_hbm,
    out_t_hbm, cot_hbm, perm_hbm, clip_bias_hbm, edge_hbm,
    result, total, embed_rows,
    video, prior, taps, basis, gain_s, gain_t, in_s, in_t, cot, perm, clip_bias, edge,
    twin_a, twin_b, pre_a, pre_b, part_a, part_b, part_c, land_a, land_b, land_c, full_a, full_b, full_c,
    clip, sent, got, sent_f, got_f, back, home, gram, direct,
    local_sem, send_sem, recv_sem,
):
    n_dp, n_ts, frames, places, columns, team, pad, rows, window = dims
    n = n_dp * n_ts
    head = 128
    width = basis.shape[1]
    tokens = frames * places
    dp, ts = lax.axis_index("dp"), lax.axis_index("ts")
    me = dp * n_ts + ts

    loads = [
        (in_s_hbm, in_s), (in_t_hbm, in_t), (gain_s_hbm, gain_s), (gain_t_hbm, gain_t),
        (embed_hbm, basis.at[0:head]), (out_s_hbm, basis.at[head : 2 * head]),
        (video_hbm, video), (edge_hbm, edge), (conv_hbm, taps), (perm_hbm, perm),
        (out_t_hbm, basis.at[2 * head : 3 * head]), (cot_hbm, cot),
        (clip_bias_hbm, clip_bias),
    ]
    copies = [pltpu.make_async_copy(s, d, local_sem.at[i]) for i, (s, d) in enumerate(loads)]
    for copy in copies:
        copy.start()

    half, quarter = n_ts // 2, n_ts // 4
    barrier = pltpu.get_barrier_semaphore()

    def leading(dev):
        group, spot = dev // n_ts, lax.rem(dev, n_ts)
        place = group * (half // 2) + (spot - quarter) // 2
        inside = jnp.logical_and(spot >= quarter, spot < quarter + half)
        return jnp.logical_and(inside, place < REDUCERS // 2)

    leads = leading(me)

    pairs = REDUCERS // 2
    seat = lax.rem(ts, team)
    base = me - seat

    def leader(side, i):
        return i // (half // 2) * n_ts + quarter + 2 * lax.rem(i, half // 2) + side

    def greet(dev):
        pl.semaphore_signal(
            barrier, inc=1, device_id=(dev // n_ts, lax.rem(dev, n_ts)), device_id_type=MESH
        )

    def greet_if(dev, wanted, count):
        related = jnp.logical_and(wanted, jnp.logical_not(leading(dev)))

        @pl.when(related)
        def _():
            greet(dev)

        return count + jnp.where(related, 1, 0)

    def greet_any(i, carry):
        greet(lax.rem(me + i, n))
        return carry

    def greet_leader(r, carry):
        greet(leader(r // pairs, lax.rem(r, pairs)))
        return carry

    @pl.when(leads)
    def _():
        lax.fori_loop(1, n, greet_any, 0)

    @pl.when(jnp.logical_not(leads))
    def _():
        lax.fori_loop(0, REDUCERS, greet_leader, 0)

    plain = jnp.logical_not(leads)
    count = lax.fori_loop(
        1, team, lambda i, c: greet_if(base + lax.rem(seat + i, team), plain, c), REDUCERS
    )
    below = jnp.logical_and(plain, jnp.logical_and(seat == 0, ts > 0))
    above = jnp.logical_and(plain, jnp.logical_and(seat == team - 1, ts < n_ts - 1))
    count = greet_if(jnp.where(below, me - 1, me), below, count)
    count = greet_if(jnp.where(above, me + 1, me), above, count)
    greeted = jnp.where(leads, n - 1, count)

    def remote(src, dst, index, dev):
        return pltpu.make_async_remote_copy(
            src_ref=src, dst_ref=dst, send_sem=send_sem.at[index], recv_sem=recv_sem.at[index],
            device_id=(dev // n_ts, lax.rem(dev, n_ts)), device_id_type=MESH,
        )

    def settle(ref, count, sem):
        piece = ref.at[pl.ds(0, count)]
        pltpu.make_async_copy(piece, piece, sem).wait()

    core = lax.rem(ts, 2)
    partner = me + 1 - 2 * core
    seated = dp * (half // 2) + (ts - quarter) // 2
    mine = core * pairs + seated

    def scatter(part, land, index):
        def step(i, carry):
            r = lax.rem(me + i, REDUCERS)
            dev = leader(r // pairs, lax.rem(r, pairs))

            @pl.when(dev != me)
            def _():
                remote(part.at[r], land.at[me], index, dev).start()

            return carry

        lax.fori_loop(0, REDUCERS, step, 0)

    def gather(part, land, full, index):
        @pl.when(leads)
        def _():
            land[pl.ds(me, 1)] = part[pl.ds(mine, 1)]
            settle(land, n - 1, recv_sem.at[index])
            total = jnp.sum(land[...].astype(F32), axis=0, keepdims=True)
            full[pl.ds(mine, 1)] = total.astype(BF16)

            def step(i, carry):
                dev = lax.rem(me + i, n)
                remote(full.at[mine], full.at[mine], index + 1, dev).start()
                return carry

            lax.fori_loop(1, n, step, 0)

    def collect(part, land, full, index):
        @pl.when(leads)
        def _():
            settle(full, REDUCERS - 1, recv_sem.at[index + 1])
            settle(part, REDUCERS - 1, send_sem.at[index])
            settle(land, n - 1, send_sem.at[index + 1])

        @pl.when(jnp.logical_not(leads))
        def _():
            settle(full, REDUCERS, recv_sem.at[index + 1])
            settle(part, REDUCERS, send_sem.at[index])

        return unstacked(full[...].astype(F32).reshape(-1, head)).astype(BF16)

    def pair_start(part, twin, index):
        other = pl.ds((1 - core) * pairs, pairs)
        remote(part.at[other], twin, index, partner).start()

    def pair_scatter(part, twin, pre, land, index, pair_index):
        settle(twin, pairs, recv_sem.at[pair_index])
        own = part[pl.ds(core * pairs, pairs)].astype(F32)
        pre[...] = (own + twin[...].astype(F32)).astype(BF16)

        def step(i, carry):
            r = lax.rem(me // 2 + i, pairs)
            dev = leader(core, r)

            @pl.when(dev != me)
            def _():
                remote(pre.at[r], land.at[me // 2], index, dev).start()

            return carry

        lax.fori_loop(0, pairs, step, 0)

    def pair_gather(pre, land, full, index):
        @pl.when(leads)
        def _():
            land[pl.ds(me // 2, 1)] = pre[pl.ds(seated, 1)]
            settle(land, n // 2 - 1, recv_sem.at[index])
            total = jnp.sum(land[...].astype(F32), axis=0, keepdims=True)
            full[pl.ds(mine, 1)] = total.astype(BF16)

            def step(i, carry):
                dev = 2 * lax.rem(me // 2 + i, n // 2) + core
                remote(full.at[mine], full.at[mine], index + 1, dev).start()
                return carry

            lax.fori_loop(1, n // 2, step, 0)

    def pair_forward(pre, land, full, index, pair_index):
        @pl.when(leads)
        def _():
            settle(full, pairs - 1, recv_sem.at[index + 1])
            settle(pre, pairs - 1, send_sem.at[index])
            settle(land, n // 2 - 1, send_sem.at[index + 1])

        @pl.when(jnp.logical_not(leads))
        def _():
            settle(full, pairs, recv_sem.at[index + 1])
            settle(pre, pairs, send_sem.at[index])

        own = pl.ds(core * pairs, pairs)
        remote(full.at[own], full.at[own], pair_index + 2, partner).start()

    def pair_collect(twin, full, pair_index):
        settle(full, pairs, recv_sem.at[pair_index + 2])
        settle(twin, pairs, send_sem.at[pair_index])
        settle(full, pairs, send_sem.at[pair_index + 2])
        return unstacked(full[...].astype(F32).reshape(-1, head)).astype(BF16)

    for copy in copies[:6]:
        copy.wait()
    first = me * rows
    start = pl.multiple_of(first // 128 * 128, 128)
    if (n * rows - rows) // 128 * 128 + window > width:
        limit = width - window
        start = pl.multiple_of(jnp.where(start > limit, limit, start), 128)
    shift = first - start
    place = lax.broadcasted_iota(jnp.int32, (window, rows), 0)
    source = lax.broadcasted_iota(jnp.int32, (window, rows), 1)
    chosen = jnp.where(place == source + shift, 1.0, 0.0).astype(BF16)
    spread_s = mm(chosen, in_s[...]).astype(BF16)
    spread_t = mm(chosen, in_t[...]).astype(BF16)
    span = basis[0 : 2 * head, pl.ds(start, window)].astype(F32)
    span_s = (span[:head] * gain_s[:, pl.ds(start, window)]).astype(BF16)
    span_t = (span * gain_t[:, pl.ds(start, window)]).astype(BF16)
    part_a[...] = stacked(mm(span_s, spread_s)).reshape(part_a.shape).astype(BF16)
    part_b[...] = stacked(mm(span_t, spread_t)).reshape(part_b.shape).astype(BF16)
    copies[6].wait()

    pl.semaphore_wait(barrier, greeted)
    halo = remote(video.at[pl.ds(frames - 2, 2)], prior, 0, me + 1)
    halo_in = remote(video.at[pl.ds(frames - 2, 2)], prior, 0, me)

    @pl.when(ts < n_ts - 1)
    def _():
        halo.start()

    pair_start(part_a, twin_a, 11)
    pair_start(part_b, twin_b, 12)
    chunk = width // 5
    gram[...] = jnp.zeros_like(gram)
    direct[...] = jnp.zeros_like(direct)

    def gram_slab(i, carry):
        pair = basis[0 : 2 * head, pl.ds(pl.multiple_of(i * chunk, 128), chunk)]
        gram[...] += mm_t(pair, pair)
        return carry

    lax.fori_loop(0, 3, gram_slab, 0)
    pair_scatter(part_a, twin_a, pre_a, land_a, 1, 11)
    pair_scatter(part_b, twin_b, pre_b, land_b, 3, 12)
    lax.fori_loop(3, 5, gram_slab, 0)
    embed_rows[...] = mm(span_s, chosen).astype(BF16)

    @pl.when(ts == 0)
    def _():
        prior[...] = jnp.zeros_like(prior)

    @pl.when(ts > 0)
    def _():
        halo_in.wait_recv()

    for copy in copies[7:10]:
        copy.wait()
    volume = jnp.concatenate([prior[...], video[...]], axis=0)
    deep = jnp.concatenate(
        [volume[2 - a : 2 - a + frames].reshape(tokens, head) for a in range(3)], axis=1
    )
    edges = edge[...].astype(F32)
    by_col = [None, None, None]
    for b in range(3):
        weight = jnp.concatenate(
            [jnp.concatenate([taps[a, b, e] for a in range(3)], axis=0) for e in range(3)], axis=1
        )
        product = mm(deep, weight)
        product = moved(product, -(b - 1) * columns)
        if b == 0:
            product = product * edges[:, 0:1]
        if b == 2:
            product = product * edges[:, 1:2]
        for e in range(3):
            piece = product[:, e * head : (e + 1) * head]
            by_col[e] = piece if by_col[e] is None else by_col[e] + piece
    summed = (
        by_col[1] + moved(by_col[0], 1) * edges[:, 2:3] + moved(by_col[2], -1) * edges[:, 3:4]
    )
    features = jax.nn.gelu(summed, approximate=True).astype(BF16)

    grams = gram[...]

    def factor_of(tokens_in):
        squares = jnp.sum(
            wide_mm(tokens_in, grams[:head, :head]) * tokens_in.astype(F32),
            axis=-1, keepdims=True,
        )
        return lax.rsqrt(jnp.maximum(squares, 0.0) / width + epsilon)

    def swap(source_of, target, index):
        def step(i, carry):
            other = lax.rem(seat + i, team)
            remote(source_of(other), target.at[seat], index, base + other).start()
            return carry

        lax.fori_loop(1, team, step, 0)

    sent_f[...] = mm(perm[...], features).reshape(sent_f.shape).astype(BF16)
    swap(lambda other: sent_f.at[other], got_f, 10)
    got_f[pl.ds(seat, 1)] = sent_f[pl.ds(seat, 1)]
    scaled = (features.astype(F32) * factor_of(features)).astype(BF16)
    clip[pl.ds(seat, 1)] = scaled.astype(F32).reshape(1, tokens, head).astype(BF16)
    mates = team // 2 - 1

    def mate(i):
        return lax.rem(seat + 2 * i, team)

    def clip_send(i, carry):
        remote(clip.at[seat], clip.at[seat], 5, base + mate(i)).start()
        return carry

    lax.fori_loop(1, mates + 1, clip_send, 0)
    remote(clip.at[seat], clip.at[seat], 15, partner).start()

    pair_gather(pre_a, land_a, full_a, 1)

    for copy in copies[10:]:
        copy.wait()

    def direct_slab(i, carry):
        cols = pl.ds(pl.multiple_of(i * chunk, 128), chunk)
        direct[...] += mm_t(cot[:, cols], basis[head : 3 * head, cols])
        return carry

    lax.fori_loop(0, 5, direct_slab, 0)
    pair_gather(pre_b, land_b, full_b, 3)
    dealt = mm(perm[...], direct[...].astype(BF16))
    sent[...] = dealt.reshape(sent.shape).astype(BF16)
    swap(lambda other: sent.at[other], got, 6)
    got[pl.ds(seat, 1)] = sent[pl.ds(seat, 1)]


    def own_rows(ref):
        return ref[...].astype(F32).reshape(team * frames * pad, -1)

    settle(got_f, team - 1, recv_sem.at[10])
    own = own_rows(got_f).astype(BF16)
    factor_one = factor_of(own)
    own_scaled = (own.astype(F32) * factor_one).astype(BF16)
    settle(clip, mates, recv_sem.at[5])

    def clip_forward(i, carry):
        remote(clip.at[mate(i)], clip.at[mate(i)], 16, partner).start()
        return carry

    lax.fori_loop(1, mates + 1, clip_forward, 0)
    pair_forward(pre_a, land_a, full_a, 1, 11)
    settle(clip, 1, recv_sem.at[15])
    settle(clip, mates, recv_sem.at[16])
    volumes = clip[...].astype(F32).reshape(team * frames, places, head).astype(BF16)
    scale = head ** -0.5

    def frame_rows(values, f):
        return values[f * pad : (f + 1) * pad].astype(BF16)

    def by_frame(values, transposed):
        form = mm_t if transposed else mm
        return jnp.concatenate(
            [form(frame_rows(values, f), volumes[f]) for f in range(team * frames)], axis=0
        )

    map_space = pair_collect(twin_a, full_a, 11)
    map_q, map_k, map_v = (map_space[:, i * head : (i + 1) * head] for i in range(3))
    q = mm(own_scaled, map_q).astype(BF16)
    attend_one = softmax(by_frame(mm_t(q, map_k) * scale, True))
    pair_forward(pre_b, land_b, full_b, 3, 12)
    looked = by_frame(attend_one, False).astype(BF16)
    mixture_one = mm(looked, map_v).astype(BF16)
    joint = jnp.concatenate([own, mixture_one], axis=-1)
    spread = wide_mm(joint, grams)
    squares = jnp.sum(spread * joint.astype(F32), axis=-1, keepdims=True)
    factor_two = lax.rsqrt(jnp.maximum(squares, 0.0) / width + epsilon)
    settle(got, team - 1, recv_sem.at[6])
    arrived = own_rows(got)
    direct_s, g_time = arrived[:, :head], arrived[:, head:].astype(BF16)
    map_time = pair_collect(twin_b, full_b, 12)
    packed_two = (mm(joint, map_time) * factor_two).astype(BF16)
    tq, tk, tv = (packed_two[:, i * head : (i + 1) * head] for i in range(3))
    attend_two = softmax(mm_t(tq, tk) * scale + clip_bias[...].astype(F32))
    attend_bf = attend_two.astype(BF16)
    mixture_two = mm(attend_bf, tv).astype(BF16)
    back[...] = (
        jnp.concatenate([mixture_one, mixture_two], axis=-1)
        .astype(F32).reshape(back.shape).astype(BF16)
    )
    home[pl.ds(seat, 1)] = back[pl.ds(seat, 1)]

    grad_scores = softmax_grad(attend_two, mm_t(g_time, tv)).astype(BF16)
    grad_two = jnp.concatenate(
        [mm(grad_scores, tk) * scale, t_mm(grad_scores, tq) * scale, t_mm(attend_bf, g_time)],
        axis=-1,
    ).astype(BF16)
    inner = jnp.sum(grad_two.astype(F32) * packed_two.astype(F32), axis=-1, keepdims=True)
    g_space = (
        direct_s
        + factor_two * mm_t(grad_two, map_time[head:])
        - (factor_two * factor_two * inner / width) * spread[:, head:]
    ).astype(BF16)
    grad_attend = by_frame(mm_t(g_space, map_v), True)
    looked_back = by_frame(softmax_grad(attend_one, grad_attend), False).astype(BF16)
    cross = (t_mm(own_scaled, looked_back) * scale).astype(BF16)
    part = jnp.concatenate([mm(cross, map_k), t_mm(cross, map_q), t_mm(looked, g_space)], axis=1)
    part_c[...] = stacked(part).reshape(part_c.shape).astype(BF16)
    scatter(part_c, land_c, 7)
    swap(lambda other: back.at[other], home, 9)
    gather(part_c, land_c, full_c, 7)

    settle(home, team - 1, recv_sem.at[9])
    returned = home[...].astype(F32).reshape(team * frames * pad, 2 * head).astype(BF16)
    triple = jnp.concatenate([features, t_mm(perm[...], returned).astype(BF16)], axis=-1)

    def write(i, carry):
        cols = pl.ds(pl.multiple_of(i * chunk, 128), chunk)
        result[:, cols] = mm(triple, basis[:, cols]).astype(BF16)
        return carry

    lax.fori_loop(0, 5, write, 0)
    total[...] = collect(part_c, land_c, full_c, 7)

    @pl.when(ts < n_ts - 1)
    def _():
        halo.wait_send()

    settle(clip, mates, send_sem.at[5])
    settle(sent, team - 1, send_sem.at[6])
    settle(sent_f, team - 1, send_sem.at[10])
    settle(clip, 1, send_sem.at[15])
    settle(clip, mates, send_sem.at[16])
    settle(back, team - 1, send_sem.at[9])


def store_kernel(result, total, embed_rows, output, grad, grad_block, sems):
    large = pltpu.make_async_copy(result, output, sems.at[0])
    large.start()
    grad_block[...] = t_mm(embed_rows[...], total[...])
    small = pltpu.make_async_copy(grad_block, grad, sems.at[1])
    small.start()
    large.wait()
    small.wait()


def shards(
    clip_video, conv_weight, embed_weight, gain_spatial, gain_temporal, input_spatial,
    input_temporal, output_spatial, output_temporal, cotangent,
):
    frames, height, columns, channels = clip_video.shape
    rows, triple = input_spatial.shape
    head = triple // 3
    width = embed_weight.shape[-1]
    places = height * columns
    tokens = frames * places
    n_dp, n_ts = lax.axis_size("dp"), lax.axis_size("ts")
    n = n_dp * n_ts
    team = FR // frames
    share = places // team
    pad = -(-share // 8) * 8
    reach = max(i * rows % 128 + rows for i in range(n))
    window = -(-reach // 128) * 128

    token = np.arange(tokens)
    frame, spot = token // places, token % places
    slot = (spot // share * frames + frame) * pad + spot % share
    held = team * frames * pad
    perm = np.zeros((held, tokens), np.float32)
    perm[slot, token] = 1.0
    seat = np.arange(held)
    when, local = seat // pad, seat % pad
    allowed = (
        (local[:, None] == local[None, :])
        & (when[:, None] >= when[None, :])
        & (local[:, None] < share)
        & (local[None, :] < share)
    )
    clip_bias = np.where(allowed, 0.0, masked)
    edge = np.zeros((tokens, 128), np.float32)
    edge[:, 0] = spot // columns >= 1
    edge[:, 1] = spot // columns < height - 1
    edge[:, 2] = spot % columns >= 1
    edge[:, 3] = spot % columns < columns - 1

    dims = (n_dp, n_ts, frames, places, columns, team, pad, rows, window)
    any_space = pl.BlockSpec(memory_space=pltpu.HBM)
    vmem = pl.BlockSpec(memory_space=pltpu.VMEM)
    buffer = lambda *shape: pltpu.VMEM(shape, BF16)
    wide = lambda *shape: pltpu.VMEM(shape, F32)
    result, total, embed_rows = pl.pallas_call(
        functools.partial(whole_kernel, dims),
        out_shape=(
            jax.ShapeDtypeStruct((tokens, width), BF16),
            jax.ShapeDtypeStruct((head, triple), BF16),
            jax.ShapeDtypeStruct((head, rows), BF16),
        ),
        in_specs=[any_space] * 13,
        out_specs=(vmem, vmem, vmem),
        scratch_shapes=[
            buffer(frames, places, channels), buffer(2, places, channels),
            buffer(*conv_weight.shape), buffer(3 * head, width), wide(1, width), wide(1, width),
            buffer(rows, triple), buffer(rows, triple), buffer(tokens, width),
            buffer(held, tokens), buffer(held, held),
            buffer(tokens, 128),
            buffer(REDUCERS // 2, 24, 128), buffer(REDUCERS // 2, 48, 128),
            buffer(REDUCERS // 2, 24, 128), buffer(REDUCERS // 2, 48, 128),
            buffer(REDUCERS, 24, 128), buffer(REDUCERS, 48, 128), buffer(REDUCERS, 24, 128),
            buffer(n // 2, 24, 128), buffer(n // 2, 48, 128), buffer(n, 24, 128),
            buffer(REDUCERS, 24, 128), buffer(REDUCERS, 48, 128), buffer(REDUCERS, 24, 128),
            buffer(team, tokens, head),
            buffer(team, frames * pad, 2 * head), buffer(team, frames * pad, 2 * head),
            buffer(team, frames * pad, head), buffer(team, frames * pad, head),
            buffer(team, frames * pad, 2 * head), buffer(team, frames * pad, 2 * head),
            wide(2 * head, 2 * head), wide(tokens, 2 * head),
            pltpu.SemaphoreType.DMA((13,)), pltpu.SemaphoreType.DMA((17,)),
            pltpu.SemaphoreType.DMA((17,)),
        ],
        compiler_params=pltpu.CompilerParams(
            collective_id=0, has_side_effects=True, vmem_limit_bytes=36 * 1024 * 1024
        ),
    )(*(pltpu.with_memory_space_constraint(x, pltpu.HBM) for x in (
        clip_video.reshape(frames, places, channels),
        conv_weight,
        embed_weight,
        gain_spatial.reshape(1, width),
        gain_temporal.reshape(1, width),
        input_spatial,
        input_temporal,
        output_spatial,
        output_temporal,
        cotangent.reshape(tokens, width),
        jnp.asarray(perm, BF16),
        jnp.asarray(clip_bias, BF16),
        jnp.asarray(edge, BF16),
    )))
    output, grad = pl.pallas_call(
        store_kernel,
        out_shape=(
            jax.ShapeDtypeStruct((tokens, width), BF16),
            jax.ShapeDtypeStruct((rows, triple), F32),
        ),
        in_specs=[pl.BlockSpec(memory_space=pl.ANY), vmem, vmem],
        out_specs=(any_space, any_space),
        scratch_shapes=[wide(rows, triple), pltpu.SemaphoreType.DMA((2,))],
        compiler_params=pltpu.CompilerParams(vmem_limit_bytes=4 * 1024 * 1024),
    )(result, total, embed_rows)
    return output.reshape(frames, height, columns, width), grad


def solution(mesh):
    placed = (
        P(("dp", "ts"), None, None, None), P(), P(), P(), P(), P(("dp", "ts"), None),
        P(("dp", "ts"), None), P(), P(), P(("dp", "ts"), None, None, None),
    )
    return jax.shard_map(
        shards,
        mesh=mesh,
        in_specs=placed,
        out_specs=(P(("dp", "ts"), None, None, None), P(("dp", "ts"), None)),
        check_vma=False,
    )
```

```python
import functools

import jax
import jax.numpy as jnp
import numpy as np
from jax import lax
from jax.experimental import pallas as pl
from jax.experimental.pallas import tpu as pltpu
from jax.sharding import PartitionSpec as P

FR = 16
REDUCERS = 16
epsilon = 1e-06
masked = -1e30
F32 = jnp.float32
BF16 = jnp.bfloat16
MESH = pl.DeviceIdType.MESH


def mm(a, b, dims=((1,), (0,))):
    return lax.dot_general(a, b, (dims, ((), ())), preferred_element_type=F32)


def mm_t(a, b):
    return mm(a, b, ((1,), (1,)))


def t_mm(a, b):
    return mm(a, b, ((0,), (0,)))


def wide_mm(a, b):
    high = b.astype(BF16)
    low = (b - high.astype(F32)).astype(BF16)
    return mm(a, high) + mm(a, low)


def softmax(scores):
    raised = jnp.exp(scores - jnp.max(scores, axis=-1, keepdims=True))
    return raised * (1.0 / jnp.sum(raised, axis=-1, keepdims=True))


def softmax_grad(attend, grad_attend):
    inner = jnp.sum(grad_attend * attend, axis=-1, keepdims=True)
    return attend * (grad_attend - inner)


def stacked(block):
    third = block.shape[1] // 3
    return jnp.concatenate([block[:, i * third : (i + 1) * third] for i in range(3)], axis=0)


def unstacked(block):
    third = block.shape[0] // 3
    return jnp.concatenate([block[i * third : (i + 1) * third] for i in range(3)], axis=1)


def moved(block, distance):
    if distance == 0:
        return block
    return pltpu.roll(block, distance % block.shape[0], 0)


def whole_kernel(
    dims,
    video_hbm, conv_hbm, embed_hbm, gain_s_hbm, gain_t_hbm, in_s_hbm, in_t_hbm, out_s_hbm,
    out_t_hbm, cot_hbm, perm_hbm, frame_bias_hbm, clip_bias_hbm, edge_hbm,
    result, total, embed_rows,
    video, prior, taps, basis, gain_s, gain_t, in_s, in_t, cot, perm, frame_bias, clip_bias, edge,
    twin_a, twin_b, pre_a, pre_b, part_a, part_b, part_c, land_a, land_b, land_c, full_a, full_b, full_c,
    clip, sent, got, sent_f, got_f, back, home, gram, direct,
    local_sem, send_sem, recv_sem,
):
    n_dp, n_ts, frames, places, columns, team, pad, rows, window = dims
    n = n_dp * n_ts
    head = 128
    width = basis.shape[1]
    tokens = frames * places
    dp, ts = lax.axis_index("dp"), lax.axis_index("ts")
    me = dp * n_ts + ts

    loads = [
        (in_s_hbm, in_s), (in_t_hbm, in_t), (gain_s_hbm, gain_s), (gain_t_hbm, gain_t),
        (embed_hbm, basis.at[0:head]), (out_s_hbm, basis.at[head : 2 * head]),
        (video_hbm, video), (edge_hbm, edge), (conv_hbm, taps), (perm_hbm, perm),
        (out_t_hbm, basis.at[2 * head : 3 * head]), (cot_hbm, cot),
        (frame_bias_hbm, frame_bias), (clip_bias_hbm, clip_bias),
    ]
    copies = [pltpu.make_async_copy(s, d, local_sem.at[i]) for i, (s, d) in enumerate(loads)]
    for copy in copies:
        copy.start()

    half, quarter = n_ts // 2, n_ts // 4
    barrier = pltpu.get_barrier_semaphore()

    def leading(dev):
        group, spot = dev // n_ts, lax.rem(dev, n_ts)
        place = group * (half // 2) + (spot - quarter) // 2
        inside = jnp.logical_and(spot >= quarter, spot < quarter + half)
        return jnp.logical_and(inside, place < REDUCERS // 2)

    leads = leading(me)

    pairs = REDUCERS // 2
    seat = lax.rem(ts, team)
    base = me - seat

    def leader(side, i):
        return i // (half // 2) * n_ts + quarter + 2 * lax.rem(i, half // 2) + side

    def greet(dev):
        pl.semaphore_signal(
            barrier, inc=1, device_id=(dev // n_ts, lax.rem(dev, n_ts)), device_id_type=MESH
        )

    def greet_if(dev, wanted, count):
        related = jnp.logical_and(wanted, jnp.logical_not(leading(dev)))

        @pl.when(related)
        def _():
            greet(dev)

        return count + jnp.where(related, 1, 0)

    def greet_any(i, carry):
        greet(lax.rem(me + i, n))
        return carry

    def greet_leader(r, carry):
        greet(leader(r // pairs, lax.rem(r, pairs)))
        return carry

    @pl.when(leads)
    def _():
        lax.fori_loop(1, n, greet_any, 0)

    @pl.when(jnp.logical_not(leads))
    def _():
        lax.fori_loop(0, REDUCERS, greet_leader, 0)

    plain = jnp.logical_not(leads)
    count = lax.fori_loop(
        1, team, lambda i, c: greet_if(base + lax.rem(seat + i, team), plain, c), REDUCERS
    )
    below = jnp.logical_and(plain, jnp.logical_and(seat == 0, ts > 0))
    above = jnp.logical_and(plain, jnp.logical_and(seat == team - 1, ts < n_ts - 1))
    count = greet_if(jnp.where(below, me - 1, me), below, count)
    count = greet_if(jnp.where(above, me + 1, me), above, count)
    greeted = jnp.where(leads, n - 1, count)

    def remote(src, dst, index, dev):
        return pltpu.make_async_remote_copy(
            src_ref=src, dst_ref=dst, send_sem=send_sem.at[index], recv_sem=recv_sem.at[index],
            device_id=(dev // n_ts, lax.rem(dev, n_ts)), device_id_type=MESH,
        )

    def settle(ref, count, sem):
        piece = ref.at[pl.ds(0, count)]
        pltpu.make_async_copy(piece, piece, sem).wait()

    core = lax.rem(ts, 2)
    partner = me + 1 - 2 * core
    seated = dp * (half // 2) + (ts - quarter) // 2
    mine = core * pairs + seated

    def scatter(part, land, index):
        def step(i, carry):
            r = lax.rem(me + i, REDUCERS)
            dev = leader(r // pairs, lax.rem(r, pairs))

            @pl.when(dev != me)
            def _():
                remote(part.at[r], land.at[me], index, dev).start()

            return carry

        lax.fori_loop(0, REDUCERS, step, 0)

    def gather(part, land, full, index):
        @pl.when(leads)
        def _():
            land[pl.ds(me, 1)] = part[pl.ds(mine, 1)]
            settle(land, n - 1, recv_sem.at[index])
            total = jnp.sum(land[...].astype(F32), axis=0, keepdims=True)
            full[pl.ds(mine, 1)] = total.astype(BF16)

            def step(i, carry):
                dev = lax.rem(me + i, n)
                remote(full.at[mine], full.at[mine], index + 1, dev).start()
                return carry

            lax.fori_loop(1, n, step, 0)

    def collect(part, land, full, index):
        @pl.when(leads)
        def _():
            settle(full, REDUCERS - 1, recv_sem.at[index + 1])
            settle(part, REDUCERS - 1, send_sem.at[index])
            settle(land, n - 1, send_sem.at[index + 1])

        @pl.when(jnp.logical_not(leads))
        def _():
            settle(full, REDUCERS, recv_sem.at[index + 1])
            settle(part, REDUCERS, send_sem.at[index])

        return unstacked(full[...].astype(F32).reshape(-1, head)).astype(BF16)

    def pair_start(part, twin, index):
        other = pl.ds((1 - core) * pairs, pairs)
        remote(part.at[other], twin, index, partner).start()

    def pair_scatter(part, twin, pre, land, index, pair_index):
        settle(twin, pairs, recv_sem.at[pair_index])
        own = part[pl.ds(core * pairs, pairs)].astype(F32)
        pre[...] = (own + twin[...].astype(F32)).astype(BF16)

        def step(i, carry):
            r = lax.rem(me // 2 + i, pairs)
            dev = leader(core, r)

            @pl.when(dev != me)
            def _():
                remote(pre.at[r], land.at[me // 2], index, dev).start()

            return carry

        lax.fori_loop(0, pairs, step, 0)

    def pair_gather(pre, land, full, index):
        @pl.when(leads)
        def _():
            land[pl.ds(me // 2, 1)] = pre[pl.ds(seated, 1)]
            settle(land, n // 2 - 1, recv_sem.at[index])
            total = jnp.sum(land[...].astype(F32), axis=0, keepdims=True)
            full[pl.ds(mine, 1)] = total.astype(BF16)

            def step(i, carry):
                dev = 2 * lax.rem(me // 2 + i, n // 2) + core
                remote(full.at[mine], full.at[mine], index + 1, dev).start()
                return carry

            lax.fori_loop(1, n // 2, step, 0)

    def pair_forward(pre, land, full, index, pair_index):
        @pl.when(leads)
        def _():
            settle(full, pairs - 1, recv_sem.at[index + 1])
            settle(pre, pairs - 1, send_sem.at[index])
            settle(land, n // 2 - 1, send_sem.at[index + 1])

        @pl.when(jnp.logical_not(leads))
        def _():
            settle(full, pairs, recv_sem.at[index + 1])
            settle(pre, pairs, send_sem.at[index])

        own = pl.ds(core * pairs, pairs)
        remote(full.at[own], full.at[own], pair_index + 2, partner).start()

    def pair_collect(twin, full, pair_index):
        settle(full, pairs, recv_sem.at[pair_index + 2])
        settle(twin, pairs, send_sem.at[pair_index])
        settle(full, pairs, send_sem.at[pair_index + 2])
        return unstacked(full[...].astype(F32).reshape(-1, head)).astype(BF16)

    for copy in copies[:6]:
        copy.wait()
    first = me * rows
    start = pl.multiple_of(first // 128 * 128, 128)
    if (n * rows - rows) // 128 * 128 + window > width:
        limit = width - window
        start = pl.multiple_of(jnp.where(start > limit, limit, start), 128)
    shift = first - start
    place = lax.broadcasted_iota(jnp.int32, (window, rows), 0)
    source = lax.broadcasted_iota(jnp.int32, (window, rows), 1)
    chosen = jnp.where(place == source + shift, 1.0, 0.0).astype(BF16)
    spread_s = mm(chosen, in_s[...]).astype(BF16)
    spread_t = mm(chosen, in_t[...]).astype(BF16)
    span = basis[0 : 2 * head, pl.ds(start, window)].astype(F32)
    span_s = (span[:head] * gain_s[:, pl.ds(start, window)]).astype(BF16)
    span_t = (span * gain_t[:, pl.ds(start, window)]).astype(BF16)
    part_a[...] = stacked(mm(span_s, spread_s)).reshape(part_a.shape).astype(BF16)
    part_b[...] = stacked(mm(span_t, spread_t)).reshape(part_b.shape).astype(BF16)
    copies[6].wait()

    pl.semaphore_wait(barrier, greeted)
    halo = remote(video.at[pl.ds(frames - 2, 2)], prior, 0, me + 1)
    halo_in = remote(video.at[pl.ds(frames - 2, 2)], prior, 0, me)

    @pl.when(ts < n_ts - 1)
    def _():
        halo.start()

    pair_start(part_a, twin_a, 11)
    pair_start(part_b, twin_b, 12)
    chunk = width // 5
    gram[...] = jnp.zeros_like(gram)
    direct[...] = jnp.zeros_like(direct)

    def gram_slab(i, carry):
        pair = basis[0 : 2 * head, pl.ds(pl.multiple_of(i * chunk, 128), chunk)]
        gram[...] += mm_t(pair, pair)
        return carry

    lax.fori_loop(0, 3, gram_slab, 0)
    pair_scatter(part_a, twin_a, pre_a, land_a, 1, 11)
    pair_scatter(part_b, twin_b, pre_b, land_b, 3, 12)
    lax.fori_loop(3, 5, gram_slab, 0)
    embed_rows[...] = mm(span_s, chosen).astype(BF16)

    @pl.when(ts == 0)
    def _():
        prior[...] = jnp.zeros_like(prior)

    @pl.when(ts > 0)
    def _():
        halo_in.wait_recv()

    for copy in copies[7:10]:
        copy.wait()
    volume = jnp.concatenate([prior[...], video[...]], axis=0)
    deep = jnp.concatenate(
        [volume[2 - a : 2 - a + frames].reshape(tokens, head) for a in range(3)], axis=1
    )
    edges = edge[...].astype(F32)
    by_col = [None, None, None]
    for b in range(3):
        weight = jnp.concatenate(
            [jnp.concatenate([taps[a, b, e] for a in range(3)], axis=0) for e in range(3)], axis=1
        )
        product = mm(deep, weight)
        product = moved(product, -(b - 1) * columns)
        if b == 0:
            product = product * edges[:, 0:1]
        if b == 2:
            product = product * edges[:, 1:2]
        for e in range(3):
            piece = product[:, e * head : (e + 1) * head]
            by_col[e] = piece if by_col[e] is None else by_col[e] + piece
    summed = (
        by_col[1] + moved(by_col[0], 1) * edges[:, 2:3] + moved(by_col[2], -1) * edges[:, 3:4]
    )
    features = jax.nn.gelu(summed, approximate=True).astype(BF16)

    grams = gram[...]

    def factor_of(tokens_in):
        squares = jnp.sum(
            wide_mm(tokens_in, grams[:head, :head]) * tokens_in.astype(F32),
            axis=-1, keepdims=True,
        )
        return lax.rsqrt(jnp.maximum(squares, 0.0) / width + epsilon)

    def swap(source_of, target, index):
        def step(i, carry):
            other = lax.rem(seat + i, team)
            remote(source_of(other), target.at[seat], index, base + other).start()
            return carry

        lax.fori_loop(1, team, step, 0)

    sent_f[...] = mm(perm[...], features).reshape(sent_f.shape).astype(BF16)
    swap(lambda other: sent_f.at[other], got_f, 10)
    got_f[pl.ds(seat, 1)] = sent_f[pl.ds(seat, 1)]
    scaled = (features.astype(F32) * factor_of(features)).astype(BF16)
    clip[pl.ds(seat, 1)] = scaled.astype(F32).reshape(1, tokens, head).astype(BF16)
    mates = team // 2 - 1

    def mate(i):
        return lax.rem(seat + 2 * i, team)

    def clip_send(i, carry):
        remote(clip.at[seat], clip.at[seat], 5, base + mate(i)).start()
        return carry

    lax.fori_loop(1, mates + 1, clip_send, 0)
    remote(clip.at[seat], clip.at[seat], 15, partner).start()

    pair_gather(pre_a, land_a, full_a, 1)

    for copy in copies[10:]:
        copy.wait()

    def direct_slab(i, carry):
        cols = pl.ds(pl.multiple_of(i * chunk, 128), chunk)
        direct[...] += mm_t(cot[:, cols], basis[head : 3 * head, cols])
        return carry

    lax.fori_loop(0, 5, direct_slab, 0)
    pair_gather(pre_b, land_b, full_b, 3)
    dealt = mm(perm[...], direct[...].astype(BF16))
    sent[...] = dealt.reshape(sent.shape).astype(BF16)
    swap(lambda other: sent.at[other], got, 6)
    got[pl.ds(seat, 1)] = sent[pl.ds(seat, 1)]


    def own_rows(ref):
        return ref[...].astype(F32).reshape(team * pad, -1)

    settle(got_f, team - 1, recv_sem.at[10])
    own = own_rows(got_f).astype(BF16)
    factor_one = factor_of(own)
    own_scaled = (own.astype(F32) * factor_one).astype(BF16)
    settle(clip, mates, recv_sem.at[5])

    def clip_forward(i, carry):
        remote(clip.at[mate(i)], clip.at[mate(i)], 16, partner).start()
        return carry

    lax.fori_loop(1, mates + 1, clip_forward, 0)
    pair_forward(pre_a, land_a, full_a, 1, 11)
    settle(clip, 1, recv_sem.at[15])
    settle(clip, mates, recv_sem.at[16])
    scale = head ** -0.5

    def by_slot(form, values):
        return [
            form(values[i * pad : (i + 1) * pad].astype(BF16), clip[i]) for i in range(team)
        ]

    map_space = pair_collect(twin_a, full_a, 11)
    map_q, map_k, map_v = (map_space[:, i * head : (i + 1) * head] for i in range(3))
    q = mm(own_scaled, map_q).astype(BF16)
    apart = frame_bias[...].astype(F32)
    scores = [score + apart for score in by_slot(mm_t, mm_t(q, map_k) * scale)]
    attend_one = softmax(jnp.concatenate(scores, axis=0))
    pair_forward(pre_b, land_b, full_b, 3, 12)
    looked = jnp.concatenate(by_slot(mm, attend_one), axis=0).astype(BF16)
    mixture_one = mm(looked, map_v).astype(BF16)
    joint = jnp.concatenate([own, mixture_one], axis=-1)
    spread = wide_mm(joint, grams)
    squares = jnp.sum(spread * joint.astype(F32), axis=-1, keepdims=True)
    factor_two = lax.rsqrt(jnp.maximum(squares, 0.0) / width + epsilon)
    settle(got, team - 1, recv_sem.at[6])
    arrived = own_rows(got)
    direct_s, g_time = arrived[:, :head], arrived[:, head:].astype(BF16)
    map_time = pair_collect(twin_b, full_b, 12)
    packed_two = (mm(joint, map_time) * factor_two).astype(BF16)
    tq, tk, tv = (packed_two[:, i * head : (i + 1) * head] for i in range(3))
    attend_two = softmax(mm_t(tq, tk) * scale + clip_bias[...].astype(F32))
    attend_bf = attend_two.astype(BF16)
    mixture_two = mm(attend_bf, tv).astype(BF16)
    back[...] = (
        jnp.concatenate([mixture_one, mixture_two], axis=-1)
        .astype(F32).reshape(back.shape).astype(BF16)
    )
    home[pl.ds(seat, 1)] = back[pl.ds(seat, 1)]

    grad_scores = softmax_grad(attend_two, mm_t(g_time, tv)).astype(BF16)
    grad_two = jnp.concatenate(
        [mm(grad_scores, tk) * scale, t_mm(grad_scores, tq) * scale, t_mm(attend_bf, g_time)],
        axis=-1,
    ).astype(BF16)
    inner = jnp.sum(grad_two.astype(F32) * packed_two.astype(F32), axis=-1, keepdims=True)
    g_space = (
        direct_s
        + factor_two * mm_t(grad_two, map_time[head:])
        - (factor_two * factor_two * inner / width) * spread[:, head:]
    ).astype(BF16)
    grad_attend = jnp.concatenate(by_slot(mm_t, mm_t(g_space, map_v)), axis=0)
    looked_back = by_slot(mm, softmax_grad(attend_one, grad_attend))
    looked_back = jnp.concatenate(looked_back, axis=0).astype(BF16)
    cross = (t_mm(own_scaled, looked_back) * scale).astype(BF16)
    part = jnp.concatenate([mm(cross, map_k), t_mm(cross, map_q), t_mm(looked, g_space)], axis=1)
    part_c[...] = stacked(part).reshape(part_c.shape).astype(BF16)
    scatter(part_c, land_c, 7)
    swap(lambda other: back.at[other], home, 9)
    gather(part_c, land_c, full_c, 7)

    settle(home, team - 1, recv_sem.at[9])
    returned = home[...].astype(F32).reshape(team * pad, 2 * head).astype(BF16)
    triple = jnp.concatenate([features, t_mm(perm[...], returned).astype(BF16)], axis=-1)

    def write(i, carry):
        cols = pl.ds(pl.multiple_of(i * chunk, 128), chunk)
        result[:, cols] = mm(triple, basis[:, cols]).astype(BF16)
        return carry

    lax.fori_loop(0, 5, write, 0)
    total[...] = collect(part_c, land_c, full_c, 7)

    @pl.when(ts < n_ts - 1)
    def _():
        halo.wait_send()

    settle(clip, mates, send_sem.at[5])
    settle(sent, team - 1, send_sem.at[6])
    settle(sent_f, team - 1, send_sem.at[10])
    settle(clip, 1, send_sem.at[15])
    settle(clip, mates, send_sem.at[16])
    settle(back, team - 1, send_sem.at[9])


def store_kernel(result, total, embed_rows, output, grad, grad_block, sems):
    large = pltpu.make_async_copy(result, output, sems.at[0])
    large.start()
    grad_block[...] = t_mm(embed_rows[...], total[...])
    small = pltpu.make_async_copy(grad_block, grad, sems.at[1])
    small.start()
    large.wait()
    small.wait()


def shards(
    clip_video, conv_weight, embed_weight, gain_spatial, gain_temporal, input_spatial,
    input_temporal, output_spatial, output_temporal, cotangent,
):
    frames, height, columns, channels = clip_video.shape
    rows, triple = input_spatial.shape
    head = triple // 3
    width = embed_weight.shape[-1]
    places = height * columns
    tokens = frames * places
    n_dp, n_ts = lax.axis_size("dp"), lax.axis_size("ts")
    n = n_dp * n_ts
    team = FR // frames
    share = places // team
    pad = -(-frames * share // 8) * 8
    reach = max(i * rows % 128 + rows for i in range(n))
    window = -(-reach // 128) * 128

    token = np.arange(tokens)
    frame, spot = token // places, token % places
    slot = spot // share * pad + frame * share + spot % share
    held = team * pad
    perm = np.zeros((held, tokens), np.float32)
    perm[slot, token] = 1.0
    frame_bias = np.where(np.arange(pad)[:, None] // share == frame[None, :], 0.0, masked)
    seat = np.arange(held)
    local = seat % pad
    when = seat // pad * frames + local // share
    allowed = (
        (local[:, None] % share == local[None, :] % share)
        & (when[:, None] >= when[None, :])
        & (local[:, None] < frames * share)
        & (local[None, :] < frames * share)
    )
    clip_bias = np.where(allowed, 0.0, masked)
    edge = np.zeros((tokens, 128), np.float32)
    edge[:, 0] = spot // columns >= 1
    edge[:, 1] = spot // columns < height - 1
    edge[:, 2] = spot % columns >= 1
    edge[:, 3] = spot % columns < columns - 1

    dims = (n_dp, n_ts, frames, places, columns, team, pad, rows, window)
    any_space = pl.BlockSpec(memory_space=pltpu.HBM)
    vmem = pl.BlockSpec(memory_space=pltpu.VMEM)
    buffer = lambda *shape: pltpu.VMEM(shape, BF16)
    wide = lambda *shape: pltpu.VMEM(shape, F32)
    result, total, embed_rows = pl.pallas_call(
        functools.partial(whole_kernel, dims),
        out_shape=(
            jax.ShapeDtypeStruct((tokens, width), BF16),
            jax.ShapeDtypeStruct((head, triple), BF16),
            jax.ShapeDtypeStruct((head, rows), BF16),
        ),
        in_specs=[any_space] * 14,
        out_specs=(vmem, vmem, vmem),
        scratch_shapes=[
            buffer(frames, places, channels), buffer(2, places, channels),
            buffer(*conv_weight.shape), buffer(3 * head, width), wide(1, width), wide(1, width),
            buffer(rows, triple), buffer(rows, triple), buffer(tokens, width),
            buffer(held, tokens), buffer(pad, tokens), buffer(held, held),
            buffer(tokens, 128),
            buffer(REDUCERS // 2, 24, 128), buffer(REDUCERS // 2, 48, 128),
            buffer(REDUCERS // 2, 24, 128), buffer(REDUCERS // 2, 48, 128),
            buffer(REDUCERS, 24, 128), buffer(REDUCERS, 48, 128), buffer(REDUCERS, 24, 128),
            buffer(n // 2, 24, 128), buffer(n // 2, 48, 128), buffer(n, 24, 128),
            buffer(REDUCERS, 24, 128), buffer(REDUCERS, 48, 128), buffer(REDUCERS, 24, 128),
            buffer(team, tokens, head),
            buffer(team, pad, 2 * head), buffer(team, pad, 2 * head),
            buffer(team, pad, head), buffer(team, pad, head),
            buffer(team, pad, 2 * head), buffer(team, pad, 2 * head),
            wide(2 * head, 2 * head), wide(tokens, 2 * head),
            pltpu.SemaphoreType.DMA((14,)), pltpu.SemaphoreType.DMA((17,)),
            pltpu.SemaphoreType.DMA((17,)),
        ],
        compiler_params=pltpu.CompilerParams(
            collective_id=0, has_side_effects=True, vmem_limit_bytes=36 * 1024 * 1024
        ),
    )(*(pltpu.with_memory_space_constraint(x, pltpu.HBM) for x in (
        clip_video.reshape(frames, places, channels),
        conv_weight,
        embed_weight,
        gain_spatial.reshape(1, width),
        gain_temporal.reshape(1, width),
        input_spatial,
        input_temporal,
        output_spatial,
        output_temporal,
        cotangent.reshape(tokens, width),
        jnp.asarray(perm, BF16),
        jnp.asarray(frame_bias, BF16),
        jnp.asarray(clip_bias, BF16),
        jnp.asarray(edge, BF16),
    )))
    output, grad = pl.pallas_call(
        store_kernel,
        out_shape=(
            jax.ShapeDtypeStruct((tokens, width), BF16),
            jax.ShapeDtypeStruct((rows, triple), F32),
        ),
        in_specs=[pl.BlockSpec(memory_space=pl.ANY), vmem, vmem],
        out_specs=(any_space, any_space),
        scratch_shapes=[wide(rows, triple), pltpu.SemaphoreType.DMA((2,))],
        compiler_params=pltpu.CompilerParams(vmem_limit_bytes=4 * 1024 * 1024),
    )(result, total, embed_rows)
    return output.reshape(frames, height, columns, width), grad


def solution(mesh):
    placed = (
        P(("dp", "ts"), None, None, None), P(), P(), P(), P(), P(("dp", "ts"), None),
        P(("dp", "ts"), None), P(), P(), P(("dp", "ts"), None, None, None),
    )
    return jax.shard_map(
        shards,
        mesh=mesh,
        in_specs=placed,
        out_specs=(P(("dp", "ts"), None, None, None), P(("dp", "ts"), None)),
        check_vma=False,
    )
```

```python
import functools

import jax
import jax.numpy as jnp
import numpy as np
from jax import lax
from jax.experimental import pallas as pl
from jax.experimental.pallas import tpu as pltpu
from jax.sharding import PartitionSpec as P

FR = 16
REDUCERS = 16
epsilon = 1e-06
masked = -1e30
F32 = jnp.float32
BF16 = jnp.bfloat16
MESH = pl.DeviceIdType.MESH


def mm(a, b, dims=((1,), (0,))):
    return lax.dot_general(a, b, (dims, ((), ())), preferred_element_type=F32)


def mm_t(a, b):
    return mm(a, b, ((1,), (1,)))


def t_mm(a, b):
    return mm(a, b, ((0,), (0,)))


def wide_mm(a, b):
    high = b.astype(BF16)
    low = (b - high.astype(F32)).astype(BF16)
    return mm(a, high) + mm(a, low)


def softmax(scores):
    raised = jnp.exp(scores - jnp.max(scores, axis=-1, keepdims=True))
    return raised * (1.0 / jnp.sum(raised, axis=-1, keepdims=True))


def softmax_grad(attend, grad_attend):
    inner = jnp.sum(grad_attend * attend, axis=-1, keepdims=True)
    return attend * (grad_attend - inner)


def stacked(block):
    third = block.shape[1] // 3
    return jnp.concatenate([block[:, i * third : (i + 1) * third] for i in range(3)], axis=0)


def unstacked(block):
    third = block.shape[0] // 3
    return jnp.concatenate([block[i * third : (i + 1) * third] for i in range(3)], axis=1)


def moved(block, distance):
    if distance == 0:
        return block
    return pltpu.roll(block, distance % block.shape[0], 0)


def whole_kernel(
    dims,
    video_hbm, conv_hbm, embed_hbm, gain_s_hbm, gain_t_hbm, in_s_hbm, in_t_hbm, out_s_hbm,
    out_t_hbm, cot_hbm, perm_hbm, frame_bias_hbm, clip_bias_hbm, edge_hbm,
    result, total, embed_rows,
    video, prior, taps, basis, gain_s, gain_t, in_s, in_t, cot, perm, frame_bias, clip_bias, edge,
    twin_a, twin_b, pre_a, pre_b, part_a, part_b, part_c, land_a, land_b, land_c, full_a, full_b, full_c,
    clip, sent, got, sent_f, got_f, back, home, gram, direct,
    local_sem, send_sem, recv_sem,
):
    n_dp, n_ts, frames, places, columns, team, pad, rows, window = dims
    n = n_dp * n_ts
    head = 128
    width = basis.shape[1]
    tokens = frames * places
    dp, ts = lax.axis_index("dp"), lax.axis_index("ts")
    me = dp * n_ts + ts

    loads = [
        (in_s_hbm, in_s), (in_t_hbm, in_t), (gain_s_hbm, gain_s), (gain_t_hbm, gain_t),
        (embed_hbm, basis.at[0:head]), (out_s_hbm, basis.at[head : 2 * head]),
        (video_hbm, video), (edge_hbm, edge), (conv_hbm, taps), (perm_hbm, perm),
        (out_t_hbm, basis.at[2 * head : 3 * head]), (cot_hbm, cot),
        (frame_bias_hbm, frame_bias), (clip_bias_hbm, clip_bias),
    ]
    copies = [pltpu.make_async_copy(s, d, local_sem.at[i]) for i, (s, d) in enumerate(loads)]
    for copy in copies:
        copy.start()

    half, quarter = n_ts // 2, n_ts // 4
    barrier = pltpu.get_barrier_semaphore()

    def leading(dev):
        group, spot = dev // n_ts, lax.rem(dev, n_ts)
        place = group * (half // 2) + (spot - quarter) // 2
        inside = jnp.logical_and(spot >= quarter, spot < quarter + half)
        return jnp.logical_and(inside, place < REDUCERS // 2)

    leads = leading(me)

    pairs = REDUCERS // 2
    seat = lax.rem(ts, team)
    base = me - seat

    def leader(side, i):
        return i // (half // 2) * n_ts + quarter + 2 * lax.rem(i, half // 2) + side

    def greet(dev):
        pl.semaphore_signal(
            barrier, inc=1, device_id=(dev // n_ts, lax.rem(dev, n_ts)), device_id_type=MESH
        )

    def greet_any(i, carry):
        dev = lax.rem(i, n_dp) * n_ts + i // n_dp

        @pl.when(dev != me)
        def _():
            greet(dev)

        return carry

    @pl.when(leads)
    def _():
        lax.fori_loop(0, n, greet_any, 0)

    def greet_mate(i, count):
        dev = base + lax.rem(seat + i, team)

        @pl.when(jnp.logical_not(leads))
        def _():
            greet(dev)

        return count + jnp.where(leading(dev), 0, 1)

    @pl.when(jnp.logical_and(jnp.logical_not(leads), jnp.logical_and(seat == 0, ts > 0)))
    def _():
        greet(me - 1)

    last = jnp.logical_and(seat == team - 1, ts < n_ts - 1)
    after = jnp.logical_and(last, jnp.logical_not(leading(me + 1)))
    greeted = lax.fori_loop(1, team, greet_mate, REDUCERS + jnp.where(after, 1, 0))
    greeted = greeted - jnp.where(leads, 1, 0)

    def remote(src, dst, index, dev):
        return pltpu.make_async_remote_copy(
            src_ref=src, dst_ref=dst, send_sem=send_sem.at[index], recv_sem=recv_sem.at[index],
            device_id=(dev // n_ts, lax.rem(dev, n_ts)), device_id_type=MESH,
        )

    def settle(ref, count, sem):
        piece = ref.at[pl.ds(0, count)]
        pltpu.make_async_copy(piece, piece, sem).wait()

    core = lax.rem(ts, 2)
    partner = me + 1 - 2 * core
    seated = dp * (half // 2) + (ts - quarter) // 2
    mine = core * pairs + seated

    def scatter(part, land, index):
        def step(i, carry):
            r = lax.rem(me + i, REDUCERS)
            dev = leader(r // pairs, lax.rem(r, pairs))

            @pl.when(dev != me)
            def _():
                remote(part.at[r], land.at[me], index, dev).start()

            return carry

        lax.fori_loop(0, REDUCERS, step, 0)

    def gather(part, land, full, index):
        @pl.when(leads)
        def _():
            land[pl.ds(me, 1)] = part[pl.ds(mine, 1)]
            settle(land, n - 1, recv_sem.at[index])
            total = jnp.sum(land[...].astype(F32), axis=0, keepdims=True)
            full[pl.ds(mine, 1)] = total.astype(BF16)

            def step(i, carry):
                dev = lax.rem(me + i, n)
                remote(full.at[mine], full.at[mine], index + 1, dev).start()
                return carry

            lax.fori_loop(1, n, step, 0)

    def collect(part, land, full, index):
        @pl.when(leads)
        def _():
            settle(full, REDUCERS - 1, recv_sem.at[index + 1])
            settle(part, REDUCERS - 1, send_sem.at[index])
            settle(land, n - 1, send_sem.at[index + 1])

        @pl.when(jnp.logical_not(leads))
        def _():
            settle(full, REDUCERS, recv_sem.at[index + 1])
            settle(part, REDUCERS, send_sem.at[index])

        return unstacked(full[...].astype(F32).reshape(-1, head)).astype(BF16)

    def pair_start(part, twin, index):
        other = pl.ds((1 - core) * pairs, pairs)
        remote(part.at[other], twin, index, partner).start()

    def pair_scatter(part, twin, pre, land, index, pair_index):
        settle(twin, pairs, recv_sem.at[pair_index])
        own = part[pl.ds(core * pairs, pairs)].astype(F32)
        pre[...] = (own + twin[...].astype(F32)).astype(BF16)

        def step(i, carry):
            r = lax.rem(me // 2 + i, pairs)
            dev = leader(core, r)

            @pl.when(dev != me)
            def _():
                remote(pre.at[r], land.at[me // 2], index, dev).start()

            return carry

        lax.fori_loop(0, pairs, step, 0)

    def pair_gather(pre, land, full, index):
        @pl.when(leads)
        def _():
            land[pl.ds(me // 2, 1)] = pre[pl.ds(seated, 1)]
            settle(land, n // 2 - 1, recv_sem.at[index])
            total = jnp.sum(land[...].astype(F32), axis=0, keepdims=True)
            full[pl.ds(mine, 1)] = total.astype(BF16)

            def step(i, carry):
                dev = 2 * lax.rem(me // 2 + i, n // 2) + core
                remote(full.at[mine], full.at[mine], index + 1, dev).start()
                return carry

            lax.fori_loop(1, n // 2, step, 0)

    def pair_forward(pre, land, full, index, pair_index):
        @pl.when(leads)
        def _():
            settle(full, pairs - 1, recv_sem.at[index + 1])
            settle(pre, pairs - 1, send_sem.at[index])
            settle(land, n // 2 - 1, send_sem.at[index + 1])

        @pl.when(jnp.logical_not(leads))
        def _():
            settle(full, pairs, recv_sem.at[index + 1])
            settle(pre, pairs, send_sem.at[index])

        own = pl.ds(core * pairs, pairs)
        remote(full.at[own], full.at[own], pair_index + 2, partner).start()

    def pair_collect(twin, full, pair_index):
        settle(full, pairs, recv_sem.at[pair_index + 2])
        settle(twin, pairs, send_sem.at[pair_index])
        settle(full, pairs, send_sem.at[pair_index + 2])
        return unstacked(full[...].astype(F32).reshape(-1, head)).astype(BF16)

    for copy in copies[:6]:
        copy.wait()
    first = me * rows
    start = pl.multiple_of(first // 128 * 128, 128)
    if (n * rows - rows) // 128 * 128 + window > width:
        limit = width - window
        start = pl.multiple_of(jnp.where(start > limit, limit, start), 128)
    shift = first - start
    place = lax.broadcasted_iota(jnp.int32, (window, rows), 0)
    source = lax.broadcasted_iota(jnp.int32, (window, rows), 1)
    chosen = jnp.where(place == source + shift, 1.0, 0.0).astype(BF16)
    spread_s = mm(chosen, in_s[...]).astype(BF16)
    spread_t = mm(chosen, in_t[...]).astype(BF16)
    span = basis[0 : 2 * head, pl.ds(start, window)].astype(F32)
    span_s = (span[:head] * gain_s[:, pl.ds(start, window)]).astype(BF16)
    span_t = (span * gain_t[:, pl.ds(start, window)]).astype(BF16)
    part_a[...] = stacked(mm(span_s, spread_s)).reshape(part_a.shape).astype(BF16)
    part_b[...] = stacked(mm(span_t, spread_t)).reshape(part_b.shape).astype(BF16)
    copies[6].wait()

    pl.semaphore_wait(barrier, greeted)
    halo = remote(video.at[pl.ds(frames - 2, 2)], prior, 0, me + 1)
    halo_in = remote(video.at[pl.ds(frames - 2, 2)], prior, 0, me)

    @pl.when(ts < n_ts - 1)
    def _():
        halo.start()

    pair_start(part_a, twin_a, 11)
    pair_start(part_b, twin_b, 12)
    chunk = width // 5
    gram[...] = jnp.zeros_like(gram)
    direct[...] = jnp.zeros_like(direct)

    def gram_slab(i, carry):
        pair = basis[0 : 2 * head, pl.ds(pl.multiple_of(i * chunk, 128), chunk)]
        gram[...] += mm_t(pair, pair)
        return carry

    lax.fori_loop(0, 3, gram_slab, 0)
    pair_scatter(part_a, twin_a, pre_a, land_a, 1, 11)
    pair_scatter(part_b, twin_b, pre_b, land_b, 3, 12)
    lax.fori_loop(3, 5, gram_slab, 0)
    embed_rows[...] = mm(span_s, chosen).astype(BF16)

    @pl.when(ts == 0)
    def _():
        prior[...] = jnp.zeros_like(prior)

    @pl.when(ts > 0)
    def _():
        halo_in.wait_recv()

    for copy in copies[7:10]:
        copy.wait()
    volume = jnp.concatenate([prior[...], video[...]], axis=0)
    deep = jnp.concatenate(
        [volume[2 - a : 2 - a + frames].reshape(tokens, head) for a in range(3)], axis=1
    )
    edges = edge[...].astype(F32)
    by_col = [None, None, None]
    for b in range(3):
        weight = jnp.concatenate(
            [jnp.concatenate([taps[a, b, e] for a in range(3)], axis=0) for e in range(3)], axis=1
        )
        product = mm(deep, weight)
        product = moved(product, -(b - 1) * columns)
        if b == 0:
            product = product * edges[:, 0:1]
        if b == 2:
            product = product * edges[:, 1:2]
        for e in range(3):
            piece = product[:, e * head : (e + 1) * head]
            by_col[e] = piece if by_col[e] is None else by_col[e] + piece
    summed = (
        by_col[1] + moved(by_col[0], 1) * edges[:, 2:3] + moved(by_col[2], -1) * edges[:, 3:4]
    )
    features = jax.nn.gelu(summed, approximate=True).astype(BF16)

    grams = gram[...]

    def factor_of(tokens_in):
        squares = jnp.sum(
            wide_mm(tokens_in, grams[:head, :head]) * tokens_in.astype(F32),
            axis=-1, keepdims=True,
        )
        return lax.rsqrt(jnp.maximum(squares, 0.0) / width + epsilon)

    def swap(source_of, target, index):
        def step(i, carry):
            other = lax.rem(seat + i, team)
            remote(source_of(other), target.at[seat], index, base + other).start()
            return carry

        lax.fori_loop(1, team, step, 0)

    sent_f[...] = mm(perm[...], features).reshape(sent_f.shape).astype(BF16)
    swap(lambda other: sent_f.at[other], got_f, 10)
    got_f[pl.ds(seat, 1)] = sent_f[pl.ds(seat, 1)]
    scaled = (features.astype(F32) * factor_of(features)).astype(BF16)
    clip[pl.ds(seat, 1)] = scaled.astype(F32).reshape(1, tokens, head).astype(BF16)
    mates = team // 2 - 1

    def mate(i):
        return lax.rem(seat + 2 * i, team)

    def clip_send(i, carry):
        remote(clip.at[seat], clip.at[seat], 5, base + mate(i)).start()
        return carry

    lax.fori_loop(1, mates + 1, clip_send, 0)
    remote(clip.at[seat], clip.at[seat], 15, partner).start()

    pair_gather(pre_a, land_a, full_a, 1)

    for copy in copies[10:]:
        copy.wait()

    def direct_slab(i, carry):
        cols = pl.ds(pl.multiple_of(i * chunk, 128), chunk)
        direct[...] += mm_t(cot[:, cols], basis[head : 3 * head, cols])
        return carry

    lax.fori_loop(0, 5, direct_slab, 0)
    pair_gather(pre_b, land_b, full_b, 3)
    dealt = mm(perm[...], direct[...].astype(BF16))
    sent[...] = dealt.reshape(sent.shape).astype(BF16)
    swap(lambda other: sent.at[other], got, 6)
    got[pl.ds(seat, 1)] = sent[pl.ds(seat, 1)]


    def own_rows(ref):
        return ref[...].astype(F32).reshape(team * pad, -1)

    settle(got_f, team - 1, recv_sem.at[10])
    own = own_rows(got_f).astype(BF16)
    factor_one = factor_of(own)
    own_scaled = (own.astype(F32) * factor_one).astype(BF16)
    settle(clip, mates, recv_sem.at[5])

    def clip_forward(i, carry):
        remote(clip.at[mate(i)], clip.at[mate(i)], 16, partner).start()
        return carry

    lax.fori_loop(1, mates + 1, clip_forward, 0)
    pair_forward(pre_a, land_a, full_a, 1, 11)
    settle(clip, 1, recv_sem.at[15])
    settle(clip, mates, recv_sem.at[16])
    scale = head ** -0.5

    def by_slot(form, values):
        return [
            form(values[i * pad : (i + 1) * pad].astype(BF16), clip[i]) for i in range(team)
        ]

    map_space = pair_collect(twin_a, full_a, 11)
    map_q, map_k, map_v = (map_space[:, i * head : (i + 1) * head] for i in range(3))
    q = mm(own_scaled, map_q).astype(BF16)
    apart = frame_bias[...].astype(F32)
    scores = [score + apart for score in by_slot(mm_t, mm_t(q, map_k) * scale)]
    attend_one = softmax(jnp.concatenate(scores, axis=0))
    pair_forward(pre_b, land_b, full_b, 3, 12)
    looked = jnp.concatenate(by_slot(mm, attend_one), axis=0).astype(BF16)
    mixture_one = mm(looked, map_v).astype(BF16)
    joint = jnp.concatenate([own, mixture_one], axis=-1)
    spread = wide_mm(joint, grams)
    squares = jnp.sum(spread * joint.astype(F32), axis=-1, keepdims=True)
    factor_two = lax.rsqrt(jnp.maximum(squares, 0.0) / width + epsilon)
    settle(got, team - 1, recv_sem.at[6])
    arrived = own_rows(got)
    direct_s, g_time = arrived[:, :head], arrived[:, head:].astype(BF16)
    map_time = pair_collect(twin_b, full_b, 12)
    packed_two = (mm(joint, map_time) * factor_two).astype(BF16)
    tq, tk, tv = (packed_two[:, i * head : (i + 1) * head] for i in range(3))
    attend_two = softmax(mm_t(tq, tk) * scale + clip_bias[...].astype(F32))
    attend_bf = attend_two.astype(BF16)
    mixture_two = mm(attend_bf, tv).astype(BF16)
    back[...] = (
        jnp.concatenate([mixture_one, mixture_two], axis=-1)
        .astype(F32).reshape(back.shape).astype(BF16)
    )
    home[pl.ds(seat, 1)] = back[pl.ds(seat, 1)]

    grad_scores = softmax_grad(attend_two, mm_t(g_time, tv)).astype(BF16)
    grad_two = jnp.concatenate(
        [mm(grad_scores, tk) * scale, t_mm(grad_scores, tq) * scale, t_mm(attend_bf, g_time)],
        axis=-1,
    ).astype(BF16)
    inner = jnp.sum(grad_two.astype(F32) * packed_two.astype(F32), axis=-1, keepdims=True)
    g_space = (
        direct_s
        + factor_two * mm_t(grad_two, map_time[head:])
        - (factor_two * factor_two * inner / width) * spread[:, head:]
    ).astype(BF16)
    grad_attend = jnp.concatenate(by_slot(mm_t, mm_t(g_space, map_v)), axis=0)
    looked_back = by_slot(mm, softmax_grad(attend_one, grad_attend))
    looked_back = jnp.concatenate(looked_back, axis=0).astype(BF16)
    cross = (t_mm(own_scaled, looked_back) * scale).astype(BF16)
    part = jnp.concatenate([mm(cross, map_k), t_mm(cross, map_q), t_mm(looked, g_space)], axis=1)
    part_c[...] = stacked(part).reshape(part_c.shape).astype(BF16)
    scatter(part_c, land_c, 7)
    swap(lambda other: back.at[other], home, 9)
    gather(part_c, land_c, full_c, 7)

    settle(home, team - 1, recv_sem.at[9])
    returned = home[...].astype(F32).reshape(team * pad, 2 * head).astype(BF16)
    triple = jnp.concatenate([features, t_mm(perm[...], returned).astype(BF16)], axis=-1)

    def write(i, carry):
        cols = pl.ds(pl.multiple_of(i * chunk, 128), chunk)
        result[:, cols] = mm(triple, basis[:, cols]).astype(BF16)
        return carry

    lax.fori_loop(0, 5, write, 0)
    total[...] = collect(part_c, land_c, full_c, 7)

    @pl.when(ts < n_ts - 1)
    def _():
        halo.wait_send()

    settle(clip, mates, send_sem.at[5])
    settle(sent, team - 1, send_sem.at[6])
    settle(sent_f, team - 1, send_sem.at[10])
    settle(clip, 1, send_sem.at[15])
    settle(clip, mates, send_sem.at[16])
    settle(back, team - 1, send_sem.at[9])


def store_kernel(result, total, embed_rows, output, grad, grad_block, sems):
    large = pltpu.make_async_copy(result, output, sems.at[0])
    large.start()
    grad_block[...] = t_mm(embed_rows[...], total[...])
    small = pltpu.make_async_copy(grad_block, grad, sems.at[1])
    small.start()
    large.wait()
    small.wait()


def shards(
    clip_video, conv_weight, embed_weight, gain_spatial, gain_temporal, input_spatial,
    input_temporal, output_spatial, output_temporal, cotangent,
):
    frames, height, columns, channels = clip_video.shape
    rows, triple = input_spatial.shape
    head = triple // 3
    width = embed_weight.shape[-1]
    places = height * columns
    tokens = frames * places
    n_dp, n_ts = lax.axis_size("dp"), lax.axis_size("ts")
    n = n_dp * n_ts
    team = FR // frames
    share = places // team
    pad = -(-frames * share // 8) * 8
    reach = max(i * rows % 128 + rows for i in range(n))
    window = -(-reach // 128) * 128

    token = np.arange(tokens)
    frame, spot = token // places, token % places
    slot = spot // share * pad + frame * share + spot % share
    held = team * pad
    perm = np.zeros((held, tokens), np.float32)
    perm[slot, token] = 1.0
    frame_bias = np.where(np.arange(pad)[:, None] // share == frame[None, :], 0.0, masked)
    seat = np.arange(held)
    local = seat % pad
    when = seat // pad * frames + local // share
    allowed = (
        (local[:, None] % share == local[None, :] % share)
        & (when[:, None] >= when[None, :])
        & (local[:, None] < frames * share)
        & (local[None, :] < frames * share)
    )
    clip_bias = np.where(allowed, 0.0, masked)
    edge = np.zeros((tokens, 128), np.float32)
    edge[:, 0] = spot // columns >= 1
    edge[:, 1] = spot // columns < height - 1
    edge[:, 2] = spot % columns >= 1
    edge[:, 3] = spot % columns < columns - 1

    dims = (n_dp, n_ts, frames, places, columns, team, pad, rows, window)
    any_space = pl.BlockSpec(memory_space=pltpu.HBM)
    vmem = pl.BlockSpec(memory_space=pltpu.VMEM)
    buffer = lambda *shape: pltpu.VMEM(shape, BF16)
    wide = lambda *shape: pltpu.VMEM(shape, F32)
    result, total, embed_rows = pl.pallas_call(
        functools.partial(whole_kernel, dims),
        out_shape=(
            jax.ShapeDtypeStruct((tokens, width), BF16),
            jax.ShapeDtypeStruct((head, triple), BF16),
            jax.ShapeDtypeStruct((head, rows), BF16),
        ),
        in_specs=[any_space] * 14,
        out_specs=(vmem, vmem, vmem),
        scratch_shapes=[
            buffer(frames, places, channels), buffer(2, places, channels),
            buffer(*conv_weight.shape), buffer(3 * head, width), wide(1, width), wide(1, width),
            buffer(rows, triple), buffer(rows, triple), buffer(tokens, width),
            buffer(held, tokens), buffer(pad, tokens), buffer(held, held),
            buffer(tokens, 128),
            buffer(REDUCERS // 2, 24, 128), buffer(REDUCERS // 2, 48, 128),
            buffer(REDUCERS // 2, 24, 128), buffer(REDUCERS // 2, 48, 128),
            buffer(REDUCERS, 24, 128), buffer(REDUCERS, 48, 128), buffer(REDUCERS, 24, 128),
            buffer(n // 2, 24, 128), buffer(n // 2, 48, 128), buffer(n, 24, 128),
            buffer(REDUCERS, 24, 128), buffer(REDUCERS, 48, 128), buffer(REDUCERS, 24, 128),
            buffer(team, tokens, head),
            buffer(team, pad, 2 * head), buffer(team, pad, 2 * head),
            buffer(team, pad, head), buffer(team, pad, head),
            buffer(team, pad, 2 * head), buffer(team, pad, 2 * head),
            wide(2 * head, 2 * head), wide(tokens, 2 * head),
            pltpu.SemaphoreType.DMA((14,)), pltpu.SemaphoreType.DMA((17,)),
            pltpu.SemaphoreType.DMA((17,)),
        ],
        compiler_params=pltpu.CompilerParams(
            collective_id=0, has_side_effects=True, vmem_limit_bytes=36 * 1024 * 1024
        ),
    )(*(pltpu.with_memory_space_constraint(x, pltpu.HBM) for x in (
        clip_video.reshape(frames, places, channels),
        conv_weight,
        embed_weight,
        gain_spatial.reshape(1, width),
        gain_temporal.reshape(1, width),
        input_spatial,
        input_temporal,
        output_spatial,
        output_temporal,
        cotangent.reshape(tokens, width),
        jnp.asarray(perm, BF16),
        jnp.asarray(frame_bias, BF16),
        jnp.asarray(clip_bias, BF16),
        jnp.asarray(edge, BF16),
    )))
    output, grad = pl.pallas_call(
        store_kernel,
        out_shape=(
            jax.ShapeDtypeStruct((tokens, width), BF16),
            jax.ShapeDtypeStruct((rows, triple), F32),
        ),
        in_specs=[pl.BlockSpec(memory_space=pl.ANY), vmem, vmem],
        out_specs=(any_space, any_space),
        scratch_shapes=[wide(rows, triple), pltpu.SemaphoreType.DMA((2,))],
        compiler_params=pltpu.CompilerParams(vmem_limit_bytes=4 * 1024 * 1024),
    )(result, total, embed_rows)
    return output.reshape(frames, height, columns, width), grad


def solution(mesh):
    placed = (
        P(("dp", "ts"), None, None, None), P(), P(), P(), P(), P(("dp", "ts"), None),
        P(("dp", "ts"), None), P(), P(), P(("dp", "ts"), None, None, None),
    )
    return jax.shard_map(
        shards,
        mesh=mesh,
        in_specs=placed,
        out_specs=(P(("dp", "ts"), None, None, None), P(("dp", "ts"), None)),
        check_vma=False,
    )
```

```python
import functools

import jax
import jax.numpy as jnp
import numpy as np
from jax import lax
from jax.experimental import pallas as pl
from jax.experimental.pallas import tpu as pltpu
from jax.sharding import PartitionSpec as P

FR = 16
REDUCERS = 16
epsilon = 1e-06
masked = -1e30
F32 = jnp.float32
BF16 = jnp.bfloat16
MESH = pl.DeviceIdType.MESH


def mm(a, b, dims=((1,), (0,))):
    return lax.dot_general(a, b, (dims, ((), ())), preferred_element_type=F32)


def mm_t(a, b):
    return mm(a, b, ((1,), (1,)))


def t_mm(a, b):
    return mm(a, b, ((0,), (0,)))


def wide_mm(a, b):
    high = b.astype(BF16)
    low = (b - high.astype(F32)).astype(BF16)
    return mm(a, high) + mm(a, low)


def softmax(scores):
    raised = jnp.exp(scores - jnp.max(scores, axis=-1, keepdims=True))
    return raised * (1.0 / jnp.sum(raised, axis=-1, keepdims=True))


def softmax_grad(attend, grad_attend):
    inner = jnp.sum(grad_attend * attend, axis=-1, keepdims=True)
    return attend * (grad_attend - inner)


def stacked(block):
    third = block.shape[1] // 3
    return jnp.concatenate([block[:, i * third : (i + 1) * third] for i in range(3)], axis=0)


def unstacked(block):
    third = block.shape[0] // 3
    return jnp.concatenate([block[i * third : (i + 1) * third] for i in range(3)], axis=1)


def moved(block, distance):
    if distance == 0:
        return block
    return pltpu.roll(block, distance % block.shape[0], 0)


def whole_kernel(
    dims,
    video_hbm, conv_hbm, embed_hbm, gain_s_hbm, gain_t_hbm, in_s_hbm, in_t_hbm, out_s_hbm,
    out_t_hbm, cot_hbm, perm_hbm, frame_bias_hbm, clip_bias_hbm, edge_hbm,
    result, total, embed_rows,
    video, prior, shifted, taps, basis, gain_s, gain_t, in_s, in_t, cot, perm, frame_bias, clip_bias, edge,
    twin_a, twin_b, pre_a, pre_b, part_a, part_b, part_c, land_a, land_b, land_c, full_a, full_b, full_c,
    clip, sent, got, sent_f, got_f, back, home, gram, direct,
    local_sem, send_sem, recv_sem,
):
    n_dp, n_ts, frames, places, columns, team, pad, rows, window = dims
    n = n_dp * n_ts
    head = 128
    width = basis.shape[1]
    tokens = frames * places
    dp, ts = lax.axis_index("dp"), lax.axis_index("ts")
    me = dp * n_ts + ts

    loads = [
        (in_s_hbm, in_s), (in_t_hbm, in_t), (gain_s_hbm, gain_s), (gain_t_hbm, gain_t),
        (embed_hbm, basis.at[0:head]), (out_s_hbm, basis.at[head : 2 * head]),
        (video_hbm, video), (edge_hbm, edge), (conv_hbm, taps), (perm_hbm, perm),
        (out_t_hbm, basis.at[2 * head : 3 * head]), (cot_hbm, cot),
        (frame_bias_hbm, frame_bias), (clip_bias_hbm, clip_bias),
    ]
    copies = [pltpu.make_async_copy(s, d, local_sem.at[i]) for i, (s, d) in enumerate(loads)]
    for copy in copies:
        copy.start()

    half, quarter = n_ts // 2, n_ts // 4
    barrier = pltpu.get_barrier_semaphore()

    def leading(dev):
        group, spot = dev // n_ts, lax.rem(dev, n_ts)
        place = group * (half // 2) + (spot - quarter) // 2
        inside = jnp.logical_and(spot >= quarter, spot < quarter + half)
        return jnp.logical_and(inside, place < REDUCERS // 2)

    leads = leading(me)

    pairs = REDUCERS // 2
    seat = lax.rem(ts, team)
    base = me - seat

    def leader(side, i):
        return i // (half // 2) * n_ts + quarter + 2 * lax.rem(i, half // 2) + side

    def greet(dev):
        pl.semaphore_signal(
            barrier, inc=1, device_id=(dev // n_ts, lax.rem(dev, n_ts)), device_id_type=MESH
        )

    def greet_any(i, carry):
        dev = lax.rem(i, n_dp) * n_ts + i // n_dp

        @pl.when(dev != me)
        def _():
            greet(dev)

        return carry

    @pl.when(leads)
    def _():
        lax.fori_loop(0, n, greet_any, 0)

    def greet_mate(i, count):
        dev = base + lax.rem(seat + i, team)

        @pl.when(jnp.logical_not(leads))
        def _():
            greet(dev)

        return count + jnp.where(leading(dev), 0, 1)

    @pl.when(jnp.logical_and(jnp.logical_not(leads), jnp.logical_and(seat == 0, ts > 0)))
    def _():
        greet(me - 1)

    last = jnp.logical_and(seat == team - 1, ts < n_ts - 1)
    after = jnp.logical_and(last, jnp.logical_not(leading(me + 1)))
    greeted = lax.fori_loop(1, team, greet_mate, REDUCERS + jnp.where(after, 1, 0))
    greeted = greeted - jnp.where(leads, 1, 0)

    def remote(src, dst, index, dev):
        return pltpu.make_async_remote_copy(
            src_ref=src, dst_ref=dst, send_sem=send_sem.at[index], recv_sem=recv_sem.at[index],
            device_id=(dev // n_ts, lax.rem(dev, n_ts)), device_id_type=MESH,
        )

    def settle(ref, count, sem):
        piece = ref.at[pl.ds(0, count)]
        pltpu.make_async_copy(piece, piece, sem).wait()

    core = lax.rem(ts, 2)
    partner = me + 1 - 2 * core
    seated = dp * (half // 2) + (ts - quarter) // 2
    mine = core * pairs + seated

    def scatter(part, land, index):
        def step(i, carry):
            r = lax.rem(me + i, REDUCERS)
            dev = leader(r // pairs, lax.rem(r, pairs))

            @pl.when(dev != me)
            def _():
                remote(part.at[r], land.at[me], index, dev).start()

            return carry

        lax.fori_loop(0, REDUCERS, step, 0, unroll=4)

    def gather(part, land, full, index):
        @pl.when(leads)
        def _():
            land[pl.ds(me, 1)] = part[pl.ds(mine, 1)]
            settle(land, n - 1, recv_sem.at[index])
            total = jnp.sum(land[...].astype(F32), axis=0, keepdims=True)
            full[pl.ds(mine, 1)] = total.astype(BF16)

            def step(i, carry):
                dev = lax.rem(me + i, n)
                remote(full.at[mine], full.at[mine], index + 1, dev).start()
                return carry

            lax.fori_loop(1, n, step, 0, unroll=31)

    def collect(part, land, full, index):
        @pl.when(leads)
        def _():
            settle(full, REDUCERS - 1, recv_sem.at[index + 1])
            settle(part, REDUCERS - 1, send_sem.at[index])
            settle(land, n - 1, send_sem.at[index + 1])

        @pl.when(jnp.logical_not(leads))
        def _():
            settle(full, REDUCERS, recv_sem.at[index + 1])
            settle(part, REDUCERS, send_sem.at[index])

        return unstacked(full[...].astype(F32).reshape(-1, head)).astype(BF16)

    def pair_start(part, twin, index):
        other = pl.ds((1 - core) * pairs, pairs)
        remote(part.at[other], twin, index, partner).start()

    def pair_scatter(part, twin, pre, land, index, pair_index):
        settle(twin, pairs, recv_sem.at[pair_index])
        own = part[pl.ds(core * pairs, pairs)].astype(F32)
        pre[...] = (own + twin[...].astype(F32)).astype(BF16)

        def step(i, carry):
            r = lax.rem(me // 2 + i, pairs)
            dev = leader(core, r)

            @pl.when(dev != me)
            def _():
                remote(pre.at[r], land.at[me // 2], index, dev).start()

            return carry

        lax.fori_loop(0, pairs, step, 0, unroll=4)

    def pair_gather(pre, land, full, index):
        @pl.when(leads)
        def _():
            land[pl.ds(me // 2, 1)] = pre[pl.ds(seated, 1)]
            settle(land, n // 2 - 1, recv_sem.at[index])
            total = jnp.sum(land[...].astype(F32), axis=0, keepdims=True)
            full[pl.ds(mine, 1)] = total.astype(BF16)

            def step(i, carry):
                dev = 2 * lax.rem(me // 2 + i, n // 2) + core
                remote(full.at[mine], full.at[mine], index + 1, dev).start()
                return carry

            lax.fori_loop(1, n // 2, step, 0, unroll=15)

    def pair_forward(pre, land, full, index, pair_index):
        @pl.when(leads)
        def _():
            settle(full, pairs - 1, recv_sem.at[index + 1])
            settle(pre, pairs - 1, send_sem.at[index])
            settle(land, n // 2 - 1, send_sem.at[index + 1])

        @pl.when(jnp.logical_not(leads))
        def _():
            settle(full, pairs, recv_sem.at[index + 1])
            settle(pre, pairs, send_sem.at[index])

        own = pl.ds(core * pairs, pairs)
        remote(full.at[own], full.at[own], pair_index + 2, partner).start()

    def pair_collect(twin, full, pair_index):
        settle(full, pairs, recv_sem.at[pair_index + 2])
        settle(twin, pairs, send_sem.at[pair_index])
        settle(full, pairs, send_sem.at[pair_index + 2])
        if full.shape[1] % 16 == 0:
            return unstacked(full[...].reshape(-1, head))
        return unstacked(full[...].astype(F32).reshape(-1, head)).astype(BF16)

    for copy in copies[:6]:
        copy.wait()
    first = me * rows
    start = pl.multiple_of(first // 128 * 128, 128)
    if (n * rows - rows) // 128 * 128 + window > width:
        limit = width - window
        start = pl.multiple_of(jnp.where(start > limit, limit, start), 128)
    shift = first - start
    place = lax.broadcasted_iota(jnp.int32, (window, rows), 0)
    source = lax.broadcasted_iota(jnp.int32, (window, rows), 1)
    chosen = jnp.where(place == source + shift, 1.0, 0.0).astype(BF16)
    spread_s = mm(chosen, in_s[...]).astype(BF16)
    spread_t = mm(chosen, in_t[...]).astype(BF16)
    span = basis[0 : 2 * head, pl.ds(start, window)].astype(F32)
    span_s = (span[:head] * gain_s[:, pl.ds(start, window)]).astype(BF16)
    span_t = (span * gain_t[:, pl.ds(start, window)]).astype(BF16)
    part_a[...] = stacked(mm(span_s, spread_s)).reshape(part_a.shape).astype(BF16)
    part_b[...] = stacked(mm(span_t, spread_t)).reshape(part_b.shape).astype(BF16)
    blank = jnp.zeros((3, frames + 2, columns, head), BF16)
    shifted[:, :, 0:columns] = blank
    shifted[:, :, columns + places :] = blank
    copies[6].wait()

    pl.semaphore_wait(barrier, greeted)
    halo = remote(video.at[pl.ds(frames - 2, 2)], prior, 0, me + 1)
    halo_in = remote(video.at[pl.ds(frames - 2, 2)], prior, 0, me)

    @pl.when(ts < n_ts - 1)
    def _():
        halo.start()

    pair_start(part_a, twin_a, 11)
    pair_start(part_b, twin_b, 12)
    chunk = width // 5
    gram[...] = jnp.zeros_like(gram)
    direct[...] = jnp.zeros_like(direct)

    def gram_slab(i, carry):
        pair = basis[0 : 2 * head, pl.ds(pl.multiple_of(i * chunk, 128), chunk)]
        gram[...] += mm_t(pair, pair)
        return carry

    lax.fori_loop(0, 3, gram_slab, 0)
    pair_scatter(part_a, twin_a, pre_a, land_a, 1, 11)
    pair_scatter(part_b, twin_b, pre_b, land_b, 3, 12)
    lax.fori_loop(3, 5, gram_slab, 0)
    embed_rows[...] = mm(span_s, chosen).astype(BF16)

    for copy in copies[7:10]:
        copy.wait()
    edges = edge[...].astype(F32)
    sums = [None] * frames

    def lay(block, first):
        count = block.shape[0]
        flat = block.astype(F32).reshape(count * places, head)
        near = edges[: count * places]
        sides = (moved(flat, 1) * near[:, 2:3], flat, moved(flat, -1) * near[:, 3:4])
        for side, values in enumerate(sides):
            shifted[side, first : first + count, columns : columns + places] = (
                values.reshape(count, places, head).astype(BF16)
            )

    def convolve(sources):
        for source in sources:
            outs = [o for o in range(frames) if 0 <= o + 2 - source <= 2]
            for row in range(3):
                window = slice(row * columns, row * columns + places)
                left = jnp.concatenate([shifted[i, source, window] for i in range(3)], axis=1)
                right = [taps[o + 2 - source, row].reshape(3 * head, head) for o in outs]
                product = mm(left, jnp.concatenate(right, axis=1))
                for i, o in enumerate(outs):
                    piece = product[:, i * head : (i + 1) * head]
                    sums[o] = piece if sums[o] is None else sums[o] + piece

    lay(video[...], 2)
    convolve(range(2, frames + 2))

    @pl.when(ts == 0)
    def _():
        prior[...] = jnp.zeros_like(prior)

    @pl.when(ts > 0)
    def _():
        halo_in.wait_recv()

    lay(prior[...], 0)
    convolve(range(2))
    summed = jnp.concatenate(sums, axis=0)
    features = jax.nn.gelu(summed, approximate=True).astype(BF16)

    grams = gram[...]

    def factor_of(tokens_in):
        squares = jnp.sum(
            wide_mm(tokens_in, grams[:head, :head]) * tokens_in.astype(F32),
            axis=-1, keepdims=True,
        )
        return lax.rsqrt(jnp.maximum(squares, 0.0) / width + epsilon)

    def swap(source_of, target, index):
        def step(i, carry):
            other = lax.rem(seat + i, team)
            remote(source_of(other), target.at[seat], index, base + other).start()
            return carry

        lax.fori_loop(1, team, step, 0, unroll=7)

    sent_f[...] = mm(perm[...], features).reshape(sent_f.shape).astype(BF16)
    swap(lambda other: sent_f.at[other], got_f, 10)
    got_f[pl.ds(seat, 1)] = sent_f[pl.ds(seat, 1)]
    scaled = (features.astype(F32) * factor_of(features)).astype(BF16)
    clip[pl.ds(seat, 1)] = scaled.astype(F32).reshape(1, tokens, head).astype(BF16)
    mates = team // 2 - 1

    def mate(i):
        return lax.rem(seat + 2 * i, team)

    for i in range(1, mates + 1):
        remote(clip.at[seat], clip.at[seat], 16 + i, base + mate(i)).start()
    remote(clip.at[seat], clip.at[seat], 15, partner).start()

    pair_gather(pre_a, land_a, full_a, 1)

    for copy in copies[10:]:
        copy.wait()

    def direct_slab(i, carry):
        cols = pl.ds(pl.multiple_of(i * chunk, 128), chunk)
        direct[...] += mm_t(cot[:, cols], basis[head : 3 * head, cols])
        return carry

    lax.fori_loop(0, 5, direct_slab, 0)
    pair_gather(pre_b, land_b, full_b, 3)
    dealt = mm(perm[...], direct[...].astype(BF16))
    sent[...] = dealt.reshape(sent.shape).astype(BF16)
    swap(lambda other: sent.at[other], got, 6)
    got[pl.ds(seat, 1)] = sent[pl.ds(seat, 1)]


    def own_rows(ref):
        return ref[...].astype(F32).reshape(team * pad, -1)

    settle(got_f, team - 1, recv_sem.at[10])
    own = own_rows(got_f).astype(BF16)
    factor_one = factor_of(own)
    own_scaled = (own.astype(F32) * factor_one).astype(BF16)
    for i in range(1, mates + 1):
        settle(clip, 1, recv_sem.at[16 + i])
        came = mate(team // 2 - i)
        remote(clip.at[came], clip.at[came], 16, partner).start()
    pair_forward(pre_a, land_a, full_a, 1, 11)
    settle(clip, 1, recv_sem.at[15])
    settle(clip, mates, recv_sem.at[16])
    scale = head ** -0.5

    def by_slot(form, values):
        return [
            form(values[i * pad : (i + 1) * pad].astype(BF16), clip[i]) for i in range(team)
        ]

    map_space = pair_collect(twin_a, full_a, 11)
    map_q, map_k, map_v = (map_space[:, i * head : (i + 1) * head] for i in range(3))
    q = mm(own_scaled, map_q).astype(BF16)
    apart = frame_bias[...].astype(F32)
    scores = [score + apart for score in by_slot(mm_t, mm_t(q, map_k) * scale)]
    attend_one = softmax(jnp.concatenate(scores, axis=0))
    pair_forward(pre_b, land_b, full_b, 3, 12)
    looked = jnp.concatenate(by_slot(mm, attend_one), axis=0).astype(BF16)
    mixture_one = mm(looked, map_v).astype(BF16)
    joint = jnp.concatenate([own, mixture_one], axis=-1)
    spread = wide_mm(joint, grams)
    squares = jnp.sum(spread * joint.astype(F32), axis=-1, keepdims=True)
    factor_two = lax.rsqrt(jnp.maximum(squares, 0.0) / width + epsilon)
    settle(got, team - 1, recv_sem.at[6])
    arrived = own_rows(got)
    direct_s, g_time = arrived[:, :head], arrived[:, head:].astype(BF16)
    map_time = pair_collect(twin_b, full_b, 12)
    packed_two = (mm(joint, map_time) * factor_two).astype(BF16)
    tq, tk, tv = (packed_two[:, i * head : (i + 1) * head] for i in range(3))
    attend_two = softmax(mm_t(tq, tk) * scale + clip_bias[...].astype(F32))
    attend_bf = attend_two.astype(BF16)
    mixture_two = mm(attend_bf, tv).astype(BF16)
    back[...] = (
        jnp.concatenate([mixture_one, mixture_two], axis=-1)
        .astype(F32).reshape(back.shape).astype(BF16)
    )
    home[pl.ds(seat, 1)] = back[pl.ds(seat, 1)]

    grad_scores = softmax_grad(attend_two, mm_t(g_time, tv)).astype(BF16)
    grad_two = jnp.concatenate(
        [mm(grad_scores, tk) * scale, t_mm(grad_scores, tq) * scale, t_mm(attend_bf, g_time)],
        axis=-1,
    ).astype(BF16)
    inner = jnp.sum(grad_two.astype(F32) * packed_two.astype(F32), axis=-1, keepdims=True)
    g_space = (
        direct_s
        + factor_two * mm_t(grad_two, map_time[head:])
        - (factor_two * factor_two * inner / width) * spread[:, head:]
    ).astype(BF16)
    grad_attend = jnp.concatenate(by_slot(mm_t, mm_t(g_space, map_v)), axis=0)
    looked_back = by_slot(mm, softmax_grad(attend_one, grad_attend))
    looked_back = jnp.concatenate(looked_back, axis=0).astype(BF16)
    cross = (t_mm(own_scaled, looked_back) * scale).astype(BF16)
    part = jnp.concatenate([mm(cross, map_k), t_mm(cross, map_q), t_mm(looked, g_space)], axis=1)
    part_c[...] = stacked(part).reshape(part_c.shape).astype(BF16)
    scatter(part_c, land_c, 7)
    swap(lambda other: back.at[other], home, 9)
    gather(part_c, land_c, full_c, 7)

    settle(home, team - 1, recv_sem.at[9])
    returned = home[...].astype(F32).reshape(team * pad, 2 * head).astype(BF16)
    triple = jnp.concatenate([features, t_mm(perm[...], returned).astype(BF16)], axis=-1)

    def write(i, carry):
        cols = pl.ds(pl.multiple_of(i * chunk, 128), chunk)
        result[:, cols] = mm(triple, basis[:, cols]).astype(BF16)
        return carry

    lax.fori_loop(0, 5, write, 0)
    total[...] = collect(part_c, land_c, full_c, 7)

    @pl.when(ts < n_ts - 1)
    def _():
        halo.wait_send()

    for i in range(1, mates + 1):
        settle(clip, 1, send_sem.at[16 + i])
    settle(sent, team - 1, send_sem.at[6])
    settle(sent_f, team - 1, send_sem.at[10])
    settle(clip, 1, send_sem.at[15])
    settle(clip, mates, send_sem.at[16])
    settle(back, team - 1, send_sem.at[9])


def store_kernel(result, total, embed_rows, output, grad, grad_block, sems):
    large = pltpu.make_async_copy(result, output, sems.at[0])
    large.start()
    grad_block[...] = t_mm(embed_rows[...], total[...])
    small = pltpu.make_async_copy(grad_block, grad, sems.at[1])
    small.start()
    large.wait()
    small.wait()


def shards(
    clip_video, conv_weight, embed_weight, gain_spatial, gain_temporal, input_spatial,
    input_temporal, output_spatial, output_temporal, cotangent,
):
    frames, height, columns, channels = clip_video.shape
    rows, triple = input_spatial.shape
    head = triple // 3
    width = embed_weight.shape[-1]
    places = height * columns
    tokens = frames * places
    n_dp, n_ts = lax.axis_size("dp"), lax.axis_size("ts")
    n = n_dp * n_ts
    team = FR // frames
    share = places // team
    pad = -(-frames * share // 8) * 8
    reach = max(i * rows % 128 + rows for i in range(n))
    window = -(-reach // 128) * 128

    token = np.arange(tokens)
    frame, spot = token // places, token % places
    slot = spot // share * pad + frame * share + spot % share
    held = team * pad
    perm = np.zeros((held, tokens), np.float32)
    perm[slot, token] = 1.0
    frame_bias = np.where(np.arange(pad)[:, None] // share == frame[None, :], 0.0, masked)
    seat = np.arange(held)
    local = seat % pad
    when = seat // pad * frames + local // share
    allowed = (
        (local[:, None] % share == local[None, :] % share)
        & (when[:, None] >= when[None, :])
        & (local[:, None] < frames * share)
        & (local[None, :] < frames * share)
    )
    clip_bias = np.where(allowed, 0.0, masked)
    edge = np.zeros((tokens, 128), np.float32)
    edge[:, 0] = spot // columns >= 1
    edge[:, 1] = spot // columns < height - 1
    edge[:, 2] = spot % columns >= 1
    edge[:, 3] = spot % columns < columns - 1

    dims = (n_dp, n_ts, frames, places, columns, team, pad, rows, window)
    any_space = pl.BlockSpec(memory_space=pltpu.HBM)
    vmem = pl.BlockSpec(memory_space=pltpu.VMEM)
    buffer = lambda *shape: pltpu.VMEM(shape, BF16)
    wide = lambda *shape: pltpu.VMEM(shape, F32)
    result, total, embed_rows = pl.pallas_call(
        functools.partial(whole_kernel, dims),
        out_shape=(
            jax.ShapeDtypeStruct((tokens, width), BF16),
            jax.ShapeDtypeStruct((head, triple), BF16),
            jax.ShapeDtypeStruct((head, rows), BF16),
        ),
        in_specs=[any_space] * 14,
        out_specs=(vmem, vmem, vmem),
        scratch_shapes=[
            buffer(frames, places, channels), buffer(2, places, channels),
            buffer(3, frames + 2, places + 2 * columns, channels),
            buffer(*conv_weight.shape), buffer(3 * head, width), wide(1, width), wide(1, width),
            buffer(rows, triple), buffer(rows, triple), buffer(tokens, width),
            buffer(held, tokens), buffer(pad, tokens), buffer(held, held),
            buffer(tokens, 128),
            buffer(REDUCERS // 2, 24, 128), buffer(REDUCERS // 2, 48, 128),
            buffer(REDUCERS // 2, 24, 128), buffer(REDUCERS // 2, 48, 128),
            buffer(REDUCERS, 24, 128), buffer(REDUCERS, 48, 128), buffer(REDUCERS, 24, 128),
            buffer(n // 2, 24, 128), buffer(n // 2, 48, 128), buffer(n, 24, 128),
            buffer(REDUCERS, 24, 128), buffer(REDUCERS, 48, 128), buffer(REDUCERS, 24, 128),
            buffer(team, tokens, head),
            buffer(team, pad, 2 * head), buffer(team, pad, 2 * head),
            buffer(team, pad, head), buffer(team, pad, head),
            buffer(team, pad, 2 * head), buffer(team, pad, 2 * head),
            wide(2 * head, 2 * head), wide(tokens, 2 * head),
            pltpu.SemaphoreType.DMA((14,)), pltpu.SemaphoreType.DMA((20,)),
            pltpu.SemaphoreType.DMA((20,)),
        ],
        compiler_params=pltpu.CompilerParams(
            collective_id=0, has_side_effects=True, vmem_limit_bytes=36 * 1024 * 1024
        ),
    )(*(pltpu.with_memory_space_constraint(x, pltpu.HBM) for x in (
        clip_video.reshape(frames, places, channels),
        conv_weight,
        embed_weight,
        gain_spatial.reshape(1, width),
        gain_temporal.reshape(1, width),
        input_spatial,
        input_temporal,
        output_spatial,
        output_temporal,
        cotangent.reshape(tokens, width),
        jnp.asarray(perm, BF16),
        jnp.asarray(frame_bias, BF16),
        jnp.asarray(clip_bias, BF16),
        jnp.asarray(edge, BF16),
    )))
    output, grad = pl.pallas_call(
        store_kernel,
        out_shape=(
            jax.ShapeDtypeStruct((tokens, width), BF16),
            jax.ShapeDtypeStruct((rows, triple), F32),
        ),
        in_specs=[pl.BlockSpec(memory_space=pl.ANY), vmem, vmem],
        out_specs=(any_space, any_space),
        scratch_shapes=[wide(rows, triple), pltpu.SemaphoreType.DMA((2,))],
        compiler_params=pltpu.CompilerParams(vmem_limit_bytes=4 * 1024 * 1024),
    )(result, total, embed_rows)
    return output.reshape(frames, height, columns, width), grad


def solution(mesh):
    placed = (
        P(("dp", "ts"), None, None, None), P(), P(), P(), P(), P(("dp", "ts"), None),
        P(("dp", "ts"), None), P(), P(), P(("dp", "ts"), None, None, None),
    )
    return jax.shard_map(
        shards,
        mesh=mesh,
        in_specs=placed,
        out_specs=(P(("dp", "ts"), None, None, None), P(("dp", "ts"), None)),
        check_vma=False,
    )
```

```python
import functools

import jax
import jax.numpy as jnp
import numpy as np
from jax import lax
from jax.experimental import pallas as pl
from jax.experimental.pallas import tpu as pltpu
from jax.sharding import PartitionSpec as P

FR = 16
REDUCERS = 16
epsilon = 1e-06
masked = -1e30
F32 = jnp.float32
BF16 = jnp.bfloat16
MESH = pl.DeviceIdType.MESH


def mm(a, b, dims=((1,), (0,))):
    return lax.dot_general(a, b, (dims, ((), ())), preferred_element_type=F32)


def mm_t(a, b):
    return mm(a, b, ((1,), (1,)))


def t_mm(a, b):
    return mm(a, b, ((0,), (0,)))


def softmax(scores):
    raised = jnp.exp(scores - jnp.max(scores, axis=-1, keepdims=True))
    return raised * (1.0 / jnp.sum(raised, axis=-1, keepdims=True))


def softmax_grad(attend, grad_attend):
    inner = jnp.sum(grad_attend * attend, axis=-1, keepdims=True)
    return attend * (grad_attend - inner)


def stacked(block):
    third = block.shape[1] // 3
    return jnp.concatenate([block[:, i * third : (i + 1) * third] for i in range(3)], axis=0)


def unstacked(block):
    third = block.shape[0] // 3
    return jnp.concatenate([block[i * third : (i + 1) * third] for i in range(3)], axis=1)


def moved(block, distance):
    if distance == 0:
        return block
    return pltpu.roll(block, distance % block.shape[0], 0)


def whole_kernel(
    dims,
    video_hbm, conv_hbm, embed_hbm, gain_s_hbm, gain_t_hbm, in_s_hbm, in_t_hbm, out_s_hbm,
    out_t_hbm, cot_hbm, perm_hbm, frame_bias_hbm, clip_bias_hbm, edge_hbm,
    result, total, embed_rows,
    video, prior, shifted, taps, basis, gain_s, gain_t, in_s, in_t, cot, perm, frame_bias, clip_bias, edge,
    twin_a, twin_b, pre_a, pre_b, part_a, part_b, part_c, land_a, land_b, land_c, full_a, full_b, full_c,
    clip, sent, got, sent_f, got_f, back, home, gram, direct,
    local_sem, send_sem, recv_sem,
):
    n_dp, n_ts, frames, places, columns, team, pad, rows, window = dims
    n = n_dp * n_ts
    head = 128
    width = basis.shape[1]
    tokens = frames * places
    dp, ts = lax.axis_index("dp"), lax.axis_index("ts")
    me = dp * n_ts + ts

    loads = [
        (in_s_hbm, in_s), (in_t_hbm, in_t), (gain_s_hbm, gain_s), (gain_t_hbm, gain_t),
        (embed_hbm, basis.at[0:head]), (out_s_hbm, basis.at[head : 2 * head]),
        (video_hbm, video), (edge_hbm, edge), (conv_hbm, taps), (perm_hbm, perm),
        (out_t_hbm, basis.at[2 * head : 3 * head]), (cot_hbm, cot),
        (frame_bias_hbm, frame_bias), (clip_bias_hbm, clip_bias),
    ]
    copies = [pltpu.make_async_copy(s, d, local_sem.at[i]) for i, (s, d) in enumerate(loads)]
    for copy in copies:
        copy.start()

    half, quarter = n_ts // 2, n_ts // 4
    barrier = pltpu.get_barrier_semaphore()

    def leading(dev):
        group, spot = dev // n_ts, lax.rem(dev, n_ts)
        place = group * (half // 2) + (spot - quarter) // 2
        inside = jnp.logical_and(spot >= quarter, spot < quarter + half)
        return jnp.logical_and(inside, place < REDUCERS // 2)

    leads = leading(me)

    pairs = REDUCERS // 2
    seat = lax.rem(ts, team)
    base = me - seat

    def leader(side, i):
        return i // (half // 2) * n_ts + quarter + 2 * lax.rem(i, half // 2) + side

    def greet(dev):
        pl.semaphore_signal(
            barrier, inc=1, device_id=(dev // n_ts, lax.rem(dev, n_ts)), device_id_type=MESH
        )

    def greet_any(i, carry):
        dev = lax.rem(i, n_dp) * n_ts + i // n_dp

        @pl.when(dev != me)
        def _():
            greet(dev)

        return carry

    @pl.when(leads)
    def _():
        lax.fori_loop(0, n, greet_any, 0)

    def greet_mate(i, count):
        dev = base + lax.rem(seat + i, team)

        @pl.when(jnp.logical_not(leads))
        def _():
            greet(dev)

        return count + jnp.where(leading(dev), 0, 1)

    @pl.when(jnp.logical_and(jnp.logical_not(leads), jnp.logical_and(seat == 0, ts > 0)))
    def _():
        greet(me - 1)

    last = jnp.logical_and(seat == team - 1, ts < n_ts - 1)
    after = jnp.logical_and(last, jnp.logical_not(leading(me + 1)))
    greeted = lax.fori_loop(1, team, greet_mate, REDUCERS + jnp.where(after, 1, 0))
    greeted = greeted - jnp.where(leads, 1, 0)

    def remote(src, dst, index, dev):
        return pltpu.make_async_remote_copy(
            src_ref=src, dst_ref=dst, send_sem=send_sem.at[index], recv_sem=recv_sem.at[index],
            device_id=(dev // n_ts, lax.rem(dev, n_ts)), device_id_type=MESH,
        )

    def settle(ref, count, sem):
        piece = ref.at[pl.ds(0, count)]
        pltpu.make_async_copy(piece, piece, sem).wait()

    core = lax.rem(ts, 2)
    partner = me + 1 - 2 * core
    seated = dp * (half // 2) + (ts - quarter) // 2
    mine = core * pairs + seated

    def scatter(part, land, index):
        def step(i, carry):
            r = lax.rem(me + i, REDUCERS)
            dev = leader(r // pairs, lax.rem(r, pairs))

            @pl.when(dev != me)
            def _():
                remote(part.at[r], land.at[me], index, dev).start()

            return carry

        lax.fori_loop(0, REDUCERS, step, 0, unroll=4)

    def gather(part, land, full, index):
        @pl.when(leads)
        def _():
            land[pl.ds(me, 1)] = part[pl.ds(mine, 1)]
            settle(land, n - 1, recv_sem.at[index])
            total = jnp.sum(land[...].astype(F32), axis=0, keepdims=True)
            full[pl.ds(mine, 1)] = total.astype(BF16)

            def step(i, carry):
                dev = lax.rem(me + i, n)
                remote(full.at[mine], full.at[mine], index + 1, dev).start()
                return carry

            lax.fori_loop(1, n, step, 0, unroll=31)

    def collect(part, land, full, index):
        @pl.when(leads)
        def _():
            settle(full, REDUCERS - 1, recv_sem.at[index + 1])
            settle(part, REDUCERS - 1, send_sem.at[index])
            settle(land, n - 1, send_sem.at[index + 1])

        @pl.when(jnp.logical_not(leads))
        def _():
            settle(full, REDUCERS, recv_sem.at[index + 1])
            settle(part, REDUCERS, send_sem.at[index])

        return unstacked(full[...].astype(F32).reshape(-1, head)).astype(BF16)

    def pair_start(part, twin, index):
        other = pl.ds((1 - core) * pairs, pairs)
        remote(part.at[other], twin, index, partner).start()

    def pair_scatter(part, twin, pre, land, index, pair_index):
        settle(twin, pairs, recv_sem.at[pair_index])
        own = part[pl.ds(core * pairs, pairs)].astype(F32)
        pre[...] = (own + twin[...].astype(F32)).astype(BF16)

        def step(i, carry):
            r = lax.rem(me // 2 + i, pairs)
            dev = leader(core, r)

            @pl.when(dev != me)
            def _():
                remote(pre.at[r], land.at[me // 2], index, dev).start()

            return carry

        lax.fori_loop(0, pairs, step, 0, unroll=4)

    def pair_gather(pre, land, full, index):
        @pl.when(leads)
        def _():
            land[pl.ds(me // 2, 1)] = pre[pl.ds(seated, 1)]
            settle(land, n // 2 - 1, recv_sem.at[index])
            total = jnp.sum(land[...].astype(F32), axis=0, keepdims=True)
            full[pl.ds(mine, 1)] = total.astype(BF16)

            def step(i, carry):
                dev = 2 * lax.rem(me // 2 + i, n // 2) + core
                remote(full.at[mine], full.at[mine], index + 1, dev).start()
                return carry

            lax.fori_loop(1, n // 2, step, 0, unroll=15)

    def pair_forward(pre, land, full, index, pair_index):
        @pl.when(leads)
        def _():
            settle(full, pairs - 1, recv_sem.at[index + 1])
            settle(pre, pairs - 1, send_sem.at[index])
            settle(land, n // 2 - 1, send_sem.at[index + 1])

        @pl.when(jnp.logical_not(leads))
        def _():
            settle(full, pairs, recv_sem.at[index + 1])
            settle(pre, pairs, send_sem.at[index])

        own = pl.ds(core * pairs, pairs)
        remote(full.at[own], full.at[own], pair_index + 2, partner).start()

    def pair_collect(twin, full, pair_index):
        settle(full, pairs, recv_sem.at[pair_index + 2])
        settle(twin, pairs, send_sem.at[pair_index])
        settle(full, pairs, send_sem.at[pair_index + 2])
        if full.shape[1] % 16 == 0:
            return unstacked(full[...].reshape(-1, head))
        return unstacked(full[...].astype(F32).reshape(-1, head)).astype(BF16)

    for copy in copies[:6]:
        copy.wait()
    first = me * rows
    start = pl.multiple_of(first // 128 * 128, 128)
    if (n * rows - rows) // 128 * 128 + window > width:
        limit = width - window
        start = pl.multiple_of(jnp.where(start > limit, limit, start), 128)
    shift = first - start
    place = lax.broadcasted_iota(jnp.int32, (window, rows), 0)
    source = lax.broadcasted_iota(jnp.int32, (window, rows), 1)
    chosen = jnp.where(place == source + shift, 1.0, 0.0).astype(BF16)
    spread_s = mm(chosen, in_s[...]).astype(BF16)
    spread_t = mm(chosen, in_t[...]).astype(BF16)
    span = basis[0 : 2 * head, pl.ds(start, window)].astype(F32)
    span_s = (span[:head] * gain_s[:, pl.ds(start, window)]).astype(BF16)
    span_t = (span * gain_t[:, pl.ds(start, window)]).astype(BF16)
    part_a[...] = stacked(mm(span_s, spread_s)).reshape(part_a.shape).astype(BF16)
    part_b[...] = stacked(mm(span_t, spread_t)).reshape(part_b.shape).astype(BF16)
    blank = jnp.zeros((3, frames + 2, columns, head), BF16)
    shifted[:, :, 0:columns] = blank
    shifted[:, :, columns + places :] = blank
    copies[6].wait()

    pl.semaphore_wait(barrier, greeted)
    halo = remote(video.at[pl.ds(frames - 2, 2)], prior, 0, me + 1)
    halo_in = remote(video.at[pl.ds(frames - 2, 2)], prior, 0, me)

    @pl.when(ts < n_ts - 1)
    def _():
        halo.start()

    pair_start(part_a, twin_a, 11)
    pair_start(part_b, twin_b, 12)
    chunk = width // 5
    gram[...] = jnp.zeros_like(gram)
    direct[...] = jnp.zeros_like(direct)

    def gram_slab(i, carry):
        pair = basis[0 : 2 * head, pl.ds(pl.multiple_of(i * chunk, 128), chunk)]
        gram[...] += mm_t(pair, pair)
        return carry

    lax.fori_loop(0, 3, gram_slab, 0)
    pair_scatter(part_a, twin_a, pre_a, land_a, 1, 11)
    pair_scatter(part_b, twin_b, pre_b, land_b, 3, 12)
    lax.fori_loop(3, 5, gram_slab, 0)
    embed_rows[...] = mm(span_s, chosen).astype(BF16)

    for copy in copies[7:10]:
        copy.wait()
    edges = edge[...].astype(F32)
    sums = [None] * frames

    def lay(block, first):
        count = block.shape[0]
        flat = block.astype(F32).reshape(count * places, head)
        near = edges[: count * places]
        sides = (moved(flat, 1) * near[:, 2:3], flat, moved(flat, -1) * near[:, 3:4])
        for side, values in enumerate(sides):
            shifted[side, first : first + count, columns : columns + places] = (
                values.reshape(count, places, head).astype(BF16)
            )

    def convolve(sources):
        for source in sources:
            outs = [o for o in range(frames) if 0 <= o + 2 - source <= 2]
            for row in range(3):
                window = slice(row * columns, row * columns + places)
                left = jnp.concatenate([shifted[i, source, window] for i in range(3)], axis=1)
                right = [taps[o + 2 - source, row].reshape(3 * head, head) for o in outs]
                product = mm(left, jnp.concatenate(right, axis=1))
                for i, o in enumerate(outs):
                    piece = product[:, i * head : (i + 1) * head]
                    sums[o] = piece if sums[o] is None else sums[o] + piece

    lay(video[...], 2)
    convolve(range(2, frames + 2))

    @pl.when(ts == 0)
    def _():
        prior[...] = jnp.zeros_like(prior)

    @pl.when(ts > 0)
    def _():
        halo_in.wait_recv()

    lay(prior[...], 0)
    convolve(range(2))
    summed = jnp.concatenate(sums, axis=0)
    features = jax.nn.gelu(summed, approximate=True).astype(BF16)

    grams = gram[...].astype(BF16)

    def factor_of(tokens_in):
        squares = jnp.sum(
            mm(tokens_in, grams[:head, :head]) * tokens_in.astype(F32),
            axis=-1, keepdims=True,
        )
        return lax.rsqrt(jnp.maximum(squares, 0.0) / width + epsilon)

    def swap(source_of, target, index):
        def step(i, carry):
            other = lax.rem(seat + i, team)
            remote(source_of(other), target.at[seat], index, base + other).start()
            return carry

        lax.fori_loop(1, team, step, 0, unroll=7)

    sent_f[...] = mm(perm[...], features).reshape(sent_f.shape).astype(BF16)
    swap(lambda other: sent_f.at[other], got_f, 10)
    got_f[pl.ds(seat, 1)] = sent_f[pl.ds(seat, 1)]
    scaled = (features.astype(F32) * factor_of(features)).astype(BF16)
    clip[pl.ds(seat, 1)] = scaled.astype(F32).reshape(1, tokens, head).astype(BF16)
    mates = team // 2 - 1

    def mate(i):
        return lax.rem(seat + 2 * i, team)

    for i in range(1, mates + 1):
        remote(clip.at[seat], clip.at[seat], 16 + i, base + mate(i)).start()
    remote(clip.at[seat], clip.at[seat], 15, partner).start()

    pair_gather(pre_a, land_a, full_a, 1)

    for copy in copies[10:]:
        copy.wait()

    def direct_slab(i, carry):
        cols = pl.ds(pl.multiple_of(i * chunk, 128), chunk)
        direct[...] += mm_t(cot[:, cols], basis[head : 3 * head, cols])
        return carry

    lax.fori_loop(0, 5, direct_slab, 0)
    pair_gather(pre_b, land_b, full_b, 3)
    dealt = mm(perm[...], direct[...].astype(BF16))
    sent[...] = dealt.reshape(sent.shape).astype(BF16)
    swap(lambda other: sent.at[other], got, 6)
    got[pl.ds(seat, 1)] = sent[pl.ds(seat, 1)]


    def own_rows(ref):
        return ref[...].astype(F32).reshape(team * pad, -1)

    settle(got_f, team - 1, recv_sem.at[10])
    own = own_rows(got_f).astype(BF16)
    factor_one = factor_of(own)
    own_scaled = (own.astype(F32) * factor_one).astype(BF16)
    for i in range(1, mates + 1):
        settle(clip, 1, recv_sem.at[16 + i])
        came = mate(team // 2 - i)
        remote(clip.at[came], clip.at[came], 16, partner).start()
    pair_forward(pre_a, land_a, full_a, 1, 11)
    settle(clip, 1, recv_sem.at[15])
    settle(clip, mates, recv_sem.at[16])
    scale = head ** -0.5

    def by_slot(form, values):
        return [
            form(values[i * pad : (i + 1) * pad].astype(BF16), clip[i]) for i in range(team)
        ]

    map_space = pair_collect(twin_a, full_a, 11)
    map_q, map_k, map_v = (map_space[:, i * head : (i + 1) * head] for i in range(3))
    q = mm(own_scaled, map_q).astype(BF16)
    apart = frame_bias[...].astype(F32)
    scores = [score + apart for score in by_slot(mm_t, mm_t(q, map_k) * scale)]
    attend_one = softmax(jnp.concatenate(scores, axis=0))
    pair_forward(pre_b, land_b, full_b, 3, 12)
    looked = jnp.concatenate(by_slot(mm, attend_one), axis=0).astype(BF16)
    mixture_one = mm(looked, map_v).astype(BF16)
    joint = jnp.concatenate([own, mixture_one], axis=-1)
    spread = mm(joint, grams)
    squares = jnp.sum(spread * joint.astype(F32), axis=-1, keepdims=True)
    factor_two = lax.rsqrt(jnp.maximum(squares, 0.0) / width + epsilon)
    settle(got, team - 1, recv_sem.at[6])
    arrived = own_rows(got)
    direct_s, g_time = arrived[:, :head], arrived[:, head:].astype(BF16)
    map_time = pair_collect(twin_b, full_b, 12)
    packed_two = (mm(joint, map_time) * factor_two).astype(BF16)
    tq, tk, tv = (packed_two[:, i * head : (i + 1) * head] for i in range(3))
    attend_two = softmax(mm_t(tq, tk) * scale + clip_bias[...].astype(F32))
    attend_bf = attend_two.astype(BF16)
    mixture_two = mm(attend_bf, tv).astype(BF16)
    back[...] = (
        jnp.concatenate([mixture_one, mixture_two], axis=-1)
        .astype(F32).reshape(back.shape).astype(BF16)
    )
    home[pl.ds(seat, 1)] = back[pl.ds(seat, 1)]

    grad_scores = softmax_grad(attend_two, mm_t(g_time, tv)).astype(BF16)
    grad_two = jnp.concatenate(
        [mm(grad_scores, tk) * scale, t_mm(grad_scores, tq) * scale, t_mm(attend_bf, g_time)],
        axis=-1,
    ).astype(BF16)
    inner = jnp.sum(grad_two.astype(F32) * packed_two.astype(F32), axis=-1, keepdims=True)
    g_space = (
        direct_s
        + factor_two * mm_t(grad_two, map_time[head:])
        - (factor_two * factor_two * inner / width) * spread[:, head:]
    ).astype(BF16)
    grad_attend = jnp.concatenate(by_slot(mm_t, mm_t(g_space, map_v)), axis=0)
    looked_back = by_slot(mm, softmax_grad(attend_one, grad_attend))
    looked_back = jnp.concatenate(looked_back, axis=0).astype(BF16)
    cross = (t_mm(own_scaled, looked_back) * scale).astype(BF16)
    part = jnp.concatenate([mm(cross, map_k), t_mm(cross, map_q), t_mm(looked, g_space)], axis=1)
    part_c[...] = stacked(part).reshape(part_c.shape).astype(BF16)
    scatter(part_c, land_c, 7)
    swap(lambda other: back.at[other], home, 9)
    gather(part_c, land_c, full_c, 7)

    settle(home, team - 1, recv_sem.at[9])
    returned = home[...].astype(F32).reshape(team * pad, 2 * head).astype(BF16)
    triple = jnp.concatenate([features, t_mm(perm[...], returned).astype(BF16)], axis=-1)

    def write(i, carry):
        cols = pl.ds(pl.multiple_of(i * chunk, 128), chunk)
        result[:, cols] = mm(triple, basis[:, cols]).astype(BF16)
        return carry

    lax.fori_loop(0, 5, write, 0)
    total[...] = collect(part_c, land_c, full_c, 7)

    @pl.when(ts < n_ts - 1)
    def _():
        halo.wait_send()

    for i in range(1, mates + 1):
        settle(clip, 1, send_sem.at[16 + i])
    settle(sent, team - 1, send_sem.at[6])
    settle(sent_f, team - 1, send_sem.at[10])
    settle(clip, 1, send_sem.at[15])
    settle(clip, mates, send_sem.at[16])
    settle(back, team - 1, send_sem.at[9])


def store_kernel(result, total, embed_rows, output, grad, grad_block, sems):
    large = pltpu.make_async_copy(result, output, sems.at[0])
    large.start()
    grad_block[...] = t_mm(embed_rows[...], total[...])
    small = pltpu.make_async_copy(grad_block, grad, sems.at[1])
    small.start()
    large.wait()
    small.wait()


def shards(
    clip_video, conv_weight, embed_weight, gain_spatial, gain_temporal, input_spatial,
    input_temporal, output_spatial, output_temporal, cotangent,
):
    frames, height, columns, channels = clip_video.shape
    rows, triple = input_spatial.shape
    head = triple // 3
    width = embed_weight.shape[-1]
    places = height * columns
    tokens = frames * places
    n_dp, n_ts = lax.axis_size("dp"), lax.axis_size("ts")
    n = n_dp * n_ts
    team = FR // frames
    share = places // team
    pad = -(-frames * share // 8) * 8
    reach = max(i * rows % 128 + rows for i in range(n))
    window = -(-reach // 128) * 128

    token = np.arange(tokens)
    frame, spot = token // places, token % places
    slot = spot // share * pad + frame * share + spot % share
    held = team * pad
    perm = np.zeros((held, tokens), np.float32)
    perm[slot, token] = 1.0
    frame_bias = np.where(np.arange(pad)[:, None] // share == frame[None, :], 0.0, masked)
    seat = np.arange(held)
    local = seat % pad
    when = seat // pad * frames + local // share
    allowed = (
        (local[:, None] % share == local[None, :] % share)
        & (when[:, None] >= when[None, :])
        & (local[:, None] < frames * share)
        & (local[None, :] < frames * share)
    )
    clip_bias = np.where(allowed, 0.0, masked)
    edge = np.zeros((tokens, 128), np.float32)
    edge[:, 0] = spot // columns >= 1
    edge[:, 1] = spot // columns < height - 1
    edge[:, 2] = spot % columns >= 1
    edge[:, 3] = spot % columns < columns - 1

    dims = (n_dp, n_ts, frames, places, columns, team, pad, rows, window)
    any_space = pl.BlockSpec(memory_space=pltpu.HBM)
    vmem = pl.BlockSpec(memory_space=pltpu.VMEM)
    buffer = lambda *shape: pltpu.VMEM(shape, BF16)
    wide = lambda *shape: pltpu.VMEM(shape, F32)
    result, total, embed_rows = pl.pallas_call(
        functools.partial(whole_kernel, dims),
        out_shape=(
            jax.ShapeDtypeStruct((tokens, width), BF16),
            jax.ShapeDtypeStruct((head, triple), BF16),
            jax.ShapeDtypeStruct((head, rows), BF16),
        ),
        in_specs=[any_space] * 14,
        out_specs=(vmem, vmem, vmem),
        scratch_shapes=[
            buffer(frames, places, channels), buffer(2, places, channels),
            buffer(3, frames + 2, places + 2 * columns, channels),
            buffer(*conv_weight.shape), buffer(3 * head, width), wide(1, width), wide(1, width),
            buffer(rows, triple), buffer(rows, triple), buffer(tokens, width),
            buffer(held, tokens), buffer(pad, tokens), buffer(held, held),
            buffer(tokens, 128),
            buffer(REDUCERS // 2, 24, 128), buffer(REDUCERS // 2, 48, 128),
            buffer(REDUCERS // 2, 24, 128), buffer(REDUCERS // 2, 48, 128),
            buffer(REDUCERS, 24, 128), buffer(REDUCERS, 48, 128), buffer(REDUCERS, 24, 128),
            buffer(n // 2, 24, 128), buffer(n // 2, 48, 128), buffer(n, 24, 128),
            buffer(REDUCERS, 24, 128), buffer(REDUCERS, 48, 128), buffer(REDUCERS, 24, 128),
            buffer(team, tokens, head),
            buffer(team, pad, 2 * head), buffer(team, pad, 2 * head),
            buffer(team, pad, head), buffer(team, pad, head),
            buffer(team, pad, 2 * head), buffer(team, pad, 2 * head),
            wide(2 * head, 2 * head), wide(tokens, 2 * head),
            pltpu.SemaphoreType.DMA((14,)), pltpu.SemaphoreType.DMA((20,)),
            pltpu.SemaphoreType.DMA((20,)),
        ],
        compiler_params=pltpu.CompilerParams(
            collective_id=0, has_side_effects=True, vmem_limit_bytes=36 * 1024 * 1024
        ),
    )(*(pltpu.with_memory_space_constraint(x, pltpu.HBM) for x in (
        clip_video.reshape(frames, places, channels),
        conv_weight,
        embed_weight,
        gain_spatial.reshape(1, width),
        gain_temporal.reshape(1, width),
        input_spatial,
        input_temporal,
        output_spatial,
        output_temporal,
        cotangent.reshape(tokens, width),
        jnp.asarray(perm, BF16),
        jnp.asarray(frame_bias, BF16),
        jnp.asarray(clip_bias, BF16),
        jnp.asarray(edge, BF16),
    )))
    output, grad = pl.pallas_call(
        store_kernel,
        out_shape=(
            jax.ShapeDtypeStruct((tokens, width), BF16),
            jax.ShapeDtypeStruct((rows, triple), F32),
        ),
        in_specs=[pl.BlockSpec(memory_space=pl.ANY), vmem, vmem],
        out_specs=(any_space, any_space),
        scratch_shapes=[wide(rows, triple), pltpu.SemaphoreType.DMA((2,))],
        compiler_params=pltpu.CompilerParams(vmem_limit_bytes=4 * 1024 * 1024),
    )(result, total, embed_rows)
    return output.reshape(frames, height, columns, width), grad


def solution(mesh):
    placed = (
        P(("dp", "ts"), None, None, None), P(), P(), P(), P(), P(("dp", "ts"), None),
        P(("dp", "ts"), None), P(), P(), P(("dp", "ts"), None, None, None),
    )
    return jax.shard_map(
        shards,
        mesh=mesh,
        in_specs=placed,
        out_specs=(P(("dp", "ts"), None, None, None), P(("dp", "ts"), None)),
        check_vma=False,
    )
```

```python
import functools

import jax
import jax.numpy as jnp
import numpy as np
from jax import lax
from jax.experimental import pallas as pl
from jax.experimental.pallas import tpu as pltpu
from jax.sharding import PartitionSpec as P

FR = 16
REDUCERS = 16
epsilon = 1e-06
masked = -1e30
F32 = jnp.float32
BF16 = jnp.bfloat16
MESH = pl.DeviceIdType.MESH


def mm(a, b, dims=((1,), (0,))):
    return lax.dot_general(a, b, (dims, ((), ())), preferred_element_type=F32)


def mm_t(a, b):
    return mm(a, b, ((1,), (1,)))


def t_mm(a, b):
    return mm(a, b, ((0,), (0,)))


def softmax(scores):
    raised = jnp.exp(scores - jnp.max(scores, axis=-1, keepdims=True))
    return raised * (1.0 / jnp.sum(raised, axis=-1, keepdims=True))


def softmax_grad(attend, grad_attend):
    inner = jnp.sum(grad_attend * attend, axis=-1, keepdims=True)
    return attend * (grad_attend - inner)


def stacked(block):
    third = block.shape[1] // 3
    return jnp.concatenate([block[:, i * third : (i + 1) * third] for i in range(3)], axis=0)


def unstacked(block):
    third = block.shape[0] // 3
    return jnp.concatenate([block[i * third : (i + 1) * third] for i in range(3)], axis=1)


def moved(block, distance):
    if distance == 0:
        return block
    return pltpu.roll(block, distance % block.shape[0], 0)


def whole_kernel(
    dims,
    video_hbm, conv_hbm, embed_hbm, gain_s_hbm, gain_t_hbm, in_s_hbm, in_t_hbm, out_s_hbm,
    out_t_hbm, cot_hbm, perm_hbm, frame_bias_hbm, clip_bias_hbm, edge_hbm,
    result, total, embed_rows,
    video, prior, shifted, taps, basis, gain_s, gain_t, in_s, in_t, cot, perm, frame_bias, clip_bias, edge,
    twin_a, twin_b, pre_a, pre_b, part_a, part_b, part_c, land_a, land_b, land_c, full_a, full_b, full_c,
    clip, sent, got, sent_f, got_f, back, home, gram, direct,
    local_sem, send_sem, recv_sem,
):
    n_dp, n_ts, frames, places, columns, team, pad, rows, window = dims
    n = n_dp * n_ts
    head = 128
    width = basis.shape[1]
    tokens = frames * places
    dp, ts = lax.axis_index("dp"), lax.axis_index("ts")
    me = dp * n_ts + ts

    loads = [
        (in_s_hbm, in_s), (in_t_hbm, in_t), (gain_s_hbm, gain_s), (gain_t_hbm, gain_t),
        (embed_hbm, basis.at[0:head]), (out_s_hbm, basis.at[head : 2 * head]),
        (video_hbm, video), (edge_hbm, edge), (conv_hbm, taps), (perm_hbm, perm),
        (out_t_hbm, basis.at[2 * head : 3 * head]), (cot_hbm, cot),
        (frame_bias_hbm, frame_bias), (clip_bias_hbm, clip_bias),
    ]
    copies = [pltpu.make_async_copy(s, d, local_sem.at[i]) for i, (s, d) in enumerate(loads)]
    for copy in copies:
        copy.start()

    half, quarter = n_ts // 2, n_ts // 4
    barrier = pltpu.get_barrier_semaphore()

    def leading(dev):
        group, spot = dev // n_ts, lax.rem(dev, n_ts)
        place = group * (half // 2) + (spot - quarter) // 2
        inside = jnp.logical_and(spot >= quarter, spot < quarter + half)
        return jnp.logical_and(inside, place < REDUCERS // 2)

    leads = leading(me)

    pairs = REDUCERS // 2
    core = lax.rem(ts, 2)
    seat = lax.rem(ts, team)
    base = me - seat

    def leader(side, i):
        return i // (half // 2) * n_ts + quarter + 2 * lax.rem(i, half // 2) + side

    def greet(dev):
        pl.semaphore_signal(
            barrier, inc=1, device_id=(dev // n_ts, lax.rem(dev, n_ts)), device_id_type=MESH
        )

    def greet_same(i, carry):
        dev = lax.rem(i, n_dp) * n_ts + i // n_dp * 2 + core

        @pl.when(dev != me)
        def _():
            greet(dev)

        return carry

    @pl.when(leads)
    def _():
        lax.fori_loop(0, n // 2, greet_same, 0)

    def greet_mate(i, count):
        dev = base + lax.rem(seat + i, team)
        same = lax.rem(i, 2) == 0

        @pl.when(jnp.logical_not(jnp.logical_and(leads, same)))
        def _():
            greet(dev)

        return count + jnp.where(jnp.logical_and(leading(dev), same), 0, 1)

    @pl.when(jnp.logical_and(seat == 0, ts > 0))
    def _():
        greet(me - 1)

    after = jnp.logical_and(seat == team - 1, ts < n_ts - 1)
    greeted = lax.fori_loop(1, team, greet_mate, pairs + jnp.where(after, 1, 0))
    greeted = greeted - jnp.where(leads, 1, 0)

    def remote(src, dst, index, dev):
        return pltpu.make_async_remote_copy(
            src_ref=src, dst_ref=dst, send_sem=send_sem.at[index], recv_sem=recv_sem.at[index],
            device_id=(dev // n_ts, lax.rem(dev, n_ts)), device_id_type=MESH,
        )

    def settle(ref, count, sem):
        piece = ref.at[pl.ds(0, count)]
        pltpu.make_async_copy(piece, piece, sem).wait()

    partner = me + 1 - 2 * core
    seated = dp * (half // 2) + (ts - quarter) // 2
    mine = core * pairs + seated

    def scatter(part, land, index):
        def step(i, carry):
            r = lax.rem(me + i, REDUCERS)
            dev = leader(r // pairs, lax.rem(r, pairs))

            @pl.when(dev != me)
            def _():
                remote(part.at[r], land.at[me], index, dev).start()

            return carry

        lax.fori_loop(0, REDUCERS, step, 0, unroll=4)

    def gather(part, land, full, index):
        @pl.when(leads)
        def _():
            land[pl.ds(me, 1)] = part[pl.ds(mine, 1)]
            settle(land, n - 1, recv_sem.at[index])
            total = jnp.sum(land[...].astype(F32), axis=0, keepdims=True)
            full[pl.ds(mine, 1)] = total.astype(BF16)

            def step(i, carry):
                dev = lax.rem(me + i, n)
                remote(full.at[mine], full.at[mine], index + 1, dev).start()
                return carry

            lax.fori_loop(1, n, step, 0, unroll=31)

    def collect(part, land, full, index):
        @pl.when(leads)
        def _():
            settle(full, REDUCERS - 1, recv_sem.at[index + 1])
            settle(part, REDUCERS - 1, send_sem.at[index])
            settle(land, n - 1, send_sem.at[index + 1])

        @pl.when(jnp.logical_not(leads))
        def _():
            settle(full, REDUCERS, recv_sem.at[index + 1])
            settle(part, REDUCERS, send_sem.at[index])

        return unstacked(full[...].astype(F32).reshape(-1, head)).astype(BF16)

    def pair_start(part, twin, index):
        other = pl.ds((1 - core) * pairs, pairs)
        remote(part.at[other], twin, index, partner).start()

    def pair_scatter(part, twin, pre, land, index, pair_index):
        settle(twin, pairs, recv_sem.at[pair_index])
        own = part[pl.ds(core * pairs, pairs)].astype(F32)
        pre[...] = (own + twin[...].astype(F32)).astype(BF16)

        def step(i, carry):
            r = lax.rem(me // 2 + i, pairs)
            dev = leader(core, r)

            @pl.when(dev != me)
            def _():
                remote(pre.at[r], land.at[me // 2], index, dev).start()

            return carry

        lax.fori_loop(0, pairs, step, 0, unroll=4)

    def pair_gather(pre, land, full, index):
        @pl.when(leads)
        def _():
            land[pl.ds(me // 2, 1)] = pre[pl.ds(seated, 1)]
            settle(land, n // 2 - 1, recv_sem.at[index])
            total = jnp.sum(land[...].astype(F32), axis=0, keepdims=True)
            full[pl.ds(mine, 1)] = total.astype(BF16)

            def step(i, carry):
                dev = 2 * lax.rem(me // 2 + i, n // 2) + core
                remote(full.at[mine], full.at[mine], index + 1, dev).start()
                return carry

            lax.fori_loop(1, n // 2, step, 0, unroll=15)

    def pair_forward(pre, land, full, index, pair_index):
        @pl.when(leads)
        def _():
            settle(full, pairs - 1, recv_sem.at[index + 1])
            settle(pre, pairs - 1, send_sem.at[index])
            settle(land, n // 2 - 1, send_sem.at[index + 1])

        @pl.when(jnp.logical_not(leads))
        def _():
            settle(full, pairs, recv_sem.at[index + 1])
            settle(pre, pairs, send_sem.at[index])

        own = pl.ds(core * pairs, pairs)
        remote(full.at[own], full.at[own], pair_index + 2, partner).start()

    def pair_collect(twin, full, pair_index):
        settle(full, pairs, recv_sem.at[pair_index + 2])
        settle(twin, pairs, send_sem.at[pair_index])
        settle(full, pairs, send_sem.at[pair_index + 2])
        if full.shape[1] % 16 == 0:
            return unstacked(full[...].reshape(-1, head))
        return unstacked(full[...].astype(F32).reshape(-1, head)).astype(BF16)

    for copy in copies[:6]:
        copy.wait()
    first = me * rows
    start = pl.multiple_of(first // 128 * 128, 128)
    if (n * rows - rows) // 128 * 128 + window > width:
        limit = width - window
        start = pl.multiple_of(jnp.where(start > limit, limit, start), 128)
    shift = first - start
    place = lax.broadcasted_iota(jnp.int32, (window, rows), 0)
    source = lax.broadcasted_iota(jnp.int32, (window, rows), 1)
    chosen = jnp.where(place == source + shift, 1.0, 0.0).astype(BF16)
    spread_s = mm(chosen, in_s[...]).astype(BF16)
    spread_t = mm(chosen, in_t[...]).astype(BF16)
    span = basis[0 : 2 * head, pl.ds(start, window)].astype(F32)
    span_s = (span[:head] * gain_s[:, pl.ds(start, window)]).astype(BF16)
    span_t = (span * gain_t[:, pl.ds(start, window)]).astype(BF16)
    part_a[...] = stacked(mm(span_s, spread_s)).reshape(part_a.shape).astype(BF16)
    part_b[...] = stacked(mm(span_t, spread_t)).reshape(part_b.shape).astype(BF16)
    blank = jnp.zeros((3, frames + 2, columns, head), BF16)
    shifted[:, :, 0:columns] = blank
    shifted[:, :, columns + places :] = blank
    copies[6].wait()

    pl.semaphore_wait(barrier, greeted)
    halo = remote(video.at[pl.ds(frames - 2, 2)], prior, 0, me + 1)
    halo_in = remote(video.at[pl.ds(frames - 2, 2)], prior, 0, me)

    @pl.when(ts < n_ts - 1)
    def _():
        halo.start()

    pair_start(part_a, twin_a, 11)
    pair_start(part_b, twin_b, 12)
    chunk = width // 5
    gram[...] = jnp.zeros_like(gram)
    direct[...] = jnp.zeros_like(direct)

    def gram_slab(i, carry):
        pair = basis[0 : 2 * head, pl.ds(pl.multiple_of(i * chunk, 128), chunk)]
        gram[...] += mm_t(pair, pair)
        return carry

    lax.fori_loop(0, 3, gram_slab, 0)
    pair_scatter(part_a, twin_a, pre_a, land_a, 1, 11)
    pair_scatter(part_b, twin_b, pre_b, land_b, 3, 12)
    lax.fori_loop(3, 5, gram_slab, 0)
    embed_rows[...] = mm(span_s, chosen).astype(BF16)

    for copy in copies[7:10]:
        copy.wait()
    edges = edge[...].astype(F32)
    sums = [None] * frames

    def lay(block, first):
        count = block.shape[0]
        flat = block.astype(F32).reshape(count * places, head)
        near = edges[: count * places]
        sides = (moved(flat, 1) * near[:, 2:3], flat, moved(flat, -1) * near[:, 3:4])
        for side, values in enumerate(sides):
            shifted[side, first : first + count, columns : columns + places] = (
                values.reshape(count, places, head).astype(BF16)
            )

    def convolve(sources):
        for source in sources:
            outs = [o for o in range(frames) if 0 <= o + 2 - source <= 2]
            for row in range(3):
                window = slice(row * columns, row * columns + places)
                left = jnp.concatenate([shifted[i, source, window] for i in range(3)], axis=1)
                right = [taps[o + 2 - source, row].reshape(3 * head, head) for o in outs]
                product = mm(left, jnp.concatenate(right, axis=1))
                for i, o in enumerate(outs):
                    piece = product[:, i * head : (i + 1) * head]
                    sums[o] = piece if sums[o] is None else sums[o] + piece

    lay(video[...], 2)
    convolve(range(2, frames + 2))

    @pl.when(ts == 0)
    def _():
        prior[...] = jnp.zeros_like(prior)

    @pl.when(ts > 0)
    def _():
        halo_in.wait_recv()

    lay(prior[...], 0)
    convolve(range(2))
    summed = jnp.concatenate(sums, axis=0)
    features = jax.nn.gelu(summed, approximate=True).astype(BF16)

    grams = gram[...].astype(BF16)

    def factor_of(tokens_in):
        squares = jnp.sum(
            mm(tokens_in, grams[:head, :head]) * tokens_in.astype(F32),
            axis=-1, keepdims=True,
        )
        return lax.rsqrt(jnp.maximum(squares, 0.0) / width + epsilon)

    def swap(source_of, target, index):
        def step(i, carry):
            other = lax.rem(seat + i, team)
            remote(source_of(other), target.at[seat], index, base + other).start()
            return carry

        lax.fori_loop(1, team, step, 0, unroll=7)

    sent_f[...] = mm(perm[...], features).reshape(sent_f.shape).astype(BF16)
    swap(lambda other: sent_f.at[other], got_f, 10)
    got_f[pl.ds(seat, 1)] = sent_f[pl.ds(seat, 1)]
    scaled = (features.astype(F32) * factor_of(features)).astype(BF16)
    clip[pl.ds(seat, 1)] = scaled.astype(F32).reshape(1, tokens, head).astype(BF16)
    mates = team // 2 - 1

    def mate(i):
        return lax.rem(seat + 2 * i, team)

    for i in range(1, mates + 1):
        remote(clip.at[seat], clip.at[seat], 16 + i, base + mate(i)).start()
    remote(clip.at[seat], clip.at[seat], 15, partner).start()

    pair_gather(pre_a, land_a, full_a, 1)

    for copy in copies[10:]:
        copy.wait()

    def direct_slab(i, carry):
        cols = pl.ds(pl.multiple_of(i * chunk, 128), chunk)
        direct[...] += mm_t(cot[:, cols], basis[head : 3 * head, cols])
        return carry

    lax.fori_loop(0, 5, direct_slab, 0)
    pair_gather(pre_b, land_b, full_b, 3)
    dealt = mm(perm[...], direct[...].astype(BF16))
    sent[...] = dealt.reshape(sent.shape).astype(BF16)
    swap(lambda other: sent.at[other], got, 6)
    got[pl.ds(seat, 1)] = sent[pl.ds(seat, 1)]


    def own_rows(ref):
        return ref[...].astype(F32).reshape(team * pad, -1)

    settle(got_f, team - 1, recv_sem.at[10])
    own = own_rows(got_f).astype(BF16)
    factor_one = factor_of(own)
    own_scaled = (own.astype(F32) * factor_one).astype(BF16)
    for i in range(1, mates + 1):
        settle(clip, 1, recv_sem.at[16 + i])
        came = mate(team // 2 - i)
        remote(clip.at[came], clip.at[came], 16, partner).start()
    pair_forward(pre_a, land_a, full_a, 1, 11)
    settle(clip, 1, recv_sem.at[15])
    settle(clip, mates, recv_sem.at[16])
    scale = head ** -0.5

    def by_slot(form, values):
        return [
            form(values[i * pad : (i + 1) * pad].astype(BF16), clip[i]) for i in range(team)
        ]

    map_space = pair_collect(twin_a, full_a, 11)
    map_q, map_k, map_v = (map_space[:, i * head : (i + 1) * head] for i in range(3))
    q = mm(own_scaled, map_q).astype(BF16)
    apart = frame_bias[...].astype(F32)
    scores = [score + apart for score in by_slot(mm_t, mm_t(q, map_k) * scale)]
    attend_one = softmax(jnp.concatenate(scores, axis=0))
    pair_forward(pre_b, land_b, full_b, 3, 12)
    looked = jnp.concatenate(by_slot(mm, attend_one), axis=0).astype(BF16)
    mixture_one = mm(looked, map_v).astype(BF16)
    joint = jnp.concatenate([own, mixture_one], axis=-1)
    spread = mm(joint, grams)
    squares = jnp.sum(spread * joint.astype(F32), axis=-1, keepdims=True)
    factor_two = lax.rsqrt(jnp.maximum(squares, 0.0) / width + epsilon)
    settle(got, team - 1, recv_sem.at[6])
    arrived = own_rows(got)
    direct_s, g_time = arrived[:, :head], arrived[:, head:].astype(BF16)
    map_time = pair_collect(twin_b, full_b, 12)
    packed_two = (mm(joint, map_time) * factor_two).astype(BF16)
    tq, tk, tv = (packed_two[:, i * head : (i + 1) * head] for i in range(3))
    attend_two = softmax(mm_t(tq, tk) * scale + clip_bias[...].astype(F32))
    attend_bf = attend_two.astype(BF16)
    mixture_two = mm(attend_bf, tv).astype(BF16)
    back[...] = (
        jnp.concatenate([mixture_one, mixture_two], axis=-1)
        .astype(F32).reshape(back.shape).astype(BF16)
    )
    home[pl.ds(seat, 1)] = back[pl.ds(seat, 1)]

    grad_scores = softmax_grad(attend_two, mm_t(g_time, tv)).astype(BF16)
    grad_two = jnp.concatenate(
        [mm(grad_scores, tk) * scale, t_mm(grad_scores, tq) * scale, t_mm(attend_bf, g_time)],
        axis=-1,
    ).astype(BF16)
    inner = jnp.sum(grad_two.astype(F32) * packed_two.astype(F32), axis=-1, keepdims=True)
    g_space = (
        direct_s
        + factor_two * mm_t(grad_two, map_time[head:])
        - (factor_two * factor_two * inner / width) * spread[:, head:]
    ).astype(BF16)
    grad_attend = jnp.concatenate(by_slot(mm_t, mm_t(g_space, map_v)), axis=0)
    looked_back = by_slot(mm, softmax_grad(attend_one, grad_attend))
    looked_back = jnp.concatenate(looked_back, axis=0).astype(BF16)
    cross = (t_mm(own_scaled, looked_back) * scale).astype(BF16)
    part = jnp.concatenate([mm(cross, map_k), t_mm(cross, map_q), t_mm(looked, g_space)], axis=1)
    part_c[...] = stacked(part).reshape(part_c.shape).astype(BF16)
    scatter(part_c, land_c, 7)
    swap(lambda other: back.at[other], home, 9)
    gather(part_c, land_c, full_c, 7)

    settle(home, team - 1, recv_sem.at[9])
    returned = home[...].astype(F32).reshape(team * pad, 2 * head).astype(BF16)
    triple = jnp.concatenate([features, t_mm(perm[...], returned).astype(BF16)], axis=-1)

    def write(i, carry):
        cols = pl.ds(pl.multiple_of(i * chunk, 128), chunk)
        result[:, cols] = mm(triple, basis[:, cols]).astype(BF16)
        return carry

    lax.fori_loop(0, 5, write, 0)
    total[...] = collect(part_c, land_c, full_c, 7)

    @pl.when(ts < n_ts - 1)
    def _():
        halo.wait_send()

    for i in range(1, mates + 1):
        settle(clip, 1, send_sem.at[16 + i])
    settle(sent, team - 1, send_sem.at[6])
    settle(sent_f, team - 1, send_sem.at[10])
    settle(clip, 1, send_sem.at[15])
    settle(clip, mates, send_sem.at[16])
    settle(back, team - 1, send_sem.at[9])


def store_kernel(result, total, embed_rows, output, grad, grad_block, sems):
    large = pltpu.make_async_copy(result, output, sems.at[0])
    large.start()
    grad_block[...] = t_mm(embed_rows[...], total[...])
    small = pltpu.make_async_copy(grad_block, grad, sems.at[1])
    small.start()
    large.wait()
    small.wait()


def shards(
    clip_video, conv_weight, embed_weight, gain_spatial, gain_temporal, input_spatial,
    input_temporal, output_spatial, output_temporal, cotangent,
):
    frames, height, columns, channels = clip_video.shape
    rows, triple = input_spatial.shape
    head = triple // 3
    width = embed_weight.shape[-1]
    places = height * columns
    tokens = frames * places
    n_dp, n_ts = lax.axis_size("dp"), lax.axis_size("ts")
    n = n_dp * n_ts
    team = FR // frames
    share = places // team
    pad = -(-frames * share // 8) * 8
    reach = max(i * rows % 128 + rows for i in range(n))
    window = -(-reach // 128) * 128

    token = np.arange(tokens)
    frame, spot = token // places, token % places
    slot = spot // share * pad + frame * share + spot % share
    held = team * pad
    perm = np.zeros((held, tokens), np.float32)
    perm[slot, token] = 1.0
    frame_bias = np.where(np.arange(pad)[:, None] // share == frame[None, :], 0.0, masked)
    seat = np.arange(held)
    local = seat % pad
    when = seat // pad * frames + local // share
    allowed = (
        (local[:, None] % share == local[None, :] % share)
        & (when[:, None] >= when[None, :])
        & (local[:, None] < frames * share)
        & (local[None, :] < frames * share)
    )
    clip_bias = np.where(allowed, 0.0, masked)
    edge = np.zeros((tokens, 128), np.float32)
    edge[:, 0] = spot // columns >= 1
    edge[:, 1] = spot // columns < height - 1
    edge[:, 2] = spot % columns >= 1
    edge[:, 3] = spot % columns < columns - 1

    dims = (n_dp, n_ts, frames, places, columns, team, pad, rows, window)
    any_space = pl.BlockSpec(memory_space=pltpu.HBM)
    vmem = pl.BlockSpec(memory_space=pltpu.VMEM)
    buffer = lambda *shape: pltpu.VMEM(shape, BF16)
    wide = lambda *shape: pltpu.VMEM(shape, F32)
    result, total, embed_rows = pl.pallas_call(
        functools.partial(whole_kernel, dims),
        out_shape=(
            jax.ShapeDtypeStruct((tokens, width), BF16),
            jax.ShapeDtypeStruct((head, triple), BF16),
            jax.ShapeDtypeStruct((head, rows), BF16),
        ),
        in_specs=[any_space] * 14,
        out_specs=(vmem, vmem, vmem),
        scratch_shapes=[
            buffer(frames, places, channels), buffer(2, places, channels),
            buffer(3, frames + 2, places + 2 * columns, channels),
            buffer(*conv_weight.shape), buffer(3 * head, width), wide(1, width), wide(1, width),
            buffer(rows, triple), buffer(rows, triple), buffer(tokens, width),
            buffer(held, tokens), buffer(pad, tokens), buffer(held, held),
            buffer(tokens, 128),
            buffer(REDUCERS // 2, 24, 128), buffer(REDUCERS // 2, 48, 128),
            buffer(REDUCERS // 2, 24, 128), buffer(REDUCERS // 2, 48, 128),
            buffer(REDUCERS, 24, 128), buffer(REDUCERS, 48, 128), buffer(REDUCERS, 24, 128),
            buffer(n // 2, 24, 128), buffer(n // 2, 48, 128), buffer(n, 24, 128),
            buffer(REDUCERS, 24, 128), buffer(REDUCERS, 48, 128), buffer(REDUCERS, 24, 128),
            buffer(team, tokens, head),
            buffer(team, pad, 2 * head), buffer(team, pad, 2 * head),
            buffer(team, pad, head), buffer(team, pad, head),
            buffer(team, pad, 2 * head), buffer(team, pad, 2 * head),
            wide(2 * head, 2 * head), wide(tokens, 2 * head),
            pltpu.SemaphoreType.DMA((14,)), pltpu.SemaphoreType.DMA((20,)),
            pltpu.SemaphoreType.DMA((20,)),
        ],
        compiler_params=pltpu.CompilerParams(
            collective_id=0, has_side_effects=True, vmem_limit_bytes=36 * 1024 * 1024
        ),
    )(*(pltpu.with_memory_space_constraint(x, pltpu.HBM) for x in (
        clip_video.reshape(frames, places, channels),
        conv_weight,
        embed_weight,
        gain_spatial.reshape(1, width),
        gain_temporal.reshape(1, width),
        input_spatial,
        input_temporal,
        output_spatial,
        output_temporal,
        cotangent.reshape(tokens, width),
        jnp.asarray(perm, BF16),
        jnp.asarray(frame_bias, BF16),
        jnp.asarray(clip_bias, BF16),
        jnp.asarray(edge, BF16),
    )))
    output, grad = pl.pallas_call(
        store_kernel,
        out_shape=(
            jax.ShapeDtypeStruct((tokens, width), BF16),
            jax.ShapeDtypeStruct((rows, triple), F32),
        ),
        in_specs=[pl.BlockSpec(memory_space=pl.ANY), vmem, vmem],
        out_specs=(any_space, any_space),
        scratch_shapes=[wide(rows, triple), pltpu.SemaphoreType.DMA((2,))],
        compiler_params=pltpu.CompilerParams(vmem_limit_bytes=4 * 1024 * 1024),
    )(result, total, embed_rows)
    return output.reshape(frames, height, columns, width), grad


def solution(mesh):
    placed = (
        P(("dp", "ts"), None, None, None), P(), P(), P(), P(), P(("dp", "ts"), None),
        P(("dp", "ts"), None), P(), P(), P(("dp", "ts"), None, None, None),
    )
    return jax.shard_map(
        shards,
        mesh=mesh,
        in_specs=placed,
        out_specs=(P(("dp", "ts"), None, None, None), P(("dp", "ts"), None)),
        check_vma=False,
    )
```

```python
import functools

import jax
import jax.numpy as jnp
import numpy as np
from jax import lax
from jax.experimental import pallas as pl
from jax.experimental.pallas import tpu as pltpu
from jax.sharding import PartitionSpec as P

FR = 16
REDUCERS = 16
epsilon = 1e-06
masked = -1e30
F32 = jnp.float32
BF16 = jnp.bfloat16
MESH = pl.DeviceIdType.MESH


def mm(a, b, dims=((1,), (0,))):
    return lax.dot_general(a, b, (dims, ((), ())), preferred_element_type=F32)


def mm_t(a, b):
    return mm(a, b, ((1,), (1,)))


def t_mm(a, b):
    return mm(a, b, ((0,), (0,)))


def softmax(scores):
    raised = jnp.exp(scores - jnp.max(scores, axis=-1, keepdims=True))
    return raised * (1.0 / jnp.sum(raised, axis=-1, keepdims=True))


def softmax_grad(attend, grad_attend):
    inner = jnp.sum(grad_attend * attend, axis=-1, keepdims=True)
    return attend * (grad_attend - inner)


def stacked(block):
    third = block.shape[1] // 3
    return jnp.concatenate([block[:, i * third : (i + 1) * third] for i in range(3)], axis=0)


def unstacked(block):
    third = block.shape[0] // 3
    return jnp.concatenate([block[i * third : (i + 1) * third] for i in range(3)], axis=1)


def moved(block, distance):
    if distance == 0:
        return block
    return pltpu.roll(block, distance % block.shape[0], 0)


def whole_kernel(
    dims,
    video_hbm, conv_hbm, embed_hbm, gain_s_hbm, gain_t_hbm, in_s_hbm, in_t_hbm, out_s_hbm,
    out_t_hbm, cot_hbm, perm_hbm, frame_bias_hbm, clip_bias_hbm, edge_hbm,
    result, total, embed_rows,
    video, prior, shifted, taps, basis, gain_s, gain_t, in_s, in_t, cot, perm, frame_bias, clip_bias, edge,
    twin_a, twin_b, pre_a, pre_b, part_a, part_b, part_c, land_a, land_b, land_c, full_a, full_b, full_c,
    clip, sent, got, sent_f, got_f, back, home, gram, direct,
    local_sem, send_sem, recv_sem,
):
    n_dp, n_ts, frames, places, columns, team, pad, rows, window = dims
    n = n_dp * n_ts
    head = 128
    width = basis.shape[1]
    tokens = frames * places
    dp, ts = lax.axis_index("dp"), lax.axis_index("ts")
    me = dp * n_ts + ts

    loads = [
        (in_s_hbm, in_s), (in_t_hbm, in_t), (gain_s_hbm, gain_s), (gain_t_hbm, gain_t),
        (embed_hbm, basis.at[0:head]), (out_s_hbm, basis.at[head : 2 * head]),
        (video_hbm, video), (edge_hbm, edge), (conv_hbm, taps), (perm_hbm, perm),
        (out_t_hbm, basis.at[2 * head : 3 * head]), (cot_hbm, cot),
        (frame_bias_hbm, frame_bias), (clip_bias_hbm, clip_bias),
    ]
    copies = [pltpu.make_async_copy(s, d, local_sem.at[i]) for i, (s, d) in enumerate(loads)]
    for copy in copies[:7]:
        copy.start()

    half, quarter = n_ts // 2, n_ts // 4
    barrier = pltpu.get_barrier_semaphore()

    def leading(dev):
        group, spot = dev // n_ts, lax.rem(dev, n_ts)
        place = group * (half // 2) + (spot - quarter) // 2
        inside = jnp.logical_and(spot >= quarter, spot < quarter + half)
        return jnp.logical_and(inside, place < REDUCERS // 2)

    leads = leading(me)

    pairs = REDUCERS // 2
    core = lax.rem(ts, 2)
    seat = lax.rem(ts, team)
    base = me - seat

    def leader(side, i):
        return i // (half // 2) * n_ts + quarter + 2 * lax.rem(i, half // 2) + side

    def greet(dev):
        pl.semaphore_signal(
            barrier, inc=1, device_id=(dev // n_ts, lax.rem(dev, n_ts)), device_id_type=MESH
        )

    def greet_same(i, carry):
        dev = lax.rem(i, n_dp) * n_ts + i // n_dp * 2 + core

        @pl.when(dev != me)
        def _():
            greet(dev)

        return carry

    @pl.when(leads)
    def _():
        lax.fori_loop(0, n // 2, greet_same, 0)

    def greet_mate(i, count):
        dev = base + lax.rem(seat + i, team)
        same = lax.rem(i, 2) == 0

        @pl.when(jnp.logical_not(jnp.logical_and(leads, same)))
        def _():
            greet(dev)

        return count + jnp.where(jnp.logical_and(leading(dev), same), 0, 1)

    @pl.when(jnp.logical_and(seat == 0, ts > 0))
    def _():
        greet(me - 1)

    for copy in copies[7:]:
        copy.start()
    after = jnp.logical_and(seat == team - 1, ts < n_ts - 1)
    greeted = lax.fori_loop(1, team, greet_mate, pairs + jnp.where(after, 1, 0))
    greeted = greeted - jnp.where(leads, 1, 0)

    def remote(src, dst, index, dev):
        return pltpu.make_async_remote_copy(
            src_ref=src, dst_ref=dst, send_sem=send_sem.at[index], recv_sem=recv_sem.at[index],
            device_id=(dev // n_ts, lax.rem(dev, n_ts)), device_id_type=MESH,
        )

    def settle(ref, count, sem):
        piece = ref.at[pl.ds(0, count)]
        pltpu.make_async_copy(piece, piece, sem).wait()

    partner = me + 1 - 2 * core
    seated = dp * (half // 2) + (ts - quarter) // 2
    mine = core * pairs + seated

    def scatter(part, land, index):
        def step(i, carry):
            r = lax.rem(me + i, REDUCERS)
            dev = leader(r // pairs, lax.rem(r, pairs))

            @pl.when(dev != me)
            def _():
                remote(part.at[r], land.at[me], index, dev).start()

            return carry

        lax.fori_loop(0, REDUCERS, step, 0, unroll=4)

    def gather(part, land, full, index):
        @pl.when(leads)
        def _():
            land[pl.ds(me, 1)] = part[pl.ds(mine, 1)]
            settle(land, n - 1, recv_sem.at[index])
            total = jnp.sum(land[...].astype(F32), axis=0, keepdims=True)
            full[pl.ds(mine, 1)] = total.astype(BF16)

            def step(i, carry):
                dev = lax.rem(me + i, n)
                remote(full.at[mine], full.at[mine], index + 1, dev).start()
                return carry

            lax.fori_loop(1, n, step, 0, unroll=31)

    def collect(part, land, full, index):
        @pl.when(leads)
        def _():
            settle(full, REDUCERS - 1, recv_sem.at[index + 1])
            settle(part, REDUCERS - 1, send_sem.at[index])
            settle(land, n - 1, send_sem.at[index + 1])

        @pl.when(jnp.logical_not(leads))
        def _():
            settle(full, REDUCERS, recv_sem.at[index + 1])
            settle(part, REDUCERS, send_sem.at[index])

        return unstacked(full[...].astype(F32).reshape(-1, head)).astype(BF16)

    def pair_start(part, twin, index):
        other = pl.ds((1 - core) * pairs, pairs)
        remote(part.at[other], twin, index, partner).start()

    def pair_scatter(part, twin, pre, land, index, pair_index):
        settle(twin, pairs, recv_sem.at[pair_index])
        own = part[pl.ds(core * pairs, pairs)].astype(F32)
        pre[...] = (own + twin[...].astype(F32)).astype(BF16)

        def step(i, carry):
            r = lax.rem(me // 2 + i, pairs)
            dev = leader(core, r)

            @pl.when(dev != me)
            def _():
                remote(pre.at[r], land.at[me // 2], index, dev).start()

            return carry

        lax.fori_loop(0, pairs, step, 0, unroll=4)

    def pair_gather(pre, land, full, index):
        @pl.when(leads)
        def _():
            land[pl.ds(me // 2, 1)] = pre[pl.ds(seated, 1)]
            settle(land, n // 2 - 1, recv_sem.at[index])
            total = jnp.sum(land[...].astype(F32), axis=0, keepdims=True)
            full[pl.ds(mine, 1)] = total.astype(BF16)

            def step(i, carry):
                dev = 2 * lax.rem(me // 2 + i, n // 2) + core
                remote(full.at[mine], full.at[mine], index + 1, dev).start()
                return carry

            lax.fori_loop(1, n // 2, step, 0, unroll=15)

    def pair_forward(pre, land, full, index, pair_index):
        @pl.when(leads)
        def _():
            settle(full, pairs - 1, recv_sem.at[index + 1])
            settle(pre, pairs - 1, send_sem.at[index])
            settle(land, n // 2 - 1, send_sem.at[index + 1])

        @pl.when(jnp.logical_not(leads))
        def _():
            settle(full, pairs, recv_sem.at[index + 1])
            settle(pre, pairs, send_sem.at[index])

        own = pl.ds(core * pairs, pairs)
        remote(full.at[own], full.at[own], pair_index + 2, partner).start()

    def pair_collect(twin, full, pair_index):
        settle(full, pairs, recv_sem.at[pair_index + 2])
        settle(twin, pairs, send_sem.at[pair_index])
        settle(full, pairs, send_sem.at[pair_index + 2])
        if full.shape[1] % 16 == 0:
            return unstacked(full[...].reshape(-1, head))
        return unstacked(full[...].astype(F32).reshape(-1, head)).astype(BF16)

    for copy in copies[:6]:
        copy.wait()
    first = me * rows
    start = pl.multiple_of(first // 128 * 128, 128)
    if (n * rows - rows) // 128 * 128 + window > width:
        limit = width - window
        start = pl.multiple_of(jnp.where(start > limit, limit, start), 128)
    shift = first - start
    place = lax.broadcasted_iota(jnp.int32, (window, rows), 0)
    source = lax.broadcasted_iota(jnp.int32, (window, rows), 1)
    chosen = jnp.where(place == source + shift, 1.0, 0.0).astype(BF16)
    spread_s = mm(chosen, in_s[...]).astype(BF16)
    spread_t = mm(chosen, in_t[...]).astype(BF16)
    span = basis[0 : 2 * head, pl.ds(start, window)].astype(F32)
    span_s = (span[:head] * gain_s[:, pl.ds(start, window)]).astype(BF16)
    span_t = (span * gain_t[:, pl.ds(start, window)]).astype(BF16)
    part_a[...] = stacked(mm(span_s, spread_s)).reshape(part_a.shape).astype(BF16)
    part_b[...] = stacked(mm(span_t, spread_t)).reshape(part_b.shape).astype(BF16)
    blank = jnp.zeros((3, frames + 2, columns, head), BF16)
    shifted[:, :, 0:columns] = blank
    shifted[:, :, columns + places :] = blank
    copies[6].wait()

    pl.semaphore_wait(barrier, greeted)
    halo = remote(video.at[pl.ds(frames - 2, 2)], prior, 0, me + 1)
    halo_in = remote(video.at[pl.ds(frames - 2, 2)], prior, 0, me)

    @pl.when(ts < n_ts - 1)
    def _():
        halo.start()

    pair_start(part_a, twin_a, 11)
    pair_start(part_b, twin_b, 12)
    chunk = width // 5
    gram[...] = jnp.zeros_like(gram)
    direct[...] = jnp.zeros_like(direct)

    def gram_slab(i, carry):
        pair = basis[0 : 2 * head, pl.ds(pl.multiple_of(i * chunk, 128), chunk)]
        gram[...] += mm_t(pair, pair)
        return carry

    lax.fori_loop(0, 3, gram_slab, 0)
    pair_scatter(part_a, twin_a, pre_a, land_a, 1, 11)
    pair_scatter(part_b, twin_b, pre_b, land_b, 3, 12)
    lax.fori_loop(3, 5, gram_slab, 0)
    embed_rows[...] = mm(span_s, chosen).astype(BF16)

    for copy in copies[7:10]:
        copy.wait()
    edges = edge[...].astype(F32)
    sums = [None] * frames

    def lay(block, first):
        count = block.shape[0]
        flat = block.astype(F32).reshape(count * places, head)
        near = edges[: count * places]
        sides = (moved(flat, 1) * near[:, 2:3], flat, moved(flat, -1) * near[:, 3:4])
        for side, values in enumerate(sides):
            shifted[side, first : first + count, columns : columns + places] = (
                values.reshape(count, places, head).astype(BF16)
            )

    def convolve(sources):
        for source in sources:
            outs = [o for o in range(frames) if 0 <= o + 2 - source <= 2]
            for row in range(3):
                window = slice(row * columns, row * columns + places)
                left = jnp.concatenate([shifted[i, source, window] for i in range(3)], axis=1)
                right = [taps[o + 2 - source, row].reshape(3 * head, head) for o in outs]
                product = mm(left, jnp.concatenate(right, axis=1))
                for i, o in enumerate(outs):
                    piece = product[:, i * head : (i + 1) * head]
                    sums[o] = piece if sums[o] is None else sums[o] + piece

    lay(video[...], 2)
    convolve(range(2, frames + 2))

    @pl.when(ts == 0)
    def _():
        prior[...] = jnp.zeros_like(prior)

    @pl.when(ts > 0)
    def _():
        halo_in.wait_recv()

    lay(prior[...], 0)
    convolve(range(2))
    summed = jnp.concatenate(sums, axis=0)
    features = jax.nn.gelu(summed, approximate=True).astype(BF16)

    grams = gram[...].astype(BF16)

    def factor_of(tokens_in):
        squares = jnp.sum(
            mm(tokens_in, grams[:head, :head]) * tokens_in.astype(F32),
            axis=-1, keepdims=True,
        )
        return lax.rsqrt(jnp.maximum(squares, 0.0) / width + epsilon)

    def swap(source_of, target, index):
        def step(i, carry):
            other = lax.rem(seat + i, team)
            remote(source_of(other), target.at[seat], index, base + other).start()
            return carry

        lax.fori_loop(1, team, step, 0, unroll=7)

    sent_f[...] = mm(perm[...], features).reshape(sent_f.shape).astype(BF16)
    swap(lambda other: sent_f.at[other], got_f, 10)
    got_f[pl.ds(seat, 1)] = sent_f[pl.ds(seat, 1)]
    scaled = (features.astype(F32) * factor_of(features)).astype(BF16)
    clip[pl.ds(seat, 1)] = scaled.astype(F32).reshape(1, tokens, head).astype(BF16)
    mates = team // 2 - 1

    def mate(i):
        return lax.rem(seat + 2 * i, team)

    for i in range(1, mates + 1):
        remote(clip.at[seat], clip.at[seat], 16 + i, base + mate(i)).start()
    remote(clip.at[seat], clip.at[seat], 15, partner).start()

    pair_gather(pre_a, land_a, full_a, 1)

    for copy in copies[10:]:
        copy.wait()

    def direct_slab(i, carry):
        cols = pl.ds(pl.multiple_of(i * chunk, 128), chunk)
        direct[...] += mm_t(cot[:, cols], basis[head : 3 * head, cols])
        return carry

    lax.fori_loop(0, 5, direct_slab, 0)
    pair_gather(pre_b, land_b, full_b, 3)
    dealt = mm(perm[...], direct[...].astype(BF16))
    sent[...] = dealt.reshape(sent.shape).astype(BF16)
    swap(lambda other: sent.at[other], got, 6)
    got[pl.ds(seat, 1)] = sent[pl.ds(seat, 1)]


    def own_rows(ref):
        return ref[...].astype(F32).reshape(team * pad, -1)

    settle(got_f, team - 1, recv_sem.at[10])
    own = own_rows(got_f).astype(BF16)
    factor_one = factor_of(own)
    own_scaled = (own.astype(F32) * factor_one).astype(BF16)
    for i in range(1, mates + 1):
        settle(clip, 1, recv_sem.at[16 + i])
        came = mate(team // 2 - i)
        remote(clip.at[came], clip.at[came], 16, partner).start()
    pair_forward(pre_a, land_a, full_a, 1, 11)
    settle(clip, 1, recv_sem.at[15])
    settle(clip, mates, recv_sem.at[16])
    scale = head ** -0.5

    def by_slot(form, values):
        return [
            form(values[i * pad : (i + 1) * pad].astype(BF16), clip[i]) for i in range(team)
        ]

    map_space = pair_collect(twin_a, full_a, 11)
    map_q, map_k, map_v = (map_space[:, i * head : (i + 1) * head] for i in range(3))
    pair_forward(pre_b, land_b, full_b, 3, 12)
    q = mm(own_scaled, map_q).astype(BF16)
    apart = frame_bias[...].astype(F32)
    scores = [score + apart for score in by_slot(mm_t, mm_t(q, map_k) * scale)]
    attend_one = softmax(jnp.concatenate(scores, axis=0))
    looked = jnp.concatenate(by_slot(mm, attend_one), axis=0).astype(BF16)
    mixture_one = mm(looked, map_v).astype(BF16)
    joint = jnp.concatenate([own, mixture_one], axis=-1)
    spread = mm(joint, grams)
    squares = jnp.sum(spread * joint.astype(F32), axis=-1, keepdims=True)
    factor_two = lax.rsqrt(jnp.maximum(squares, 0.0) / width + epsilon)
    settle(got, team - 1, recv_sem.at[6])
    arrived = own_rows(got)
    direct_s, g_time = arrived[:, :head], arrived[:, head:].astype(BF16)
    map_time = pair_collect(twin_b, full_b, 12)
    packed_two = (mm(joint, map_time) * factor_two).astype(BF16)
    tq, tk, tv = (packed_two[:, i * head : (i + 1) * head] for i in range(3))
    attend_two = softmax(mm_t(tq, tk) * scale + clip_bias[...].astype(F32))
    attend_bf = attend_two.astype(BF16)
    mixture_two = mm(attend_bf, tv).astype(BF16)
    back[...] = (
        jnp.concatenate([mixture_one, mixture_two], axis=-1)
        .astype(F32).reshape(back.shape).astype(BF16)
    )
    home[pl.ds(seat, 1)] = back[pl.ds(seat, 1)]

    grad_scores = softmax_grad(attend_two, mm_t(g_time, tv)).astype(BF16)
    grad_two = jnp.concatenate(
        [mm(grad_scores, tk) * scale, t_mm(grad_scores, tq) * scale, t_mm(attend_bf, g_time)],
        axis=-1,
    ).astype(BF16)
    inner = jnp.sum(grad_two.astype(F32) * packed_two.astype(F32), axis=-1, keepdims=True)
    g_space = (
        direct_s
        + factor_two * mm_t(grad_two, map_time[head:])
        - (factor_two * factor_two * inner / width) * spread[:, head:]
    ).astype(BF16)
    grad_attend = jnp.concatenate(by_slot(mm_t, mm_t(g_space, map_v)), axis=0)
    looked_back = by_slot(mm, softmax_grad(attend_one, grad_attend))
    looked_back = jnp.concatenate(looked_back, axis=0).astype(BF16)
    cross = (t_mm(own_scaled, looked_back) * scale).astype(BF16)
    part = jnp.concatenate([mm(cross, map_k), t_mm(cross, map_q), t_mm(looked, g_space)], axis=1)
    part_c[...] = stacked(part).reshape(part_c.shape).astype(BF16)
    scatter(part_c, land_c, 7)
    swap(lambda other: back.at[other], home, 9)
    gather(part_c, land_c, full_c, 7)

    settle(home, team - 1, recv_sem.at[9])
    returned = home[...].astype(F32).reshape(team * pad, 2 * head).astype(BF16)
    triple = jnp.concatenate([features, t_mm(perm[...], returned).astype(BF16)], axis=-1)

    def write(i, carry):
        cols = pl.ds(pl.multiple_of(i * chunk, 128), chunk)
        result[:, cols] = mm(triple, basis[:, cols]).astype(BF16)
        return carry

    lax.fori_loop(0, 5, write, 0)
    total[...] = collect(part_c, land_c, full_c, 7)

    @pl.when(ts < n_ts - 1)
    def _():
        halo.wait_send()

    for i in range(1, mates + 1):
        settle(clip, 1, send_sem.at[16 + i])
    settle(sent, team - 1, send_sem.at[6])
    settle(sent_f, team - 1, send_sem.at[10])
    settle(clip, 1, send_sem.at[15])
    settle(clip, mates, send_sem.at[16])
    settle(back, team - 1, send_sem.at[9])


def store_kernel(result, total, embed_rows, output, grad, grad_block, sems):
    large = pltpu.make_async_copy(result, output, sems.at[0])
    large.start()
    grad_block[...] = t_mm(embed_rows[...], total[...])
    small = pltpu.make_async_copy(grad_block, grad, sems.at[1])
    small.start()
    large.wait()
    small.wait()


def shards(
    clip_video, conv_weight, embed_weight, gain_spatial, gain_temporal, input_spatial,
    input_temporal, output_spatial, output_temporal, cotangent,
):
    frames, height, columns, channels = clip_video.shape
    rows, triple = input_spatial.shape
    head = triple // 3
    width = embed_weight.shape[-1]
    places = height * columns
    tokens = frames * places
    n_dp, n_ts = lax.axis_size("dp"), lax.axis_size("ts")
    n = n_dp * n_ts
    team = FR // frames
    share = places // team
    pad = -(-frames * share // 8) * 8
    reach = max(i * rows % 128 + rows for i in range(n))
    window = -(-reach // 128) * 128

    token = np.arange(tokens)
    frame, spot = token // places, token % places
    slot = spot // share * pad + frame * share + spot % share
    held = team * pad
    perm = np.zeros((held, tokens), np.float32)
    perm[slot, token] = 1.0
    frame_bias = np.where(np.arange(pad)[:, None] // share == frame[None, :], 0.0, masked)
    seat = np.arange(held)
    local = seat % pad
    when = seat // pad * frames + local // share
    allowed = (
        (local[:, None] % share == local[None, :] % share)
        & (when[:, None] >= when[None, :])
        & (local[:, None] < frames * share)
        & (local[None, :] < frames * share)
    )
    clip_bias = np.where(allowed, 0.0, masked)
    edge = np.zeros((tokens, 128), np.float32)
    edge[:, 0] = spot // columns >= 1
    edge[:, 1] = spot // columns < height - 1
    edge[:, 2] = spot % columns >= 1
    edge[:, 3] = spot % columns < columns - 1

    dims = (n_dp, n_ts, frames, places, columns, team, pad, rows, window)
    any_space = pl.BlockSpec(memory_space=pltpu.HBM)
    vmem = pl.BlockSpec(memory_space=pltpu.VMEM)
    buffer = lambda *shape: pltpu.VMEM(shape, BF16)
    wide = lambda *shape: pltpu.VMEM(shape, F32)
    result, total, embed_rows = pl.pallas_call(
        functools.partial(whole_kernel, dims),
        out_shape=(
            jax.ShapeDtypeStruct((tokens, width), BF16),
            jax.ShapeDtypeStruct((head, triple), BF16),
            jax.ShapeDtypeStruct((head, rows), BF16),
        ),
        in_specs=[any_space] * 14,
        out_specs=(vmem, vmem, vmem),
        scratch_shapes=[
            buffer(frames, places, channels), buffer(2, places, channels),
            buffer(3, frames + 2, places + 2 * columns, channels),
            buffer(*conv_weight.shape), buffer(3 * head, width), wide(1, width), wide(1, width),
            buffer(rows, triple), buffer(rows, triple), buffer(tokens, width),
            buffer(held, tokens), buffer(pad, tokens), buffer(held, held),
            buffer(tokens, 128),
            buffer(REDUCERS // 2, 24, 128), buffer(REDUCERS // 2, 48, 128),
            buffer(REDUCERS // 2, 24, 128), buffer(REDUCERS // 2, 48, 128),
            buffer(REDUCERS, 24, 128), buffer(REDUCERS, 48, 128), buffer(REDUCERS, 24, 128),
            buffer(n // 2, 24, 128), buffer(n // 2, 48, 128), buffer(n, 24, 128),
            buffer(REDUCERS, 24, 128), buffer(REDUCERS, 48, 128), buffer(REDUCERS, 24, 128),
            buffer(team, tokens, head),
            buffer(team, pad, 2 * head), buffer(team, pad, 2 * head),
            buffer(team, pad, head), buffer(team, pad, head),
            buffer(team, pad, 2 * head), buffer(team, pad, 2 * head),
            wide(2 * head, 2 * head), wide(tokens, 2 * head),
            pltpu.SemaphoreType.DMA((14,)), pltpu.SemaphoreType.DMA((20,)),
            pltpu.SemaphoreType.DMA((20,)),
        ],
        compiler_params=pltpu.CompilerParams(
            collective_id=0, has_side_effects=True, vmem_limit_bytes=36 * 1024 * 1024
        ),
    )(*(pltpu.with_memory_space_constraint(x, pltpu.HBM) for x in (
        clip_video.reshape(frames, places, channels),
        conv_weight,
        embed_weight,
        gain_spatial.reshape(1, width),
        gain_temporal.reshape(1, width),
        input_spatial,
        input_temporal,
        output_spatial,
        output_temporal,
        cotangent.reshape(tokens, width),
        jnp.asarray(perm, BF16),
        jnp.asarray(frame_bias, BF16),
        jnp.asarray(clip_bias, BF16),
        jnp.asarray(edge, BF16),
    )))
    output, grad = pl.pallas_call(
        store_kernel,
        out_shape=(
            jax.ShapeDtypeStruct((tokens, width), BF16),
            jax.ShapeDtypeStruct((rows, triple), F32),
        ),
        in_specs=[pl.BlockSpec(memory_space=pl.ANY), vmem, vmem],
        out_specs=(any_space, any_space),
        scratch_shapes=[wide(rows, triple), pltpu.SemaphoreType.DMA((2,))],
        compiler_params=pltpu.CompilerParams(vmem_limit_bytes=4 * 1024 * 1024),
    )(result, total, embed_rows)
    return output.reshape(frames, height, columns, width), grad


def solution(mesh):
    placed = (
        P(("dp", "ts"), None, None, None), P(), P(), P(), P(), P(("dp", "ts"), None),
        P(("dp", "ts"), None), P(), P(), P(("dp", "ts"), None, None, None),
    )
    return jax.shard_map(
        shards,
        mesh=mesh,
        in_specs=placed,
        out_specs=(P(("dp", "ts"), None, None, None), P(("dp", "ts"), None)),
        check_vma=False,
    )
```

```python
import functools

import jax
import jax.numpy as jnp
import numpy as np
from jax import lax
from jax.experimental import pallas as pl
from jax.experimental.pallas import tpu as pltpu
from jax.sharding import PartitionSpec as P

FR = 16
REDUCERS = 16
epsilon = 1e-06
masked = -1e30
F32 = jnp.float32
BF16 = jnp.bfloat16
MESH = pl.DeviceIdType.MESH


def mm(a, b, dims=((1,), (0,))):
    return lax.dot_general(a, b, (dims, ((), ())), preferred_element_type=F32)


def mm_t(a, b):
    return mm(a, b, ((1,), (1,)))


def t_mm(a, b):
    return mm(a, b, ((0,), (0,)))


def softmax(scores):
    raised = jnp.exp(scores - jnp.max(scores, axis=-1, keepdims=True))
    return raised * (1.0 / jnp.sum(raised, axis=-1, keepdims=True))


def softmax_grad(attend, grad_attend):
    inner = jnp.sum(grad_attend * attend, axis=-1, keepdims=True)
    return attend * (grad_attend - inner)


def stacked(block):
    third = block.shape[1] // 3
    return jnp.concatenate([block[:, i * third : (i + 1) * third] for i in range(3)], axis=0)


def unstacked(block):
    third = block.shape[0] // 3
    return jnp.concatenate([block[i * third : (i + 1) * third] for i in range(3)], axis=1)


def moved(block, distance):
    if distance == 0:
        return block
    return pltpu.roll(block, distance % block.shape[0], 0)


def whole_kernel(
    dims,
    video_hbm, conv_hbm, embed_hbm, gain_s_hbm, gain_t_hbm, in_s_hbm, in_t_hbm, out_s_hbm,
    out_t_hbm, cot_hbm, perm_hbm, frame_bias_hbm, clip_bias_hbm, edge_hbm,
    result, total, embed_rows,
    video, prior, shifted, taps, basis, gain_s, gain_t, in_s, in_t, cot, perm, frame_bias, clip_bias, edge,
    twin_a, twin_b, pre_a, pre_b, part_a, part_b, part_c, land_a, land_b, land_c, full_a, full_b, full_c,
    clip, sent, got, sent_f, got_f, back, home, gram, direct,
    local_sem, send_sem, recv_sem,
):
    n_dp, n_ts, frames, places, columns, team, pad, rows, window = dims
    n = n_dp * n_ts
    head = 128
    width = basis.shape[1]
    tokens = frames * places
    dp, ts = lax.axis_index("dp"), lax.axis_index("ts")
    me = dp * n_ts + ts

    loads = [
        (in_s_hbm, in_s), (in_t_hbm, in_t), (gain_s_hbm, gain_s), (gain_t_hbm, gain_t),
        (embed_hbm, basis.at[0:head]), (out_s_hbm, basis.at[head : 2 * head]),
        (video_hbm, video), (edge_hbm, edge), (conv_hbm, taps), (perm_hbm, perm),
        (out_t_hbm, basis.at[2 * head : 3 * head]), (cot_hbm, cot),
        (frame_bias_hbm, frame_bias), (clip_bias_hbm, clip_bias),
    ]
    copies = [pltpu.make_async_copy(s, d, local_sem.at[i]) for i, (s, d) in enumerate(loads)]
    for copy in copies[:7]:
        copy.start()

    half, quarter = n_ts // 2, n_ts // 4
    barrier = pltpu.get_barrier_semaphore()

    def leading(dev):
        group, spot = dev // n_ts, lax.rem(dev, n_ts)
        place = group * (half // 2) + (spot - quarter) // 2
        inside = jnp.logical_and(spot >= quarter, spot < quarter + half)
        return jnp.logical_and(inside, place < REDUCERS // 2)

    leads = leading(me)

    pairs = REDUCERS // 2
    core = lax.rem(ts, 2)
    seat = lax.rem(ts, team)
    base = me - seat

    def leader(side, i):
        return i // (half // 2) * n_ts + quarter + 2 * lax.rem(i, half // 2) + side

    def greet(dev):
        pl.semaphore_signal(
            barrier, inc=1, device_id=(dev // n_ts, lax.rem(dev, n_ts)), device_id_type=MESH
        )

    def greet_same(i, carry):
        dev = lax.rem(i, n_dp) * n_ts + i // n_dp * 2 + core

        @pl.when(dev != me)
        def _():
            greet(dev)

        return carry

    @pl.when(leads)
    def _():
        lax.fori_loop(0, n // 2, greet_same, 0)

    def greet_mate(i, count):
        dev = base + lax.rem(seat + i, team)
        same = lax.rem(i, 2) == 0

        @pl.when(jnp.logical_not(jnp.logical_and(leads, same)))
        def _():
            greet(dev)

        return count + jnp.where(jnp.logical_and(leading(dev), same), 0, 1)

    @pl.when(jnp.logical_and(seat == 0, ts > 0))
    def _():
        greet(me - 1)

    for copy in copies[7:]:
        copy.start()
    after = jnp.logical_and(seat == team - 1, ts < n_ts - 1)
    greeted = lax.fori_loop(1, team, greet_mate, pairs + jnp.where(after, 1, 0))
    greeted = greeted - jnp.where(leads, 1, 0)

    def remote(src, dst, index, dev):
        return pltpu.make_async_remote_copy(
            src_ref=src, dst_ref=dst, send_sem=send_sem.at[index], recv_sem=recv_sem.at[index],
            device_id=(dev // n_ts, lax.rem(dev, n_ts)), device_id_type=MESH,
        )

    def settle(ref, count, sem):
        piece = ref.at[pl.ds(0, count)]
        pltpu.make_async_copy(piece, piece, sem).wait()

    partner = me + 1 - 2 * core
    seated = dp * (half // 2) + (ts - quarter) // 2
    mine = core * pairs + seated

    def scatter(part, land, index):
        def step(i, carry):
            r = lax.rem(me + i, REDUCERS)
            dev = leader(r // pairs, lax.rem(r, pairs))

            @pl.when(dev != me)
            def _():
                remote(part.at[r], land.at[me], index, dev).start()

            return carry

        lax.fori_loop(0, REDUCERS, step, 0, unroll=4)

    def gather(part, land, full, index):
        @pl.when(leads)
        def _():
            land[pl.ds(me, 1)] = part[pl.ds(mine, 1)]
            settle(land, n - 1, recv_sem.at[index])
            total = jnp.sum(land[...].astype(F32), axis=0, keepdims=True)
            full[pl.ds(mine, 1)] = total.astype(BF16)

            def step(i, carry):
                dev = lax.rem(me + i, n)
                remote(full.at[mine], full.at[mine], index + 1, dev).start()
                return carry

            lax.fori_loop(1, n, step, 0, unroll=31)

    def collect(part, land, full, index):
        @pl.when(leads)
        def _():
            settle(full, REDUCERS - 1, recv_sem.at[index + 1])
            settle(part, REDUCERS - 1, send_sem.at[index])
            settle(land, n - 1, send_sem.at[index + 1])

        @pl.when(jnp.logical_not(leads))
        def _():
            settle(full, REDUCERS, recv_sem.at[index + 1])
            settle(part, REDUCERS, send_sem.at[index])

        return unstacked(full[...].astype(F32).reshape(-1, head)).astype(BF16)

    def pair_start(part, twin, index):
        other = pl.ds((1 - core) * pairs, pairs)
        remote(part.at[other], twin, index, partner).start()

    def pair_scatter(part, twin, pre, land, index, pair_index):
        settle(twin, pairs, recv_sem.at[pair_index])
        own = part[pl.ds(core * pairs, pairs)].astype(F32)
        pre[...] = (own + twin[...].astype(F32)).astype(BF16)

        def step(i, carry):
            r = lax.rem(me // 2 + i, pairs)
            dev = leader(core, r)

            @pl.when(dev != me)
            def _():
                remote(pre.at[r], land.at[me // 2], index, dev).start()

            return carry

        lax.fori_loop(0, pairs, step, 0, unroll=4)

    def pair_gather(pre, land, full, index):
        @pl.when(leads)
        def _():
            land[pl.ds(me // 2, 1)] = pre[pl.ds(seated, 1)]
            settle(land, n // 2 - 1, recv_sem.at[index])
            total = jnp.sum(land[...].astype(F32), axis=0, keepdims=True)
            full[pl.ds(mine, 1)] = total.astype(BF16)

            def step(i, carry):
                dev = 2 * lax.rem(me // 2 + i, n // 2) + core
                remote(full.at[mine], full.at[mine], index + 1, dev).start()
                return carry

            lax.fori_loop(1, n // 2, step, 0, unroll=15)

    def pair_forward(pre, land, full, index, pair_index):
        @pl.when(leads)
        def _():
            settle(full, pairs - 1, recv_sem.at[index + 1])
            settle(pre, pairs - 1, send_sem.at[index])
            settle(land, n // 2 - 1, send_sem.at[index + 1])

        @pl.when(jnp.logical_not(leads))
        def _():
            settle(full, pairs, recv_sem.at[index + 1])
            settle(pre, pairs, send_sem.at[index])

        own = pl.ds(core * pairs, pairs)
        remote(full.at[own], full.at[own], pair_index + 2, partner).start()

    def pair_collect(twin, full, pair_index):
        settle(full, pairs, recv_sem.at[pair_index + 2])
        settle(twin, pairs, send_sem.at[pair_index])
        settle(full, pairs, send_sem.at[pair_index + 2])
        if full.shape[1] % 16 == 0:
            return unstacked(full[...].reshape(-1, head))
        return unstacked(full[...].astype(F32).reshape(-1, head)).astype(BF16)

    for copy in copies[:6]:
        copy.wait()
    first = me * rows
    start = pl.multiple_of(first // 128 * 128, 128)
    if (n * rows - rows) // 128 * 128 + window > width:
        limit = width - window
        start = pl.multiple_of(jnp.where(start > limit, limit, start), 128)
    shift = first - start
    place = lax.broadcasted_iota(jnp.int32, (window, rows), 0)
    source = lax.broadcasted_iota(jnp.int32, (window, rows), 1)
    chosen = jnp.where(place == source + shift, 1.0, 0.0).astype(BF16)
    spread_s = mm(chosen, in_s[...]).astype(BF16)
    spread_t = mm(chosen, in_t[...]).astype(BF16)
    span = basis[0 : 2 * head, pl.ds(start, window)].astype(F32)
    span_s = (span[:head] * gain_s[:, pl.ds(start, window)]).astype(BF16)
    span_t = (span * gain_t[:, pl.ds(start, window)]).astype(BF16)
    part_a[...] = stacked(mm(span_s, spread_s)).reshape(part_a.shape).astype(BF16)
    part_b[...] = stacked(mm(span_t, spread_t)).reshape(part_b.shape).astype(BF16)
    blank = jnp.zeros((3, frames + 2, columns, head), BF16)
    shifted[:, :, 0:columns] = blank
    shifted[:, :, columns + places :] = blank
    copies[6].wait()

    pl.semaphore_wait(barrier, greeted)
    halo = remote(video.at[pl.ds(frames - 2, 2)], prior, 0, me + 1)
    halo_in = remote(video.at[pl.ds(frames - 2, 2)], prior, 0, me)

    @pl.when(ts < n_ts - 1)
    def _():
        halo.start()

    pair_start(part_a, twin_a, 11)
    pair_start(part_b, twin_b, 12)
    chunk = width // 5
    gram[...] = jnp.zeros_like(gram)
    direct[...] = jnp.zeros_like(direct)

    def gram_slab(i, carry):
        pair = basis[0 : 2 * head, pl.ds(pl.multiple_of(i * chunk, 128), chunk)]
        gram[...] += mm_t(pair, pair)
        return carry

    lax.fori_loop(0, 3, gram_slab, 0)
    pair_scatter(part_a, twin_a, pre_a, land_a, 1, 11)
    pair_scatter(part_b, twin_b, pre_b, land_b, 3, 12)
    lax.fori_loop(3, 5, gram_slab, 0)
    embed_rows[...] = mm(span_s, chosen).astype(BF16)

    for copy in copies[7:10]:
        copy.wait()
    edges = edge[...].astype(F32)
    sums = [None] * frames

    def lay(block, first):
        count = block.shape[0]
        flat = block.astype(F32).reshape(count * places, head)
        near = edges[: count * places]
        sides = (moved(flat, 1) * near[:, 2:3], flat, moved(flat, -1) * near[:, 3:4])
        for side, values in enumerate(sides):
            shifted[side, first : first + count, columns : columns + places] = (
                values.reshape(count, places, head).astype(BF16)
            )

    def convolve(sources):
        for source in sources:
            outs = [o for o in range(frames) if 0 <= o + 2 - source <= 2]
            for row in range(3):
                window = slice(row * columns, row * columns + places)
                left = jnp.concatenate([shifted[i, source, window] for i in range(3)], axis=1)
                right = [taps[o + 2 - source, row].reshape(3 * head, head) for o in outs]
                product = mm(left, jnp.concatenate(right, axis=1))
                for i, o in enumerate(outs):
                    piece = product[:, i * head : (i + 1) * head]
                    sums[o] = piece if sums[o] is None else sums[o] + piece

    lay(video[...], 2)
    convolve(range(2, frames + 2))

    @pl.when(ts == 0)
    def _():
        prior[...] = jnp.zeros_like(prior)

    @pl.when(ts > 0)
    def _():
        halo_in.wait_recv()

    lay(prior[...], 0)
    convolve(range(2))
    summed = jnp.concatenate(sums, axis=0)
    features = jax.nn.gelu(summed, approximate=True).astype(BF16)

    grams = gram[...].astype(BF16)

    def factor_of(tokens_in):
        squares = jnp.sum(
            mm(tokens_in, grams[:head, :head]) * tokens_in.astype(F32),
            axis=-1, keepdims=True,
        )
        return lax.rsqrt(jnp.maximum(squares, 0.0) / width + epsilon)

    def swap(source_of, target, index):
        def step(i, carry):
            other = lax.rem(seat + i, team)
            remote(source_of(other), target.at[seat], index, base + other).start()
            return carry

        lax.fori_loop(1, team, step, 0, unroll=7)

    sent_f[...] = mm(perm[...], features).reshape(sent_f.shape).astype(BF16)
    swap(lambda other: sent_f.at[other], got_f, 10)
    got_f[pl.ds(seat, 1)] = sent_f[pl.ds(seat, 1)]
    scaled = (features.astype(F32) * factor_of(features)).astype(BF16)
    clip[pl.ds(seat, 1)] = scaled.astype(F32).reshape(1, tokens, head).astype(BF16)
    mates = team // 2 - 1

    def mate(i):
        return lax.rem(seat + 2 * i, team)

    remote(clip.at[seat], clip.at[seat], 15, partner).start()
    for i in range(mates, 0, -1):
        remote(clip.at[seat], clip.at[seat], 16 + i, base + mate(i)).start()

    pair_gather(pre_a, land_a, full_a, 1)

    for copy in copies[10:]:
        copy.wait()

    def direct_slab(i, carry):
        cols = pl.ds(pl.multiple_of(i * chunk, 128), chunk)
        direct[...] += mm_t(cot[:, cols], basis[head : 3 * head, cols])
        return carry

    lax.fori_loop(0, 5, direct_slab, 0)
    pair_gather(pre_b, land_b, full_b, 3)
    dealt = mm(perm[...], direct[...].astype(BF16))
    sent[...] = dealt.reshape(sent.shape).astype(BF16)
    swap(lambda other: sent.at[other], got, 6)
    got[pl.ds(seat, 1)] = sent[pl.ds(seat, 1)]


    def own_rows(ref):
        return ref[...].astype(F32).reshape(team * pad, -1)

    settle(got_f, team - 1, recv_sem.at[10])
    own = own_rows(got_f).astype(BF16)
    factor_one = factor_of(own)
    own_scaled = (own.astype(F32) * factor_one).astype(BF16)
    for i in range(1, mates + 1):
        settle(clip, 1, recv_sem.at[16 + i])
        came = mate(team // 2 - i)
        remote(clip.at[came], clip.at[came], 16, partner).start()
    pair_forward(pre_a, land_a, full_a, 1, 11)
    settle(clip, 1, recv_sem.at[15])
    settle(clip, mates, recv_sem.at[16])
    scale = head ** -0.5

    def by_slot(form, values):
        return [
            form(values[i * pad : (i + 1) * pad].astype(BF16), clip[i]) for i in range(team)
        ]

    map_space = pair_collect(twin_a, full_a, 11)
    map_q, map_k, map_v = (map_space[:, i * head : (i + 1) * head] for i in range(3))
    pair_forward(pre_b, land_b, full_b, 3, 12)
    q = mm(own_scaled, map_q).astype(BF16)
    apart = frame_bias[...].astype(F32)
    scores = [score + apart for score in by_slot(mm_t, mm_t(q, map_k) * scale)]
    attend_one = softmax(jnp.concatenate(scores, axis=0))
    looked = jnp.concatenate(by_slot(mm, attend_one), axis=0).astype(BF16)
    mixture_one = mm(looked, map_v).astype(BF16)
    joint = jnp.concatenate([own, mixture_one], axis=-1)
    spread = mm(joint, grams)
    squares = jnp.sum(spread * joint.astype(F32), axis=-1, keepdims=True)
    factor_two = lax.rsqrt(jnp.maximum(squares, 0.0) / width + epsilon)
    settle(got, team - 1, recv_sem.at[6])
    arrived = own_rows(got)
    direct_s, g_time = arrived[:, :head], arrived[:, head:].astype(BF16)
    map_time = pair_collect(twin_b, full_b, 12)
    packed_two = (mm(joint, map_time) * factor_two).astype(BF16)
    tq, tk, tv = (packed_two[:, i * head : (i + 1) * head] for i in range(3))
    attend_two = softmax(mm_t(tq, tk) * scale + clip_bias[...].astype(F32))
    attend_bf = attend_two.astype(BF16)
    mixture_two = mm(attend_bf, tv).astype(BF16)
    back[...] = (
        jnp.concatenate([mixture_one, mixture_two], axis=-1)
        .astype(F32).reshape(back.shape).astype(BF16)
    )
    home[pl.ds(seat, 1)] = back[pl.ds(seat, 1)]

    grad_scores = softmax_grad(attend_two, mm_t(g_time, tv)).astype(BF16)
    grad_two = jnp.concatenate(
        [mm(grad_scores, tk) * scale, t_mm(grad_scores, tq) * scale, t_mm(attend_bf, g_time)],
        axis=-1,
    ).astype(BF16)
    inner = jnp.sum(grad_two.astype(F32) * packed_two.astype(F32), axis=-1, keepdims=True)
    g_space = (
        direct_s
        + factor_two * mm_t(grad_two, map_time[head:])
        - (factor_two * factor_two * inner / width) * spread[:, head:]
    ).astype(BF16)
    grad_attend = jnp.concatenate(by_slot(mm_t, mm_t(g_space, map_v)), axis=0)
    looked_back = by_slot(mm, softmax_grad(attend_one, grad_attend))
    looked_back = jnp.concatenate(looked_back, axis=0).astype(BF16)
    cross = (t_mm(own_scaled, looked_back) * scale).astype(BF16)
    part = jnp.concatenate([mm(cross, map_k), t_mm(cross, map_q), t_mm(looked, g_space)], axis=1)
    part_c[...] = stacked(part).reshape(part_c.shape).astype(BF16)
    scatter(part_c, land_c, 7)
    swap(lambda other: back.at[other], home, 9)
    gather(part_c, land_c, full_c, 7)

    settle(home, team - 1, recv_sem.at[9])
    returned = home[...].astype(F32).reshape(team * pad, 2 * head).astype(BF16)
    triple = jnp.concatenate([features, t_mm(perm[...], returned).astype(BF16)], axis=-1)

    def write(i, carry):
        cols = pl.ds(pl.multiple_of(i * chunk, 128), chunk)
        result[:, cols] = mm(triple, basis[:, cols]).astype(BF16)
        return carry

    lax.fori_loop(0, 5, write, 0)
    total[...] = collect(part_c, land_c, full_c, 7)

    @pl.when(ts < n_ts - 1)
    def _():
        halo.wait_send()

    for i in range(1, mates + 1):
        settle(clip, 1, send_sem.at[16 + i])
    settle(sent, team - 1, send_sem.at[6])
    settle(sent_f, team - 1, send_sem.at[10])
    settle(clip, 1, send_sem.at[15])
    settle(clip, mates, send_sem.at[16])
    settle(back, team - 1, send_sem.at[9])


def store_kernel(result, total, embed_rows, output, grad, grad_block, sems):
    large = pltpu.make_async_copy(result, output, sems.at[0])
    large.start()
    grad_block[...] = t_mm(embed_rows[...], total[...])
    small = pltpu.make_async_copy(grad_block, grad, sems.at[1])
    small.start()
    large.wait()
    small.wait()


def shards(
    clip_video, conv_weight, embed_weight, gain_spatial, gain_temporal, input_spatial,
    input_temporal, output_spatial, output_temporal, cotangent,
):
    frames, height, columns, channels = clip_video.shape
    rows, triple = input_spatial.shape
    head = triple // 3
    width = embed_weight.shape[-1]
    places = height * columns
    tokens = frames * places
    n_dp, n_ts = lax.axis_size("dp"), lax.axis_size("ts")
    n = n_dp * n_ts
    team = FR // frames
    share = places // team
    pad = -(-frames * share // 8) * 8
    reach = max(i * rows % 128 + rows for i in range(n))
    window = -(-reach // 128) * 128

    token = np.arange(tokens)
    frame, spot = token // places, token % places
    slot = spot // share * pad + frame * share + spot % share
    held = team * pad
    perm = np.zeros((held, tokens), np.float32)
    perm[slot, token] = 1.0
    frame_bias = np.where(np.arange(pad)[:, None] // share == frame[None, :], 0.0, masked)
    seat = np.arange(held)
    local = seat % pad
    when = seat // pad * frames + local // share
    allowed = (
        (local[:, None] % share == local[None, :] % share)
        & (when[:, None] >= when[None, :])
        & (local[:, None] < frames * share)
        & (local[None, :] < frames * share)
    )
    clip_bias = np.where(allowed, 0.0, masked)
    edge = np.zeros((tokens, 128), np.float32)
    edge[:, 0] = spot // columns >= 1
    edge[:, 1] = spot // columns < height - 1
    edge[:, 2] = spot % columns >= 1
    edge[:, 3] = spot % columns < columns - 1

    dims = (n_dp, n_ts, frames, places, columns, team, pad, rows, window)
    any_space = pl.BlockSpec(memory_space=pltpu.HBM)
    vmem = pl.BlockSpec(memory_space=pltpu.VMEM)
    buffer = lambda *shape: pltpu.VMEM(shape, BF16)
    wide = lambda *shape: pltpu.VMEM(shape, F32)
    result, total, embed_rows = pl.pallas_call(
        functools.partial(whole_kernel, dims),
        out_shape=(
            jax.ShapeDtypeStruct((tokens, width), BF16),
            jax.ShapeDtypeStruct((head, triple), BF16),
            jax.ShapeDtypeStruct((head, rows), BF16),
        ),
        in_specs=[any_space] * 14,
        out_specs=(vmem, vmem, vmem),
        scratch_shapes=[
            buffer(frames, places, channels), buffer(2, places, channels),
            buffer(3, frames + 2, places + 2 * columns, channels),
            buffer(*conv_weight.shape), buffer(3 * head, width), wide(1, width), wide(1, width),
            buffer(rows, triple), buffer(rows, triple), buffer(tokens, width),
            buffer(held, tokens), buffer(pad, tokens), buffer(held, held),
            buffer(tokens, 128),
            buffer(REDUCERS // 2, 24, 128), buffer(REDUCERS // 2, 48, 128),
            buffer(REDUCERS // 2, 24, 128), buffer(REDUCERS // 2, 48, 128),
            buffer(REDUCERS, 24, 128), buffer(REDUCERS, 48, 128), buffer(REDUCERS, 24, 128),
            buffer(n // 2, 24, 128), buffer(n // 2, 48, 128), buffer(n, 24, 128),
            buffer(REDUCERS, 24, 128), buffer(REDUCERS, 48, 128), buffer(REDUCERS, 24, 128),
            buffer(team, tokens, head),
            buffer(team, pad, 2 * head), buffer(team, pad, 2 * head),
            buffer(team, pad, head), buffer(team, pad, head),
            buffer(team, pad, 2 * head), buffer(team, pad, 2 * head),
            wide(2 * head, 2 * head), wide(tokens, 2 * head),
            pltpu.SemaphoreType.DMA((14,)), pltpu.SemaphoreType.DMA((20,)),
            pltpu.SemaphoreType.DMA((20,)),
        ],
        compiler_params=pltpu.CompilerParams(
            collective_id=0, has_side_effects=True, vmem_limit_bytes=36 * 1024 * 1024
        ),
    )(*(pltpu.with_memory_space_constraint(x, pltpu.HBM) for x in (
        clip_video.reshape(frames, places, channels),
        conv_weight,
        embed_weight,
        gain_spatial.reshape(1, width),
        gain_temporal.reshape(1, width),
        input_spatial,
        input_temporal,
        output_spatial,
        output_temporal,
        cotangent.reshape(tokens, width),
        jnp.asarray(perm, BF16),
        jnp.asarray(frame_bias, BF16),
        jnp.asarray(clip_bias, BF16),
        jnp.asarray(edge, BF16),
    )))
    output, grad = pl.pallas_call(
        store_kernel,
        out_shape=(
            jax.ShapeDtypeStruct((tokens, width), BF16),
            jax.ShapeDtypeStruct((rows, triple), F32),
        ),
        in_specs=[pl.BlockSpec(memory_space=pl.ANY), vmem, vmem],
        out_specs=(any_space, any_space),
        scratch_shapes=[wide(rows, triple), pltpu.SemaphoreType.DMA((2,))],
        compiler_params=pltpu.CompilerParams(vmem_limit_bytes=4 * 1024 * 1024),
    )(result, total, embed_rows)
    return output.reshape(frames, height, columns, width), grad


def solution(mesh):
    placed = (
        P(("dp", "ts"), None, None, None), P(), P(), P(), P(), P(("dp", "ts"), None),
        P(("dp", "ts"), None), P(), P(), P(("dp", "ts"), None, None, None),
    )
    return jax.shard_map(
        shards,
        mesh=mesh,
        in_specs=placed,
        out_specs=(P(("dp", "ts"), None, None, None), P(("dp", "ts"), None)),
        check_vma=False,
    )
```
